32 devices in a mesh: grp: 8 (over z, x), seq: 4 (over y, core).
Axes of the slice: x: 2, y: 2, z: 4, core: 2. Of those that a mesh axis runs over, the one named last changes fastest.
Arguments:
- prompt_in: bfloat16 [8, 2048, 768], P('grp', 'seq'), may hold values from -6 to 6
- cont_in: bfloat16 [8, 16, 256, 768], P('grp', 'seq'), may hold values from -6 to 6
- prompt_cot: bfloat16 [8, 2048, 768], P('grp', 'seq'), may hold values from -6 to 6
- cont_cot: bfloat16 [8, 16, 256, 768], P('grp', 'seq'), may hold values from -6 to 6
- labels: int32 [8, 16], P('grp', 'seq'), may hold values from 0 to 13
- joint_weight: float32 [768, 2304], P(('grp', 'seq')), may hold values from -0.21875 to 0.21875
- query_bias: float32 [768], P(('grp', 'seq')), may hold values from -3 to 3
- value_bias: float32 [768], P(('grp', 'seq')), may hold values from -0.3 to 0.3
- output_weight: float32 [768, 768], P(('grp', 'seq')), may hold values from -3.5 to 3.5
- output_bias: float32 [768], P(('grp', 'seq')), may hold values from -2 to 2
- first_gain: float32 [768], P(('grp', 'seq')), may hold values from 0.5 to 1.5
- first_shift: float32 [768], P(('grp', 'seq')), may hold values from -2 to 2
- expand_weight: float32 [768, 3072], P(('grp', 'seq')), may hold values from -0.21875 to 0.21875
- expand_bias: float32 [3072], P(('grp', 'seq')), may hold values from -3 to 3
- reduce_weight: float32 [3072, 768], P(('grp', 'seq')), may hold values from -0.109375 to 0.109375
- reduce_bias: float32 [768], P(('grp', 'seq')), may hold values from -2 to 2
- second_gain: float32 [768], P(('grp', 'seq')), may hold values from 0.5 to 1.5
- second_shift: float32 [768], P(('grp', 'seq')), may hold values from -2 to 2
- student_weight: float32 [768, 128], replicated, may hold values from -0.21875 to 0.21875
- student_bias: float32 [128], replicated, may hold values from -2 to 2
- pool_query: float32 [128], replicated, may hold values from -4 to 4
- pool_weight: float32 [128, 128], replicated, may hold values from -0.5 to 0.5
- pool_bias: float32 [128], replicated, may hold values from -2 to 2
- class_weight: float32 [128, 14], replicated, may hold values from -1.5 to 1.5
- class_bias: float32 [14], replicated, may hold values from -3 to 3
Outputs:
- prompt_out: bfloat16 [8, 2048, 768], P('grp', 'seq')
- cont_out: bfloat16 [8, 16, 256, 768], P('grp', 'seq')
- logits: float32 [8, 16, 14], P('grp', 'seq')
- prompt_grad: float32 [8, 2048, 768], P('grp', 'seq')
- cont_grad: float32 [8, 16, 256, 768], P('grp', 'seq')
- joint_weight_grad: float32 [768, 2304], P(('grp', 'seq'))
- query_bias_grad: float32 [768], P(('grp', 'seq'))
- value_bias_grad: float32 [768], P(('grp', 'seq'))
- output_weight_grad: float32 [768, 768], P(('grp', 'seq'))
- output_bias_grad: float32 [768], P(('grp', 'seq'))
- first_gain_grad: float32 [768], P(('grp', 'seq'))
- first_shift_grad: float32 [768], P(('grp', 'seq'))
- expand_weight_grad: float32 [768, 3072], P(('grp', 'seq'))
- expand_bias_grad: float32 [3072], P(('grp', 'seq'))
- reduce_weight_grad: float32 [3072, 768], P(('grp', 'seq'))
- reduce_bias_grad: float32 [768], P(('grp', 'seq'))
- second_gain_grad: float32 [768], P(('grp', 'seq'))
- second_shift_grad: float32 [768], P(('grp', 'seq'))
- student_weight_grad: float32 [768, 128], replicated
- student_bias_grad: float32 [128], replicated
- pool_query_grad: float32 [128], replicated
- pool_weight_grad: float32 [128, 128], replicated
- pool_bias_grad: float32 [128], replicated
- class_weight_grad: float32 [128, 14], replicated
- class_bias_grad: float32 [14], replicated
The draws below stay inside these ranges and needn't reach their ends.
All inputs are finite; a program needn't handle non-finite values.
Results may differ from the reference program's by a relative error of at most 0.014.
The reference program's roundings to bfloat16 on the way count: a program that leaves them out, or rounds other values in their place, can miss the bound.
Values may be sent and summed in bfloat16 or wider, within the bound.
No kernel may reach another device: no remote copies, remote signals or barrier semaphores. Data moves between devices by JAX's collectives and lax.ppermute only.
A program may use at most 448 MiB of HBM per device.

```python
import jax
import jax.numpy as jnp
from jax import lax

D = 768
HEADS = 12
HEAD_DIM = 64
FF = 3072
CLS = 128
POOL_HEADS = 2
CLASSES = 14
PROMPT = 2048
CLEN = 256
GROUPS = 8
CONTS = 16


def with_ends(result, own_key, low, high):
    dims = result.shape
    index_at = [jax.random.randint(jax.random.fold_in(own_key, axis), (), 0, dims[axis]) for axis in range(len(dims))]
    result = result.at[tuple(index_at)].set(low)
    longest = dims.index(max(dims))
    index_at[longest] = (index_at[longest] + 1) % dims[longest]
    return result.at[tuple(index_at)].set(high)


def level_of(own_key, extent, shards, least, top_value):
    level = 1.0
    for axis_at, parts in shards:
        draws = jax.random.uniform(jax.random.fold_in(jax.random.fold_in(own_key, 6), axis_at), (parts,), jnp.float32, least / len(shards), top_value / len(shards))
        level = level * jnp.repeat(jnp.exp(draws), extent[axis_at] // parts).reshape((-1,) + (1,) * (len(extent) - 1 - axis_at))
    return level


def normal_values(rng, shape, spread, reach, shards=(), held_as=jnp.bfloat16):
    result = jax.random.normal(rng, shape, jnp.float32) * spread
    if len(shards) > 0:
        result = level_of(rng, shape, shards, -0.22, 0.18) * result
    return jnp.clip(result, min=-reach, max=reach).astype(held_as)


def setup_inputs(seed: int = 0) -> dict:
    key_list = jax.random.split(jax.random.key(seed), 26)
    prompt_in = normal_values(key_list[0], (GROUPS, PROMPT, D), 1.0, 6.0, ((0, 8), (1, 4)))
    cont_in = normal_values(key_list[1], (GROUPS, CONTS, CLEN, D), 1.0, 6.0, ((0, 8), (1, 4)))
    prompt_cot = normal_values(key_list[2], (GROUPS, PROMPT, D), 1.0, 6.0, ((0, 8), (1, 4)))
    cont_cot = normal_values(key_list[3], (GROUPS, CONTS, CLEN, D), 1.0, 6.0, ((0, 8), (1, 4)))
    labels = with_ends(jax.random.randint(key_list[4], (GROUPS, CONTS), 0, CLASSES), jax.random.fold_in(key_list[4], 1), 0, CLASSES - 1).astype(jnp.int32)
    joint_weight = normal_values(key_list[5], (D, 3 * D), D ** -0.5, 0.21875, ((0, 32),), jnp.float32)
    query_bias = normal_values(key_list[6], (D,), 0.5, 3.0, ((0, 32),), jnp.float32)
    value_bias = normal_values(key_list[7], (D,), 0.05, 0.3, ((0, 32),), jnp.float32)
    output_weight = normal_values(key_list[8], (D, D), 3 ** -0.5, 3.5, ((0, 32),), jnp.float32)
    output_bias = normal_values(key_list[9], (D,), 0.3, 2.0, ((0, 32),), jnp.float32)
    first_gain = jnp.clip(1.0 + 0.1 * jax.random.normal(key_list[10], (D,), jnp.float32), 0.5, 1.5)
    first_shift = normal_values(key_list[11], (D,), 0.3, 2.0, ((0, 32),), jnp.float32)
    expand_weight = normal_values(key_list[12], (D, FF), D ** -0.5, 0.21875, ((0, 32),), jnp.float32)
    expand_bias = normal_values(key_list[13], (FF,), 0.5, 3.0, ((0, 32),), jnp.float32)
    reduce_weight = normal_values(key_list[14], (FF, D), FF ** -0.5, 0.109375, ((0, 32),), jnp.float32)
    reduce_bias = normal_values(key_list[15], (D,), 0.3, 2.0, ((0, 32),), jnp.float32)
    second_gain = jnp.clip(1.0 + 0.1 * jax.random.normal(key_list[16], (D,), jnp.float32), 0.5, 1.5)
    second_shift = normal_values(key_list[17], (D,), 0.3, 2.0, ((0, 32),), jnp.float32)
    student_weight = normal_values(key_list[18], (D, CLS), D ** -0.5, 0.21875, (), jnp.float32)
    student_bias = normal_values(key_list[19], (CLS,), 0.3, 2.0, (), jnp.float32)
    pool_query = normal_values(key_list[20], (CLS,), 1.0, 4.0, (), jnp.float32)
    pool_weight = normal_values(key_list[21], (CLS, CLS), CLS ** -0.5, 0.5, (), jnp.float32)
    pool_bias = normal_values(key_list[22], (CLS,), 0.3, 2.0, (), jnp.float32)
    class_weight = normal_values(key_list[23], (CLS, CLASSES), 16 ** -0.5, 1.5, (), jnp.float32)
    class_bias = normal_values(key_list[24], (CLASSES,), 0.5, 3.0, (), jnp.float32)
    return {"prompt_in": prompt_in, "cont_in": cont_in, "prompt_cot": prompt_cot, "cont_cot": cont_cot, "labels": labels, "joint_weight": joint_weight, "query_bias": query_bias, "value_bias": value_bias, "output_weight": output_weight, "output_bias": output_bias, "first_gain": first_gain, "first_shift": first_shift, "expand_weight": expand_weight, "expand_bias": expand_bias, "reduce_weight": reduce_weight, "reduce_bias": reduce_bias, "second_gain": second_gain, "second_shift": second_shift, "student_weight": student_weight, "student_bias": student_bias, "pool_query": pool_query, "pool_weight": pool_weight, "pool_bias": pool_bias, "class_weight": class_weight, "class_bias": class_bias}


@jax.custom_vjp
def low(v):
    return lax.optimization_barrier(v.astype(jnp.bfloat16)).astype(jnp.float32)

@jax.custom_vjp
def low_back(v):
    return v

def low_keep(v):
    return (low(v), None)

def low_pass(kept, grad):
    return (grad,)

def back_keep(v):
    return (v, None)

def back_low(kept, grad):
    return (low(grad),)
low.defvjp(low_keep, low_pass)
low_back.defvjp(back_keep, back_low)
EPSILON = 1e-06
HIGHEST = lax.Precision.HIGHEST
NEGATIVE = -1e+30

def matmul(left, right):
    return jnp.dot(left, right, precision=HIGHEST, preferred_element_type=jnp.float32)

def layer_norm(rows, gain, shift):
    center = rows - lax.optimization_barrier(jnp.mean(rows, -1, keepdims=True))
    variance = lax.optimization_barrier(jnp.mean(center * center, -1, keepdims=True))
    return center * lax.rsqrt(variance + EPSILON) * gain + shift

def head_forward(student, pool_query, pool_weight, pool_bias, class_weight, class_bias, labels):
    count, length, width = student.shape
    split = student.reshape(count, length, POOL_HEADS, width // POOL_HEADS)
    query = pool_query.reshape(POOL_HEADS, width // POOL_HEADS)
    scores = jnp.einsum('clhd,hd->chl', split, query, precision=HIGHEST) * (width // POOL_HEADS) ** (-0.5)
    weights = jax.nn.softmax(scores, -1)
    pooled = jnp.einsum('chl,clhd->chd', weights, split, precision=HIGHEST).reshape(count, width)
    hidden = jnp.tanh(matmul(pooled, pool_weight) + pool_bias)
    logits = matmul(hidden, class_weight) + class_bias
    onehot = (labels[:, None] == jnp.arange(logits.shape[1], dtype=jnp.int32)[None, :]).astype(jnp.float32)
    loss = jnp.sum(jax.nn.logsumexp(logits, -1) - lax.optimization_barrier(jnp.sum(onehot * logits, -1)))
    return (loss, logits)

def cont_only(array):
    return jnp.concatenate([array[:PROMPT], low_back(array[PROMPT:])], 0)

def group_forward(prompt_rows, cont_rows, group_labels, layer, head):
    joint_weight, query_bias, value_bias, output_weight, output_bias, first_gain, first_shift, expand_weight, expand_bias, reduce_weight, reduce_bias, second_gain, second_shift = layer
    student_weight, student_bias, pool_query, pool_weight, pool_bias, class_weight, class_bias = head
    rows = jnp.concatenate([prompt_rows, cont_rows.reshape(CONTS * CLEN, D)], 0)
    joint = matmul(low(rows), joint_weight)
    queries = low(low_back(joint[:, :D]) + query_bias)
    keys = low(cont_only(joint[:, D:2 * D]))
    values = low(cont_only(joint[:, 2 * D:]) + value_bias)
    scale = HEAD_DIM ** (-0.5)
    far_queries = queries[:PROMPT].reshape(PROMPT, HEADS, HEAD_DIM)
    far_keys = keys[:PROMPT].reshape(PROMPT, HEADS, HEAD_DIM)
    far_values = values[:PROMPT].reshape(PROMPT, HEADS, HEAD_DIM)
    prompt_scores = low_back(jnp.einsum('qhd,khd->hqk', far_queries, far_keys, precision=HIGHEST) * scale)
    prompt_probs = low(jax.nn.softmax(prompt_scores, -1))
    prompt_context = jnp.einsum('hqk,khd->qhd', prompt_probs, far_values, precision=HIGHEST).reshape(PROMPT, D)
    allowed = jnp.concatenate([jnp.ones((CLEN, PROMPT), bool), lax.broadcasted_iota(jnp.int32, (CLEN, CLEN), 0) >= lax.broadcasted_iota(jnp.int32, (CLEN, CLEN), 1)], 1)

    def one_cont(item):
        cont_queries, cont_keys, cont_values = item
        far = jnp.einsum('qhd,khd->hqk', cont_queries, far_keys, precision=HIGHEST)
        near = jnp.einsum('qhd,khd->hqk', cont_queries, cont_keys, precision=HIGHEST)
        scores = low_back(jnp.concatenate([far, near], -1) * scale)
        scores = jnp.where(allowed, scores, NEGATIVE)
        probs = low(jax.nn.softmax(scores, -1))
        return jnp.einsum('hqk,khd->qhd', probs, jnp.concatenate([far_values, cont_values], 0), precision=HIGHEST)

    def split_conts(array):
        return array[PROMPT:].reshape(CONTS, CLEN, HEADS, HEAD_DIM)
    cont_context = lax.map(jax.checkpoint(one_cont), (split_conts(queries), split_conts(keys), split_conts(values)))
    context = low(low_back(jnp.concatenate([prompt_context, cont_context.reshape(CONTS * CLEN, D)], 0)))
    branch = low_back(matmul(context, output_weight)) + output_bias
    first = layer_norm(rows + branch, first_gain, first_shift)
    pre = low_back(matmul(low(first), expand_weight)) + expand_bias
    hidden = low(jax.nn.gelu(pre, approximate=False))
    mixed = first + low_back(matmul(hidden, reduce_weight)) + reduce_bias
    layer_rows = layer_norm(mixed, second_gain, second_shift)
    cont_layer = layer_rows[PROMPT:]
    student = low_back(matmul(low(cont_layer), student_weight)) + student_bias
    loss, logits = head_forward(student.reshape(CONTS, CLEN, CLS), pool_query, pool_weight, pool_bias, class_weight, class_bias, group_labels)
    return (layer_rows[:PROMPT], cont_layer.reshape(CONTS, CLEN, D), logits, loss)

def reference(prompt_in, cont_in, prompt_cot, cont_cot, labels, joint_weight, query_bias, value_bias, output_weight, output_bias, first_gain, first_shift, expand_weight, expand_bias, reduce_weight, reduce_bias, second_gain, second_shift, student_weight, student_bias, pool_query, pool_weight, pool_bias, class_weight, class_bias):
    prompt_rows = prompt_in.astype(jnp.float32)
    cont_rows = cont_in.astype(jnp.float32)
    layer = (joint_weight, query_bias, value_bias, output_weight, output_bias, first_gain, first_shift, expand_weight, expand_bias, reduce_weight, reduce_bias, second_gain, second_shift)
    head = (student_weight, student_bias, pool_query, pool_weight, pool_bias, class_weight, class_bias)

    def forward(prompt_rows, cont_rows, layer, head):
        layer_low = tuple((low(weight) for weight in layer))
        head_low = (low(head[0]),) + tuple(head[1:])

        def one_group(item):
            return group_forward(item[0], item[1], item[2], layer_low, head_low)
        prompt_layer, cont_layer, logits, losses = lax.map(jax.checkpoint(one_group), (prompt_rows, cont_rows, labels))
        return (prompt_layer, cont_layer, logits, jnp.sum(losses))
    outputs, pullback = jax.vjp(forward, prompt_rows, cont_rows, layer, head)
    prompt_layer, cont_layer, logits, total = outputs
    grad_prompt, grad_cont, grad_layer, grad_head = pullback((prompt_cot.astype(jnp.float32), cont_cot.astype(jnp.float32), jnp.zeros_like(logits), jnp.ones_like(total)))
    return (prompt_layer.astype(jnp.bfloat16), cont_layer.astype(jnp.bfloat16), logits, grad_prompt, grad_cont, grad_layer[0], grad_layer[1], grad_layer[2], grad_layer[3], grad_layer[4], grad_layer[5], grad_layer[6], grad_layer[7], grad_layer[8], grad_layer[9], grad_layer[10], grad_layer[11], grad_layer[12], grad_head[0], grad_head[1], grad_head[2], grad_head[3], grad_head[4], grad_head[5], grad_head[6])
```

```python
import functools

import jax
import jax.numpy as jnp
from jax import lax
from jax.experimental import pallas as pl
from jax.experimental.pallas import tpu as pltpu
from jax.sharding import PartitionSpec as P

HEAD_DIM = 64
POOL_HEADS = 2
PAIR = 2 * HEAD_DIM

EPSILON = 1e-06
HIGHEST = lax.Precision.HIGHEST
NEGATIVE = -1e30
BOTH = ("grp", "seq")
BF16 = jnp.bfloat16
F32 = jnp.float32
LOG2_E = 1.4426950408889634
SUM_LOW, SUM_HIGH = 1e-12, 1e18
VMEM_LIMIT = 56 << 20


def dot(left, right, left_dim, right_dim):
    return lax.dot_general(
        left, right, (((left_dim,), (right_dim,)), ((), ())), preferred_element_type=F32
    )


def precise(left, right):
    return jnp.dot(left, right, precision=HIGHEST, preferred_element_type=F32)


def attention_forward_kernel(near, *refs):
    if near:
        q_ref, k_ref, v_ref, kn_ref, vn_ref, out_ref, inv_ref, exp_ref, vt_ref, s_ref = refs
    else:
        q_ref, k_ref, v_ref, out_ref, inv_ref, exp_ref, vt_ref, s_ref = refs
    far = k_ref.shape[0]
    tile = q_ref.shape[0]

    @pl.when(pl.program_id(1) == 0)
    def _():
        vt_ref[...] = v_ref[...].T

    q = q_ref[...]
    lane = lax.broadcasted_iota(jnp.int32, q.shape, 1)
    masked = [
        jnp.where((lane < HEAD_DIM) if h == 0 else (lane >= HEAD_DIM), q, jnp.zeros_like(q))
        for h in range(2)
    ]
    heads = [slice(h * HEAD_DIM, (h + 1) * HEAD_DIM) for h in range(2)]
    if near:
        vnt = vn_ref[...].T
        allowed = lax.broadcasted_iota(jnp.int32, (tile, tile), 0) <= lax.broadcasted_iota(
            jnp.int32, (tile, tile), 1
        )

    def near_scores(h):
        return jnp.where(allowed, dot(kn_ref[...], masked[h], 1, 1), NEGATIVE)

    def finish(outs):
        out_ref[...] = jnp.concatenate(outs, 0).T.astype(out_ref.dtype)

    outs = []
    fine = None
    for h in range(2):
        e = jnp.exp2(dot(k_ref[...], masked[h], 1, 1) * LOG2_E)
        total = jnp.sum(e, axis=0, keepdims=True)
        low = e.astype(BF16)
        exp_ref[0, 0, h, 0:far, :] = low
        out = dot(vt_ref[heads[h], :], low, 1, 0)
        if near:
            e = jnp.exp2(near_scores(h) * LOG2_E)
            total = total + jnp.sum(e, axis=0, keepdims=True)
            low = e.astype(BF16)
            exp_ref[0, 0, h, far:, :] = low
            out = out + dot(vnt[heads[h], :], low, 1, 0)
        inverse = 1.0 / total
        inv_ref[0, 0, h : h + 1, :] = inverse
        outs.append(out * inverse)
        good = jnp.where((total > SUM_LOW) & (total < SUM_HIGH), 1.0, 0.0)
        fine = good if fine is None else jnp.minimum(fine, good)
    finish(outs)

    @pl.when(jnp.min(fine) < 0.5)
    def _():
        chunk = tile
        steps = far // chunk
        outs = []
        for h in range(2):

            def score(c, top):
                at = pl.multiple_of(c * chunk, chunk)
                s = dot(k_ref[pl.ds(at, chunk), :], masked[h], 1, 1)
                s_ref[pl.ds(at, chunk), :] = s
                return jnp.maximum(top, jnp.max(s, axis=0, keepdims=True))

            top = jnp.full((1, tile), NEGATIVE, F32)
            if near:
                sn = near_scores(h)
                top = jnp.max(sn, axis=0, keepdims=True)
            top = lax.fori_loop(0, steps, score, top)

            def weigh(c, carry):
                total, out = carry
                at = pl.multiple_of(c * chunk, chunk)
                e = jnp.exp2((s_ref[pl.ds(at, chunk), :] - top) * LOG2_E)
                low = e.astype(BF16)
                exp_ref[0, 0, h, pl.ds(at, chunk), :] = low
                part = dot(v_ref[pl.ds(at, chunk), :], low, 0, 0)[heads[h], :]
                return total + jnp.sum(e, axis=0, keepdims=True), out + part

            total = jnp.zeros((1, tile), F32)
            out = jnp.zeros((HEAD_DIM, tile), F32)
            if near:
                e = jnp.exp2((sn - top) * LOG2_E)
                low = e.astype(BF16)
                exp_ref[0, 0, h, far:, :] = low
                total = jnp.sum(e, axis=0, keepdims=True)
                out = dot(vnt[heads[h], :], low, 1, 0)
            total, out = lax.fori_loop(0, steps, weigh, (total, out))
            inverse = 1.0 / total
            inv_ref[0, 0, h : h + 1, :] = inverse
            outs.append(out * inverse)
        finish(outs)


def attention_forward(queries, q_at, far_kv, far, near_at, count, tile):
    near = near_at is not None
    width = queries.shape[1]
    pairs = width // PAIR
    tiles = count // tile
    held = far + (tile if near else 0)
    at = q_at // tile
    specs = [
        pl.BlockSpec((tile, PAIR), lambda h, t: (at + t, h)),
        pl.BlockSpec((far, PAIR), lambda h, t: (0, h)),
        pl.BlockSpec((far, PAIR), lambda h, t: (0, pairs + h)),
    ]
    operands = [queries, far_kv, far_kv]
    if near:
        first = near_at // tile
        specs += [
            pl.BlockSpec((tile, PAIR), lambda h, t: (first + t, h)),
            pl.BlockSpec((tile, PAIR), lambda h, t: (first + t, pairs + h)),
        ]
        operands += [far_kv, far_kv]
    cells = count * held * width // HEAD_DIM
    return pl.pallas_call(
        functools.partial(attention_forward_kernel, near),
        grid=(pairs, tiles),
        in_specs=specs,
        out_specs=[
            pl.BlockSpec((tile, PAIR), lambda h, t: (t, h)),
            pl.BlockSpec((1, 1, 2, tile), lambda h, t: (h, t, 0, 0)),
            pl.BlockSpec((1, 1, 2, held, tile), lambda h, t: (h, t, 0, 0, 0)),
        ],
        out_shape=[
            jax.ShapeDtypeStruct((count, width), BF16),
            jax.ShapeDtypeStruct((pairs, tiles, 2, tile), F32),
            jax.ShapeDtypeStruct((pairs, tiles, 2, held, tile), BF16),
        ],
        scratch_shapes=[pltpu.VMEM((PAIR, far), BF16), pltpu.VMEM((far, tile), F32)],
        compiler_params=pltpu.CompilerParams(vmem_limit_bytes=VMEM_LIMIT),
        cost_estimate=pl.CostEstimate(
            flops=4 * cells * HEAD_DIM, bytes_accessed=2 * cells, transcendentals=cells
        ),
        name="attention_forward",
    )(*operands)


def attention_backward_kernel(near, *refs):
    if near:
        (
            q_ref,
            k_ref,
            v_ref,
            kn_ref,
            vn_ref,
            out_ref,
            dout_ref,
            inv_ref,
            exp_ref,
            dk_in_ref,
            dv_in_ref,
            dq_ref,
            dkn_ref,
            dvn_ref,
            dk_ref,
            dv_ref,
            kt_ref,
            dkt_ref,
            dvt_ref,
        ) = refs
    else:
        (
            q_ref,
            k_ref,
            v_ref,
            out_ref,
            dout_ref,
            inv_ref,
            exp_ref,
            dq_ref,
            dk_ref,
            dv_ref,
            kt_ref,
            dkt_ref,
            dvt_ref,
        ) = refs
    far = k_ref.shape[0]
    tile = q_ref.shape[0]
    at = pl.program_id(1)

    @pl.when(at == 0)
    def _():
        kt_ref[...] = k_ref[...].T
        if near:
            dkt_ref[...] = dk_in_ref[...]
            dvt_ref[...] = dv_in_ref[...]
        else:
            dkt_ref[...] = jnp.zeros_like(dkt_ref)
            dvt_ref[...] = jnp.zeros_like(dvt_ref)

    qt = q_ref[...].T
    dout = dout_ref[...].astype(F32).T
    product = out_ref[...].astype(F32).T * dout
    if near:
        knt = kn_ref[...].T
    zero = jnp.zeros((HEAD_DIM, tile), BF16)
    dqs, dkn, dvn = [], [], []
    for h in range(2):
        rows = slice(h * HEAD_DIM, (h + 1) * HEAD_DIM)
        inverse = inv_ref[0, 0, h : h + 1, :]
        delta = jnp.sum(product[rows, :], axis=0, keepdims=True) * inverse
        do = (dout[rows, :] * inverse).astype(BF16)
        padded = jnp.concatenate([do, zero] if h == 0 else [zero, do], 0)
        e = exp_ref[0, 0, h, 0:far, :]
        ds = (e.astype(F32) * (dot(v_ref[...], padded, 1, 0) - delta)).astype(BF16)
        dvt_ref[rows, :] += dot(do, e, 1, 1)
        dkt_ref[rows, :] += dot(qt[rows, :], ds, 1, 1)
        dq = dot(kt_ref[rows, :], ds, 1, 0)
        if near:
            e = exp_ref[0, 0, h, far:, :]
            ds = (e.astype(F32) * (dot(vn_ref[...], padded, 1, 0) - delta)).astype(BF16)
            dvn.append(dot(do, e, 1, 1))
            dkn.append(dot(qt[rows, :], ds, 1, 1))
            dq = dq + dot(knt[rows, :], ds, 1, 0)
        dqs.append(dq * HEAD_DIM ** (-0.5))
    dq_ref[...] = jnp.concatenate(dqs, 0).T.astype(dq_ref.dtype)
    if near:
        dkn_ref[...] = jnp.concatenate(dkn, 0).T.astype(dkn_ref.dtype)
        dvn_ref[...] = jnp.concatenate(dvn, 0).T.astype(dvn_ref.dtype)

    @pl.when(at == pl.num_programs(1) - 1)
    def _():
        if near:
            dk_ref[...] = dkt_ref[...].T.astype(dk_ref.dtype)
            dv_ref[...] = dvt_ref[...].T.astype(dv_ref.dtype)
        else:
            dk_ref[...] = dkt_ref[...]
            dv_ref[...] = dvt_ref[...]


def attention_backward(
    queries, q_at, far_kv, far, near_at, context, d_context, inverse, held_exp, sums, tile, h0, nh
):
    near = sums is not None
    width = queries.shape[1]
    pairs = width // PAIR
    count = context.shape[0]
    tiles = count // tile
    held = held_exp.shape[3]
    at = q_at // tile
    specs = [
        pl.BlockSpec((tile, PAIR), lambda h, t: (at + t, h0 + h)),
        pl.BlockSpec((far, PAIR), lambda h, t: (0, h0 + h)),
        pl.BlockSpec((far, PAIR), lambda h, t: (0, pairs + h0 + h)),
    ]
    operands = [queries, far_kv, far_kv]
    if near:
        first = near_at // tile
        specs += [
            pl.BlockSpec((tile, PAIR), lambda h, t: (first + t, h0 + h)),
            pl.BlockSpec((tile, PAIR), lambda h, t: (first + t, pairs + h0 + h)),
        ]
        operands += [far_kv, far_kv]
    specs += [
        pl.BlockSpec((tile, PAIR), lambda h, t: (t, h0 + h)),
        pl.BlockSpec((tile, PAIR), lambda h, t: (at + t, h0 + h)),
        pl.BlockSpec((1, 1, 2, tile), lambda h, t: (h0 + h, t, 0, 0)),
        pl.BlockSpec((1, 1, 2, held, tile), lambda h, t: (h0 + h, t, 0, 0, 0)),
    ]
    operands += [context, d_context, inverse, held_exp]
    turned = pl.BlockSpec((PAIR, far), lambda h, t: (h, 0))
    row = pl.BlockSpec((tile, PAIR), lambda h, t: (t, h))
    row_shape = jax.ShapeDtypeStruct((count, nh * PAIR), BF16)
    if near:
        specs += [turned, turned]
        operands += list(sums)
        column = pl.BlockSpec((far, PAIR), lambda h, t: (0, h))
        column_shape = jax.ShapeDtypeStruct((far, nh * PAIR), BF16)
    else:
        column = turned
        column_shape = jax.ShapeDtypeStruct((nh * PAIR, far), F32)
    cells = count * held * nh * 2
    return pl.pallas_call(
        functools.partial(attention_backward_kernel, near),
        grid=(nh, tiles),
        in_specs=specs,
        out_specs=[row] + ([row, row] if near else []) + [column, column],
        out_shape=[row_shape] * (3 if near else 1) + [column_shape] * 2,
        scratch_shapes=[
            pltpu.VMEM((PAIR, far), BF16),
            pltpu.VMEM((PAIR, far), F32),
            pltpu.VMEM((PAIR, far), F32),
        ],
        compiler_params=pltpu.CompilerParams(vmem_limit_bytes=VMEM_LIMIT),
        cost_estimate=pl.CostEstimate(
            flops=8 * cells * HEAD_DIM, bytes_accessed=2 * cells, transcendentals=0
        ),
        name="attention_backward",
    )(*operands)


def layer_norm(rows, gain, shift):
    center = rows - jnp.mean(rows, -1, keepdims=True)
    variance = jnp.mean(center * center, -1, keepdims=True)
    return center * lax.rsqrt(variance + EPSILON) * gain + shift


def gelu_pair(pre):
    half = 0.5 * (1.0 + lax.erf(pre * (0.5**0.5)))
    slope = half + pre * (jnp.exp(-0.5 * pre * pre) * 0.3989422804014327)
    return pre * half, slope


def head_forward(student, pool_query, pool_weight, pool_bias, class_weight, class_bias, labels):
    count, length, width = student.shape
    split = student.reshape(count, length, POOL_HEADS, width // POOL_HEADS)
    query = pool_query.reshape(POOL_HEADS, width // POOL_HEADS)
    scores = jnp.einsum("clhd,hd->chl", split, query, precision=HIGHEST) * (
        width // POOL_HEADS
    ) ** (-0.5)
    weights = jax.nn.softmax(scores, -1)
    pooled = jnp.einsum("chl,clhd->chd", weights, split, precision=HIGHEST).reshape(count, width)
    hidden = jnp.tanh(precise(pooled, pool_weight) + pool_bias)
    logits = precise(hidden, class_weight) + class_bias
    onehot = (labels[:, None] == jnp.arange(logits.shape[1], dtype=jnp.int32)[None, :]).astype(F32)
    loss = jnp.sum(jax.nn.logsumexp(logits, -1) - jnp.sum(onehot * logits, -1))
    return (loss, logits)


def gather(shard, axes=BOTH):
    return lax.all_gather(shard, axes, axis=0, tiled=True)


def local(
    prompt_in,
    cont_in,
    prompt_cot,
    cont_cot,
    labels,
    joint_weight,
    query_bias,
    value_bias,
    output_weight,
    output_bias,
    first_gain,
    first_shift,
    expand_weight,
    expand_bias,
    reduce_weight,
    reduce_bias,
    second_gain,
    second_shift,
    student_weight,
    student_bias,
    pool_query,
    pool_weight,
    pool_bias,
    class_weight,
    class_bias,
):
    prompt_rows = prompt_in[0]
    share, width = prompt_rows.shape
    _, conts, length, _ = cont_in.shape
    cont_count = conts * length
    part = joint_weight.shape[0]
    devices = width // part
    hidden_width = expand_weight.shape[1]
    tile = min(share, length)

    vectors = [
        query_bias,
        value_bias,
        output_bias,
        first_gain,
        first_shift,
        reduce_bias,
        second_gain,
        second_shift,
    ]
    beside = jnp.concatenate(
        [v[:, None] for v in vectors] + [expand_bias.reshape(part, hidden_width // width)], 1
    )
    beside = jnp.pad(beside, ((0, 0), (0, 128 - beside.shape[1])))
    joint_all = gather(jnp.concatenate([joint_weight, beside], 1).astype(BF16))
    prompt_all = gather(prompt_rows, "seq")
    far = prompt_all.shape[0]
    out_expand = gather(jnp.concatenate([output_weight, expand_weight], 1).astype(BF16))
    reduce_full = gather(reduce_weight.astype(BF16))
    joint_full = joint_all[:, : 3 * width]
    flat = joint_all[:, 3 * width :].astype(F32)
    qbias, vbias, obias, fgain, fshift, rbias, sgain, sshift = (flat[:, i] for i in range(8))
    ebias = flat[:, 8 : 8 + hidden_width // width].reshape(hidden_width)
    output_full = out_expand[:, :width]
    expand_full = out_expand[:, width:]

    cont_rows = cont_in[0].reshape(cont_count, width)
    rows = jnp.concatenate([prompt_rows, cont_rows], 0)
    key_rows = jnp.concatenate([prompt_all, cont_rows], 0)
    queries = (dot(rows, joint_full[:, :width], 1, 0) + qbias).astype(BF16) * HEAD_DIM ** (-0.5)
    kv_bias = jnp.concatenate([jnp.zeros_like(vbias), vbias])
    keys_values = (dot(key_rows, joint_full[:, width:], 1, 0) + kv_bias).astype(BF16)

    prompt_context, prompt_inv, prompt_exp = attention_forward(
        queries, 0, keys_values, far, None, share, tile
    )
    cont_context, cont_inv, cont_exp = attention_forward(
        queries, share, keys_values, far, far, cont_count, length
    )
    context = jnp.concatenate([prompt_context, cont_context], 0)

    branch = dot(context, output_full, 1, 0) + obias
    first, first_back = jax.vjp(layer_norm, rows.astype(F32) + branch, fgain, fshift)
    first_low = first.astype(BF16)
    activated, slope = gelu_pair(dot(first_low, expand_full, 1, 0) + ebias)
    hidden = activated.astype(BF16)
    slope = slope.astype(BF16)
    mixed = first + dot(hidden, reduce_full, 1, 0) + rbias
    layer, second_back = jax.vjp(layer_norm, mixed, sgain, sshift)
    layer_low = layer.astype(BF16)
    student_low = student_weight.astype(BF16)
    cont_layer = layer_low[share:]
    student = dot(cont_layer, student_low, 1, 0) + student_bias

    def head_piece(student_rows, query, pool_w, pool_b, class_w, class_b):
        return head_forward(
            student_rows.reshape(conts, length, student_rows.shape[1]),
            query,
            pool_w,
            pool_b,
            class_w,
            class_b,
            labels[0],
        )

    loss, head_back, logits = jax.vjp(
        head_piece,
        student,
        pool_query,
        pool_weight,
        pool_bias,
        class_weight,
        class_bias,
        has_aux=True,
    )
    d_student, d_query, d_pool_weight, d_pool_bias, d_class_weight, d_class_bias = head_back(
        jnp.ones_like(loss)
    )
    d_student_bias = jnp.sum(d_student, 0)
    d_student_low = d_student.astype(BF16)
    d_student_weight = dot(cont_layer, d_student_low, 0, 0)
    cotangent = jnp.concatenate(
        [
            prompt_cot[0].astype(F32),
            cont_cot[0].reshape(cont_count, width).astype(F32)
            + dot(d_student_low, student_low, 1, 1),
        ],
        0,
    )
    d_mixed, d_second_gain, d_second_shift = second_back(cotangent)
    d_reduce_bias = jnp.sum(d_mixed, 0)
    d_mixed_low = d_mixed.astype(BF16)
    d_reduce_weight = dot(hidden, d_mixed_low, 0, 0).astype(BF16)
    d_pre = dot(d_mixed_low, reduce_full, 1, 1) * slope.astype(F32)
    d_expand_bias = jnp.sum(d_pre, 0)
    d_pre_low = d_pre.astype(BF16)
    d_expand_weight = dot(first_low, d_pre_low, 0, 0).astype(BF16)
    d_first = d_mixed + dot(d_pre_low, expand_full, 1, 1)
    d_inner, d_first_gain, d_first_shift = first_back(d_first)
    d_output_bias = jnp.sum(d_inner, 0)
    d_inner_low = d_inner.astype(BF16)
    d_output_weight = dot(context, d_inner_low, 0, 0).astype(BF16)
    d_context = dot(d_inner_low, output_full, 1, 1).astype(BF16)

    blocks = [d_output_weight.reshape(devices, part, width)]
    blocks += [
        d_expand_weight[:, i * width : (i + 1) * width].reshape(devices, part, width)
        for i in range(hidden_width // width)
    ]
    blocks += [d_reduce_weight.reshape(devices, -1, width)]
    early = lax.psum_scatter(
        jnp.concatenate(blocks, 1), BOTH, scatter_dimension=0, tiled=True
    )[0].astype(F32)
    count = hidden_width // width
    output_grad = early[:part]
    expand_grad = jnp.concatenate(
        [early[part * (1 + i) : part * (2 + i)] for i in range(count)], 1
    )
    reduce_grad = early[part * (1 + count) :]

    pairs = width // PAIR
    dq_prompt, dk_sum, dv_sum = attention_backward(
        queries, 0, keys_values, far, None, prompt_context, d_context, prompt_inv, prompt_exp,
        None, tile, 0, pairs,
    )
    dq_cont, dk_cont, dv_cont, dk_far, dv_far = attention_backward(
        queries, share, keys_values, far, far, cont_context, d_context, cont_inv, cont_exp,
        (dk_sum, dv_sum), length, 0, pairs,
    )
    d_queries = jnp.concatenate([dq_prompt, dq_cont], 0)
    d_keys = jnp.concatenate([dk_far, dk_cont], 0)
    d_values = jnp.concatenate([dv_far, dv_cont], 0)
    d_query_bias = jnp.sum(d_queries.astype(F32), 0)
    d_value_bias = jnp.sum(d_values.astype(F32), 0)
    d_joint = jnp.concatenate(
        [
            dot(rows, d_queries, 0, 0),
            dot(key_rows, d_keys, 0, 0),
            dot(key_rows, d_values, 0, 0),
        ],
        1,
    ).astype(BF16)
    joint_grad = lax.psum_scatter(d_joint, BOTH, scatter_dimension=0, tiled=True).astype(F32)
    own = lax.psum_scatter(
        jnp.concatenate([dk_far, dv_far], 1), "seq", scatter_dimension=0, tiled=True
    )
    d_kv = jnp.concatenate([own, jnp.concatenate([dk_cont, dv_cont], 1)], 0)
    d_rows = (
        d_inner
        + dot(d_queries, joint_full[:, :width], 1, 1)
        + dot(d_kv, joint_full[:, width:], 1, 1)
    )

    head_grads = (
        d_student_weight,
        d_student_bias,
        d_query,
        d_pool_weight,
        d_pool_bias,
        d_class_weight,
        d_class_bias,
    )
    vector_grads = (
        d_query_bias,
        d_value_bias,
        d_output_bias,
        d_first_gain,
        d_first_shift,
        d_expand_bias,
        d_reduce_bias,
        d_second_gain,
        d_second_shift,
    )
    head_grads, vector_grads = lax.psum((head_grads, vector_grads), BOTH)
    index = lax.axis_index(BOTH)

    def own_part(vector):
        size = vector.shape[0] // devices
        return lax.dynamic_slice(vector, (index * size,), (size,))

    (g_qbias, g_vbias, g_obias, g_fgain, g_fshift, g_ebias, g_rbias, g_sgain, g_sshift) = (
        own_part(v) for v in vector_grads
    )
    return (
        layer_low[:share][None],
        cont_layer.reshape(1, conts, length, width),
        logits[None],
        d_rows[:share][None],
        d_rows[share:].reshape(1, conts, length, width),
        joint_grad,
        g_qbias,
        g_vbias,
        output_grad,
        g_obias,
        g_fgain,
        g_fshift,
        expand_grad,
        g_ebias,
        reduce_grad,
        g_rbias,
        g_sgain,
        g_sshift,
    ) + tuple(head_grads)


def solution(mesh):
    placed = (
        P("grp", "seq", None),
        P("grp", "seq", None, None),
        P("grp", "seq", None),
        P("grp", "seq", None, None),
        P("grp", "seq"),
        P(("grp", "seq"), None),
        P(("grp", "seq")),
        P(("grp", "seq")),
        P(("grp", "seq"), None),
        P(("grp", "seq")),
        P(("grp", "seq")),
        P(("grp", "seq")),
        P(("grp", "seq"), None),
        P(("grp", "seq")),
        P(("grp", "seq"), None),
        P(("grp", "seq")),
        P(("grp", "seq")),
        P(("grp", "seq")),
        P(),
        P(),
        P(),
        P(),
        P(),
        P(),
        P(),
    )
    return jax.shard_map(
        local,
        mesh=mesh,
        in_specs=placed,
        out_specs=(
            P("grp", "seq", None),
            P("grp", "seq", None, None),
            P("grp", "seq", None),
            P("grp", "seq", None),
            P("grp", "seq", None, None),
            P(("grp", "seq"), None),
            P(("grp", "seq")),
            P(("grp", "seq")),
            P(("grp", "seq"), None),
            P(("grp", "seq")),
            P(("grp", "seq")),
            P(("grp", "seq")),
            P(("grp", "seq"), None),
            P(("grp", "seq")),
            P(("grp", "seq"), None),
            P(("grp", "seq")),
            P(("grp", "seq")),
            P(("grp", "seq")),
            P(),
            P(),
            P(),
            P(),
            P(),
            P(),
            P(),
        ),
        check_vma=False,
    )
```

```python
import functools

import jax
import jax.numpy as jnp
from jax import lax
from jax.experimental import pallas as pl
from jax.experimental.pallas import tpu as pltpu
from jax.sharding import PartitionSpec as P

HEAD_DIM = 64
POOL_HEADS = 2
PAIR = 2 * HEAD_DIM

EPSILON = 1e-06
HIGHEST = lax.Precision.HIGHEST
NEGATIVE = -1e30
BOTH = ("grp", "seq")
BF16 = jnp.bfloat16
F32 = jnp.float32
LOG2_E = 1.4426950408889634
SUM_LOW, SUM_HIGH = 1e-12, 1e18
VMEM_LIMIT = 56 << 20


def dot(left, right, left_dim, right_dim):
    return lax.dot_general(
        left, right, (((left_dim,), (right_dim,)), ((), ())), preferred_element_type=F32
    )


def precise(left, right):
    return jnp.dot(left, right, precision=HIGHEST, preferred_element_type=F32)


def attention_forward_kernel(near, *refs):
    if near:
        q_ref, k_ref, v_ref, kn_ref, vn_ref, _, out_ref, inv_ref, exp_ref, vt_ref, s_ref = refs
    else:
        q_ref, k_ref, v_ref, out_ref, inv_ref, exp_ref, vt_ref, s_ref = refs
    far = k_ref.shape[0]
    tile = q_ref.shape[0]

    @pl.when(pl.program_id(1) == 0)
    def _():
        vt_ref[...] = v_ref[...].T

    q = q_ref[...]
    lane = lax.broadcasted_iota(jnp.int32, q.shape, 1)
    masked = [
        jnp.where((lane < HEAD_DIM) if h == 0 else (lane >= HEAD_DIM), q, jnp.zeros_like(q))
        for h in range(2)
    ]
    heads = [slice(h * HEAD_DIM, (h + 1) * HEAD_DIM) for h in range(2)]
    if near:
        vnt = vn_ref[...].T
        allowed = lax.broadcasted_iota(jnp.int32, (tile, tile), 0) <= lax.broadcasted_iota(
            jnp.int32, (tile, tile), 1
        )

    def near_scores(h):
        return jnp.where(allowed, dot(kn_ref[...], masked[h], 1, 1), NEGATIVE)

    def finish(outs):
        out_ref[...] = jnp.concatenate(outs, 0).T.astype(out_ref.dtype)

    outs = []
    fine = None
    for h in range(2):
        e = jnp.exp2(dot(k_ref[...], masked[h], 1, 1) * LOG2_E)
        total = jnp.sum(e, axis=0, keepdims=True)
        low = e.astype(BF16)
        exp_ref[0, 0, h, 0:far, :] = low
        out = dot(vt_ref[heads[h], :], low, 1, 0)
        if near:
            e = jnp.exp2(near_scores(h) * LOG2_E)
            total = total + jnp.sum(e, axis=0, keepdims=True)
            low = e.astype(BF16)
            exp_ref[0, 0, h, far:, :] = low
            out = out + dot(vnt[heads[h], :], low, 1, 0)
        inverse = 1.0 / total
        inv_ref[0, 0, h : h + 1, :] = inverse
        outs.append(out * inverse)
        good = jnp.where((total > SUM_LOW) & (total < SUM_HIGH), 1.0, 0.0)
        fine = good if fine is None else jnp.minimum(fine, good)
    finish(outs)

    @pl.when(jnp.min(fine) < 0.5)
    def _():
        chunk = tile
        steps = far // chunk
        outs = []
        for h in range(2):

            def score(c, top):
                at = pl.multiple_of(c * chunk, chunk)
                s = dot(k_ref[pl.ds(at, chunk), :], masked[h], 1, 1)
                s_ref[pl.ds(at, chunk), :] = s
                return jnp.maximum(top, jnp.max(s, axis=0, keepdims=True))

            top = jnp.full((1, tile), NEGATIVE, F32)
            if near:
                sn = near_scores(h)
                top = jnp.max(sn, axis=0, keepdims=True)
            top = lax.fori_loop(0, steps, score, top)

            def weigh(c, carry):
                total, out = carry
                at = pl.multiple_of(c * chunk, chunk)
                e = jnp.exp2((s_ref[pl.ds(at, chunk), :] - top) * LOG2_E)
                low = e.astype(BF16)
                exp_ref[0, 0, h, pl.ds(at, chunk), :] = low
                part = dot(v_ref[pl.ds(at, chunk), :], low, 0, 0)[heads[h], :]
                return total + jnp.sum(e, axis=0, keepdims=True), out + part

            total = jnp.zeros((1, tile), F32)
            out = jnp.zeros((HEAD_DIM, tile), F32)
            if near:
                e = jnp.exp2((sn - top) * LOG2_E)
                low = e.astype(BF16)
                exp_ref[0, 0, h, far:, :] = low
                total = jnp.sum(e, axis=0, keepdims=True)
                out = dot(vnt[heads[h], :], low, 1, 0)
            total, out = lax.fori_loop(0, steps, weigh, (total, out))
            inverse = 1.0 / total
            inv_ref[0, 0, h : h + 1, :] = inverse
            outs.append(out * inverse)
        finish(outs)


def attention_forward(queries, keys_values, far, count, at, tile, into):
    near = into is not None
    total, width = queries.shape
    pairs = width // PAIR
    tiles = count // tile
    held = far + (tile if near else 0)
    block = at // tile
    specs = [
        pl.BlockSpec((tile, PAIR), lambda h, t: (block + t, h)),
        pl.BlockSpec((far, PAIR), lambda h, t: (0, 2 * h)),
        pl.BlockSpec((far, PAIR), lambda h, t: (0, 2 * h + 1)),
    ]
    operands = [queries, keys_values, keys_values]
    aliases = {}
    if near:
        first = far // tile
        specs += [
            pl.BlockSpec((tile, PAIR), lambda h, t: (first + t, 2 * h)),
            pl.BlockSpec((tile, PAIR), lambda h, t: (first + t, 2 * h + 1)),
            pl.BlockSpec(memory_space=pl.ANY),
        ]
        operands += [keys_values, keys_values, into]
        aliases = {5: 0}
    cells = count * held * width // HEAD_DIM
    return pl.pallas_call(
        functools.partial(attention_forward_kernel, near),
        grid=(pairs, tiles),
        in_specs=specs,
        out_specs=[
            pl.BlockSpec((tile, PAIR), lambda h, t: (block + t, h)),
            pl.BlockSpec((1, 1, 2, tile), lambda h, t: (h, t, 0, 0)),
            pl.BlockSpec((1, 1, 2, held, tile), lambda h, t: (h, t, 0, 0, 0)),
        ],
        out_shape=[
            jax.ShapeDtypeStruct((total, width), BF16),
            jax.ShapeDtypeStruct((pairs, tiles, 2, tile), F32),
            jax.ShapeDtypeStruct((pairs, tiles, 2, held, tile), BF16),
        ],
        scratch_shapes=[pltpu.VMEM((PAIR, far), BF16), pltpu.VMEM((far, tile), F32)],
        input_output_aliases=aliases,
        compiler_params=pltpu.CompilerParams(vmem_limit_bytes=VMEM_LIMIT),
        cost_estimate=pl.CostEstimate(
            flops=4 * cells * HEAD_DIM, bytes_accessed=2 * cells, transcendentals=cells
        ),
        name="attention_forward",
    )(*operands)


def attention_backward_kernel(near, *refs):
    q_ref, k_ref, v_ref, out_ref, dout_ref, inv_ref, exp_ref = refs[:7]
    if near:
        kn_ref, vn_ref, dk_in_ref, dv_in_ref, _, dq_ref, dkvn_ref, dkv_ref = refs[7:15]
    else:
        dq_ref, dk_ref, dv_ref = refs[7:10]
    kt_ref, dkt_ref, dvt_ref = refs[-3:]
    far = k_ref.shape[0]
    tile = q_ref.shape[0]
    at = pl.program_id(1)

    @pl.when(at == 0)
    def _():
        kt_ref[...] = k_ref[...].T
        if near:
            dkt_ref[...] = dk_in_ref[...]
            dvt_ref[...] = dv_in_ref[...]
        else:
            dkt_ref[...] = jnp.zeros_like(dkt_ref)
            dvt_ref[...] = jnp.zeros_like(dvt_ref)

    qt = q_ref[...].T
    dout = dout_ref[...].astype(F32).T
    product = out_ref[...].astype(F32).T * dout
    if near:
        knt = kn_ref[...].T
    zero = jnp.zeros((HEAD_DIM, tile), BF16)
    dqs, dkn, dvn = [], [], []
    for h in range(2):
        rows = slice(h * HEAD_DIM, (h + 1) * HEAD_DIM)
        inverse = inv_ref[0, 0, h : h + 1, :]
        delta = jnp.sum(product[rows, :], axis=0, keepdims=True) * inverse
        do = (dout[rows, :] * inverse).astype(BF16)
        padded = jnp.concatenate([do, zero] if h == 0 else [zero, do], 0)
        e = exp_ref[0, 0, h, 0:far, :]
        ds = (e.astype(F32) * (dot(v_ref[...], padded, 1, 0) - delta)).astype(BF16)
        dvt_ref[rows, :] += dot(do, e, 1, 1)
        dkt_ref[rows, :] += dot(qt[rows, :], ds, 1, 1)
        dq = dot(kt_ref[rows, :], ds, 1, 0)
        if near:
            e = exp_ref[0, 0, h, far:, :]
            ds = (e.astype(F32) * (dot(vn_ref[...], padded, 1, 0) - delta)).astype(BF16)
            dvn.append(dot(do, e, 1, 1))
            dkn.append(dot(qt[rows, :], ds, 1, 1))
            dq = dq + dot(knt[rows, :], ds, 1, 0)
        dqs.append(dq * HEAD_DIM ** (-0.5))
    dq_ref[...] = jnp.concatenate(dqs, 0).T.astype(dq_ref.dtype)
    if near:
        dkvn_ref[:, :PAIR] = jnp.concatenate(dkn, 0).T.astype(dkvn_ref.dtype)
        dkvn_ref[:, PAIR:] = jnp.concatenate(dvn, 0).T.astype(dkvn_ref.dtype)

    @pl.when(at == pl.num_programs(1) - 1)
    def _():
        if near:
            dkv_ref[:, :PAIR] = dkt_ref[...].T.astype(dkv_ref.dtype)
            dkv_ref[:, PAIR:] = dvt_ref[...].T.astype(dkv_ref.dtype)
        else:
            dk_ref[...] = dkt_ref[...]
            dv_ref[...] = dvt_ref[...]


def attention_backward(
    queries, keys_values, far, context, d_context, inverse, held_exp, at, tile, h0, nh, into
):
    near = into is not None
    total = queries.shape[0]
    tiles, held = held_exp.shape[1], held_exp.shape[3]
    count = tiles * tile
    block = at // tile
    row = pl.BlockSpec((tile, PAIR), lambda h, t: (block + t, h0 + h))
    specs = [
        row,
        pl.BlockSpec((far, PAIR), lambda h, t: (0, 2 * (h0 + h))),
        pl.BlockSpec((far, PAIR), lambda h, t: (0, 2 * (h0 + h) + 1)),
        row,
        row,
        pl.BlockSpec((1, 1, 2, tile), lambda h, t: (h0 + h, t, 0, 0)),
        pl.BlockSpec((1, 1, 2, held, tile), lambda h, t: (h0 + h, t, 0, 0, 0)),
    ]
    operands = [queries, keys_values, keys_values, context, d_context, inverse, held_exp]
    turned = pl.BlockSpec((PAIR, far), lambda h, t: (h, 0))
    out_specs = [pl.BlockSpec((tile, PAIR), lambda h, t: (block + t, h))]
    out_shape = [jax.ShapeDtypeStruct((total, nh * PAIR), BF16)]
    aliases = {}
    if near:
        first = far // tile
        specs += [
            pl.BlockSpec((tile, PAIR), lambda h, t: (first + t, 2 * (h0 + h))),
            pl.BlockSpec((tile, PAIR), lambda h, t: (first + t, 2 * (h0 + h) + 1)),
            turned,
            turned,
            pl.BlockSpec(memory_space=pl.ANY),
        ]
        operands += [keys_values, keys_values, into[1], into[2], into[0]]
        aliases = {11: 0}
        out_specs += [
            pl.BlockSpec((tile, 2 * PAIR), lambda h, t: (t, h)),
            pl.BlockSpec((far, 2 * PAIR), lambda h, t: (0, h)),
        ]
        out_shape += [
            jax.ShapeDtypeStruct((count, 2 * nh * PAIR), BF16),
            jax.ShapeDtypeStruct((far, 2 * nh * PAIR), BF16),
        ]
    else:
        out_specs += [turned, turned]
        out_shape += [jax.ShapeDtypeStruct((nh * PAIR, far), F32)] * 2
    cells = count * held * nh * 2
    return pl.pallas_call(
        functools.partial(attention_backward_kernel, near),
        grid=(nh, tiles),
        in_specs=specs,
        out_specs=out_specs,
        out_shape=out_shape,
        scratch_shapes=[
            pltpu.VMEM((PAIR, far), BF16),
            pltpu.VMEM((PAIR, far), F32),
            pltpu.VMEM((PAIR, far), F32),
        ],
        input_output_aliases=aliases,
        compiler_params=pltpu.CompilerParams(vmem_limit_bytes=VMEM_LIMIT),
        cost_estimate=pl.CostEstimate(flops=cells, bytes_accessed=cells, transcendentals=0),
        name="attention_backward",
    )(*operands)


def layer_norm(rows, gain, shift):
    center = rows - jnp.mean(rows, -1, keepdims=True)
    variance = jnp.mean(center * center, -1, keepdims=True)
    return center * lax.rsqrt(variance + EPSILON) * gain + shift


def gelu_pair(pre):
    half = 0.5 * (1.0 + lax.erf(pre * (0.5**0.5)))
    slope = half + pre * (jnp.exp(-0.5 * pre * pre) * 0.3989422804014327)
    return pre * half, slope


def head_forward(student, pool_query, pool_weight, pool_bias, class_weight, class_bias, labels):
    count, length, width = student.shape
    split = student.reshape(count, length, POOL_HEADS, width // POOL_HEADS)
    query = pool_query.reshape(POOL_HEADS, width // POOL_HEADS)
    scores = jnp.einsum("clhd,hd->chl", split, query, precision=HIGHEST) * (
        width // POOL_HEADS
    ) ** (-0.5)
    weights = jax.nn.softmax(scores, -1)
    pooled = jnp.einsum("chl,clhd->chd", weights, split, precision=HIGHEST).reshape(count, width)
    hidden = jnp.tanh(precise(pooled, pool_weight) + pool_bias)
    logits = precise(hidden, class_weight) + class_bias
    onehot = (labels[:, None] == jnp.arange(logits.shape[1], dtype=jnp.int32)[None, :]).astype(F32)
    loss = jnp.sum(jax.nn.logsumexp(logits, -1) - jnp.sum(onehot * logits, -1))
    return (loss, logits)


def bits_of(axis):
    size = lax.axis_size(axis)
    return [(axis, 1 << b) for b in reversed(range(size.bit_length() - 1))]


def across(array, axis, bit):
    return lax.ppermute(array, axis, [(i, i ^ bit) for i in range(lax.axis_size(axis))])


def bit_set(axis, bit):
    return (lax.axis_index(axis) // bit) % 2


def gather_bits(shard, order, dims):
    held = shard.reshape((1,) * len(dims) + shard.shape)
    for axis, bit in order:
        dim = dims.index((axis, bit))
        other = across(held, axis, bit)
        held = jnp.where(
            bit_set(axis, bit) == 0,
            jnp.concatenate([held, other], dim),
            jnp.concatenate([other, held], dim),
        )
    return held


def gather_relative(shard, axis):
    bits = bits_of(axis)
    held = shard.reshape((1,) * len(bits) + shard.shape)
    for dim, (_, bit) in enumerate(bits):
        held = jnp.concatenate([held, across(held, axis, bit)], dim)
    return held.reshape((-1,) + shard.shape[1:])


class Scatter:
    def __init__(self, blocks, order, dims, relative=False):
        self.shape = blocks.shape[1:]
        self.held = blocks.reshape((2,) * len(dims) + self.shape)
        self.order, self.dims, self.relative = list(order), dims, relative
        self.split()

    def split(self):
        axis, bit = self.order[0]
        dim = self.dims.index((axis, bit))
        mine = 0 if self.relative else bit_set(axis, bit)
        self.give = lax.dynamic_slice_in_dim(self.held, 1 - mine, 1, dim)
        self.keep = lax.dynamic_slice_in_dim(self.held, mine, 1, dim)

    def send(self):
        axis, bit = self.order.pop(0)
        self.other = across(self.give, axis, bit)

    def take(self):
        total = self.keep.astype(F32) + self.other.astype(F32)
        if not self.order:
            self.held = total.reshape(self.shape)
            return False
        self.held = total.astype(BF16)
        self.split()
        return True

    def waiting(self):
        return [self.give]

    def tied(self, values):
        (self.give,) = values


class Sum:
    def __init__(self, value, order):
        self.held, self.order = value, list(order)

    def send(self):
        axis, bit = self.order.pop(0)
        self.other = across(self.held, axis, bit)

    def take(self):
        self.held = self.held + self.other
        return bool(self.order)

    def waiting(self):
        return [self.held]

    def tied(self, values):
        (self.held,) = values


class Exchanges:
    def __init__(self):
        self.live = []

    def add(self, chain):
        self.live.append([chain, True])
        return chain

    def step(self, value):
        for entry in self.live:
            if not entry[1]:
                entry[0].more = entry[0].take()
            else:
                entry[0].more = True
            entry[1] = False
        going = [entry[0] for entry in self.live if entry[0].more]
        self.live = [[chain, False] for chain in going]
        if value is not None and going:
            flat = [v for chain in going for v in chain.waiting()]
            value, *flat = lax.optimization_barrier((value, *flat))
            for chain in going:
                size = len(chain.waiting())
                chain.tied(flat[:size])
                flat = flat[size:]
        for chain in going:
            chain.send()
        return value

    def finish(self):
        while self.live:
            self.step(None)


def local(
    prompt_in,
    cont_in,
    prompt_cot,
    cont_cot,
    labels,
    joint_weight,
    query_bias,
    value_bias,
    output_weight,
    output_bias,
    first_gain,
    first_shift,
    expand_weight,
    expand_bias,
    reduce_weight,
    reduce_bias,
    second_gain,
    second_shift,
    student_weight,
    student_bias,
    pool_query,
    pool_weight,
    pool_bias,
    class_weight,
    class_bias,
):
    prompt_rows = prompt_in[0]
    share, width = prompt_rows.shape
    _, conts, length, _ = cont_in.shape
    cont_count = conts * length
    part = joint_weight.shape[0]
    devices = width // part
    hidden_width = expand_weight.shape[1]
    fold = hidden_width // width
    tile = min(share, length)
    grp_bits, seq_bits = bits_of("grp"), bits_of("seq")
    dims = grp_bits + seq_bits
    scatter_order = [seq_bits[-1]] + seq_bits[:-1][::-1] + grp_bits[::-1]
    gather_orders = (
        grp_bits + seq_bits,
        grp_bits[:-1] + seq_bits[:-1] + grp_bits[-1:] + seq_bits[-1:],
    )

    pairs = width // PAIR
    groups = [3, 2, 1] if pairs == 6 else [pairs]
    joint_low = joint_weight.astype(BF16)
    vectors = [
        query_bias,
        value_bias,
        output_bias,
        first_gain,
        first_shift,
        reduce_bias,
        second_gain,
        second_shift,
    ]
    beside = jnp.concatenate([v[None] for v in vectors], 0).astype(BF16).T
    beside = jnp.concatenate([beside, expand_bias.astype(BF16).reshape(part, fold)], 1)
    lanes = student_weight.shape[1]
    own_joint = [joint_low[:, :width]]
    for h in range(pairs):
        own_joint += [joint_low[:, (s * pairs + h) * PAIR :][:, :PAIR] for s in (1, 2)]
    own_joint.append(jnp.pad(beside, ((0, 0), (0, lanes - beside.shape[1]))))
    own_joint = jnp.concatenate(own_joint, 1)
    half = (3 * width // 2 + lanes) // PAIR * PAIR
    joint_all = jnp.concatenate(
        [
            gather_bits(piece, order, dims).reshape(width, -1)
            for piece, order in zip((own_joint[:, :half], own_joint[:, half:]), gather_orders)
        ],
        1,
    )
    joint_full = joint_all[:, : 3 * width]
    flat = joint_all[:, 3 * width :].astype(F32)
    by_vector = flat[:, : len(vectors)].T
    qbias, vbias, obias, fgain, fshift, rbias, sgain, sshift = (by_vector[i] for i in range(8))
    ebias = flat[:, 8 : 8 + fold].reshape(hidden_width)
    prompt_all = gather_relative(prompt_rows, "seq")
    far = prompt_all.shape[0]
    out_expand = lax.all_gather(
        jnp.concatenate([output_weight, expand_weight], 1).astype(BF16), BOTH, axis=0, tiled=True
    )
    reduce_full = lax.all_gather(reduce_weight.astype(BF16), BOTH, axis=0, tiled=True)
    output_full = out_expand[:, :width]
    expand_full = out_expand[:, width:]

    cont_rows = cont_in[0].reshape(cont_count, width)
    rows = jnp.concatenate([prompt_rows, cont_rows], 0)
    key_rows = jnp.concatenate([prompt_all, cont_rows], 0)
    queries = (dot(rows, joint_full[:, :width], 1, 0) + qbias).astype(BF16) * HEAD_DIM ** (-0.5)
    kv_bias = jnp.pad(vbias.reshape(pairs, 1, PAIR), ((0, 0), (1, 0), (0, 0))).reshape(-1)
    keys_values = (dot(key_rows, joint_full[:, width:], 1, 0) + kv_bias).astype(BF16)

    context, prompt_inv, prompt_exp = attention_forward(
        queries, keys_values, far, share, 0, tile, None
    )
    context, cont_inv, cont_exp = attention_forward(
        queries, keys_values, far, cont_count, share, length, context
    )

    branch = dot(context, output_full, 1, 0) + obias
    first, first_back = jax.vjp(layer_norm, rows.astype(F32) + branch, fgain, fshift)
    first_low = first.astype(BF16)
    activated, slope = gelu_pair(dot(first_low, expand_full, 1, 0) + ebias)
    hidden = activated.astype(BF16)
    slope = slope.astype(BF16)
    mixed = first + dot(hidden, reduce_full, 1, 0) + rbias
    layer, second_back = jax.vjp(layer_norm, mixed, sgain, sshift)
    layer_low = layer.astype(BF16)
    student_low = student_weight.astype(BF16)
    cont_layer = layer_low[share:]
    student = dot(cont_layer, student_low, 1, 0) + student_bias

    def head_piece(student_rows, query, pool_w, pool_b, class_w, class_b):
        return head_forward(
            student_rows.reshape(conts, length, student_rows.shape[1]),
            query,
            pool_w,
            pool_b,
            class_w,
            class_b,
            labels[0],
        )

    loss, head_back, logits = jax.vjp(
        head_piece,
        student,
        pool_query,
        pool_weight,
        pool_bias,
        class_weight,
        class_bias,
        has_aux=True,
    )
    d_student, d_query, d_pool_weight, d_pool_bias, d_class_weight, d_class_bias = head_back(
        jnp.ones_like(loss)
    )
    d_student_bias = jnp.sum(d_student, 0)
    d_student_low = d_student.astype(BF16)
    d_student_weight = dot(cont_layer, d_student_low, 0, 0)
    cotangent = jnp.concatenate(
        [
            prompt_cot[0].astype(F32),
            cont_cot[0].reshape(cont_count, width).astype(F32)
            + dot(d_student_low, student_low, 1, 1),
        ],
        0,
    )
    d_mixed, d_second_gain, d_second_shift = second_back(cotangent)
    d_reduce_bias = jnp.sum(d_mixed, 0)
    d_mixed_low = d_mixed.astype(BF16)
    d_reduce_weight = dot(hidden, d_mixed_low, 0, 0).astype(BF16)
    d_pre = dot(d_mixed_low, reduce_full, 1, 1) * slope.astype(F32)
    d_expand_bias = jnp.sum(d_pre, 0)
    d_pre_low = d_pre.astype(BF16)
    d_expand_weight = dot(first_low, d_pre_low, 0, 0).astype(BF16)
    d_first = d_mixed + dot(d_pre_low, expand_full, 1, 1)
    d_inner, d_first_gain, d_first_shift = first_back(d_first)
    d_output_bias = jnp.sum(d_inner, 0)
    d_inner_low = d_inner.astype(BF16)
    d_output_weight = dot(context, d_inner_low, 0, 0).astype(BF16)
    d_context = dot(d_inner_low, output_full, 1, 1).astype(BF16)

    classes = class_weight.shape[1]
    small = [
        d_student_weight,
        d_pool_weight,
        jnp.pad(d_class_weight, ((0, 0), (0, lanes - classes))),
        d_student_bias[None],
        d_query[None],
        d_pool_bias[None],
        jnp.pad(d_class_bias, (0, lanes - classes))[None],
    ] + [
        v.reshape(-1, lanes)
        for v in (
            d_output_bias,
            d_first_gain,
            d_first_shift,
            d_reduce_bias,
            d_second_gain,
            d_second_shift,
            d_expand_bias,
        )
    ]
    exchanges = Exchanges()
    small = exchanges.add(Sum(jnp.concatenate(small, 0), dims))
    blocks = [d_output_weight.reshape(devices, part, width)]
    blocks += [
        d_expand_weight[:, i * width : (i + 1) * width].reshape(devices, part, width)
        for i in range(fold)
    ]
    blocks += [d_reduce_weight.reshape(devices, -1, width)]
    blocks, d_context, d_inner = lax.optimization_barrier(
        (jnp.concatenate(blocks, 1), d_context, d_inner)
    )
    early = lax.psum_scatter(blocks, BOTH, scatter_dimension=0, tiled=True)
    early = early[0].astype(F32)
    output_grad = early[:part]
    expand_grad = jnp.concatenate(
        [early[part * (1 + i) : part * (2 + i)] for i in range(fold)], 1
    )
    reduce_grad = early[part * (1 + fold) :]

    dqs, owns, dkv_conts, joint_parts, sums = [], [], [], [], []
    pick = lax.broadcasted_iota(jnp.int32, (1, lanes), 1)
    ones = [jnp.where(pick == i, 1.0, 0.0).astype(BF16) for i in range(2)]
    h0 = 0
    for g, nh in enumerate(groups):
        d_context = exchanges.step(d_context)
        partial_sums = attention_backward(
            queries, keys_values, far, context, d_context, prompt_inv, prompt_exp, 0, tile, h0, nh, None
        )
        d_context = exchanges.step(d_context)
        dq, dkv_cont, dkv_far = attention_backward(
            queries, keys_values, far, context, d_context, cont_inv, cont_exp, share, length, h0, nh,
            partial_sums,
        )
        owns.append(
            exchanges.add(
                Scatter(
                    dkv_far.reshape(lax.axis_size("seq"), share, -1),
                    seq_bits[::-1],
                    seq_bits,
                    relative=True,
                )
            )
        )
        dqs.append(dq)
        dkv_conts.append(dkv_cont)
        columns = [
            dot(rows, dq, 0, 0),
            dot(prompt_all, dkv_far, 0, 0) + dot(cont_rows, dkv_cont, 0, 0),
        ]
        ones_of = [jnp.broadcast_to(ones[i], (dq.shape[0], lanes)) for i in range(2)]
        value_sums = dot(dkv_far, jnp.broadcast_to(ones[1], (far, lanes)), 0, 0) + dot(
            dkv_cont, ones_of[1][:cont_count], 0, 0
        )
        value_sums = value_sums.reshape(nh, 2, PAIR, lanes)[:, 1].reshape(-1, lanes)
        sums.append(dot(dq, ones_of[0], 0, 0) + value_sums)
        if g == len(groups) - 1:
            columns.append(jnp.concatenate(sums, 0))
        columns = jnp.concatenate(columns, 1).astype(BF16).reshape(devices, part, -1)
        joint_parts.append(exchanges.add(Scatter(columns, scatter_order, dims)))
        h0 += nh
    exchanges.finish()
    parts = [p.held for p in joint_parts]
    pieces = [[], [], []]
    for p, nh in zip(parts, groups):
        pieces[0].append(p[:, : nh * PAIR])
        for h in range(nh):
            for s in range(2):
                at = (nh + 2 * h + s) * PAIR
                pieces[1 + s].append(p[:, at : at + PAIR])
    joint_grad = jnp.concatenate(pieces[0] + pieces[1] + pieces[2], 1)
    at = 3 * groups[-1] * PAIR
    g_qbias, g_vbias = parts[-1][:, at], parts[-1][:, at + 1]

    d_queries = jnp.concatenate(dqs, 1)
    d_own = jnp.concatenate([d_queries[:share]] + [o.held.astype(BF16) for o in owns], 1)
    d_cont = jnp.concatenate([d_queries[share:]] + dkv_conts, 1)
    d_cont_rows = d_inner[share:] + dot(d_cont, joint_full, 1, 1)
    d_prompt_rows = d_inner[:share] + dot(d_own, joint_full, 1, 1)

    small = small.held
    index = lax.axis_index(BOTH)
    at = width + lanes
    head_grads = (
        small[:width],
        small[at + lanes],
        small[at + lanes + 1],
        small[width:at],
        small[at + lanes + 2],
        small[at : at + lanes, :classes],
        small[at + lanes + 3, :classes],
    )
    at += lanes + 4
    vector_grads = []
    for size in [width] * 6 + [hidden_width]:
        vector = small[at : at + size // lanes].reshape(size)
        own = size // devices
        vector_grads.append(lax.dynamic_slice(vector, (index * own,), (own,)))
        at += size // lanes
    g_obias, g_fgain, g_fshift, g_rbias, g_sgain, g_sshift, g_ebias = vector_grads
    return (
        layer_low[:share][None],
        cont_layer.reshape(1, conts, length, width),
        logits[None],
        d_prompt_rows[None],
        d_cont_rows.reshape(1, conts, length, width),
        joint_grad,
        g_qbias,
        g_vbias,
        output_grad,
        g_obias,
        g_fgain,
        g_fshift,
        expand_grad,
        g_ebias,
        reduce_grad,
        g_rbias,
        g_sgain,
        g_sshift,
    ) + head_grads


def solution(mesh):
    placed = (
        P("grp", "seq", None),
        P("grp", "seq", None, None),
        P("grp", "seq", None),
        P("grp", "seq", None, None),
        P("grp", "seq"),
        P(("grp", "seq"), None),
        P(("grp", "seq")),
        P(("grp", "seq")),
        P(("grp", "seq"), None),
        P(("grp", "seq")),
        P(("grp", "seq")),
        P(("grp", "seq")),
        P(("grp", "seq"), None),
        P(("grp", "seq")),
        P(("grp", "seq"), None),
        P(("grp", "seq")),
        P(("grp", "seq")),
        P(("grp", "seq")),
        P(),
        P(),
        P(),
        P(),
        P(),
        P(),
        P(),
    )
    return jax.shard_map(
        local,
        mesh=mesh,
        in_specs=placed,
        out_specs=(
            P("grp", "seq", None),
            P("grp", "seq", None, None),
            P("grp", "seq", None),
            P("grp", "seq", None),
            P("grp", "seq", None, None),
            P(("grp", "seq"), None),
            P(("grp", "seq")),
            P(("grp", "seq")),
            P(("grp", "seq"), None),
            P(("grp", "seq")),
            P(("grp", "seq")),
            P(("grp", "seq")),
            P(("grp", "seq"), None),
            P(("grp", "seq")),
            P(("grp", "seq"), None),
            P(("grp", "seq")),
            P(("grp", "seq")),
            P(("grp", "seq")),
            P(),
            P(),
            P(),
            P(),
            P(),
            P(),
            P(),
        ),
        check_vma=False,
    )
```

```python
import functools

import jax
import jax.numpy as jnp
from jax import lax
from jax.experimental import pallas as pl
from jax.experimental.pallas import tpu as pltpu
from jax.sharding import PartitionSpec as P

HEAD_DIM = 64
POOL_HEADS = 2
PAIR = 2 * HEAD_DIM

EPSILON = 1e-06
HIGHEST = lax.Precision.HIGHEST
NEGATIVE = -1e30
BOTH = ("grp", "seq")
BF16 = jnp.bfloat16
F32 = jnp.float32
LOG2_E = 1.4426950408889634
SUM_LOW, SUM_HIGH = 1e-12, 1e18
VMEM_LIMIT = 56 << 20


def dot(left, right, left_dim, right_dim):
    return lax.dot_general(
        left, right, (((left_dim,), (right_dim,)), ((), ())), preferred_element_type=F32
    )


def precise(left, right):
    return jnp.dot(left, right, precision=HIGHEST, preferred_element_type=F32)


def attention_forward_kernel(near, *refs):
    if near:
        q_ref, k_ref, v_ref, kn_ref, vn_ref, _, out_ref, inv_ref, exp_ref, vt_ref, s_ref = refs
    else:
        q_ref, k_ref, v_ref, out_ref, inv_ref, exp_ref, vt_ref, s_ref = refs
    far = k_ref.shape[0]
    tile = q_ref.shape[0]

    @pl.when(pl.program_id(1) == 0)
    def _():
        vt_ref[...] = v_ref[...].T

    q = q_ref[...]
    lane = lax.broadcasted_iota(jnp.int32, q.shape, 1)
    masked = [
        jnp.where((lane < HEAD_DIM) if h == 0 else (lane >= HEAD_DIM), q, jnp.zeros_like(q))
        for h in range(2)
    ]
    heads = [slice(h * HEAD_DIM, (h + 1) * HEAD_DIM) for h in range(2)]
    if near:
        vnt = vn_ref[...].T
        allowed = lax.broadcasted_iota(jnp.int32, (tile, tile), 0) <= lax.broadcasted_iota(
            jnp.int32, (tile, tile), 1
        )

    def near_scores(h):
        return jnp.where(allowed, dot(kn_ref[...], masked[h], 1, 1), NEGATIVE)

    def finish(outs):
        out_ref[...] = jnp.concatenate(outs, 0).T.astype(out_ref.dtype)

    outs = []
    fine = None
    for h in range(2):
        e = jnp.exp2(dot(k_ref[...], masked[h], 1, 1) * LOG2_E)
        total = jnp.sum(e, axis=0, keepdims=True)
        low = e.astype(BF16)
        exp_ref[0, 0, h, 0:far, :] = low
        out = dot(vt_ref[heads[h], :], low, 1, 0)
        if near:
            e = jnp.exp2(near_scores(h) * LOG2_E)
            total = total + jnp.sum(e, axis=0, keepdims=True)
            low = e.astype(BF16)
            exp_ref[0, 0, h, far:, :] = low
            out = out + dot(vnt[heads[h], :], low, 1, 0)
        inverse = 1.0 / total
        inv_ref[0, 0, h : h + 1, :] = inverse
        outs.append(out * inverse)
        good = jnp.where((total > SUM_LOW) & (total < SUM_HIGH), 1.0, 0.0)
        fine = good if fine is None else jnp.minimum(fine, good)
    finish(outs)

    @pl.when(jnp.min(fine) < 0.5)
    def _():
        chunk = tile
        steps = far // chunk
        outs = []
        for h in range(2):

            def score(c, top):
                at = pl.multiple_of(c * chunk, chunk)
                s = dot(k_ref[pl.ds(at, chunk), :], masked[h], 1, 1)
                s_ref[pl.ds(at, chunk), :] = s
                return jnp.maximum(top, jnp.max(s, axis=0, keepdims=True))

            top = jnp.full((1, tile), NEGATIVE, F32)
            if near:
                sn = near_scores(h)
                top = jnp.max(sn, axis=0, keepdims=True)
            top = lax.fori_loop(0, steps, score, top)

            def weigh(c, carry):
                total, out = carry
                at = pl.multiple_of(c * chunk, chunk)
                e = jnp.exp2((s_ref[pl.ds(at, chunk), :] - top) * LOG2_E)
                low = e.astype(BF16)
                exp_ref[0, 0, h, pl.ds(at, chunk), :] = low
                part = dot(v_ref[pl.ds(at, chunk), :], low, 0, 0)[heads[h], :]
                return total + jnp.sum(e, axis=0, keepdims=True), out + part

            total = jnp.zeros((1, tile), F32)
            out = jnp.zeros((HEAD_DIM, tile), F32)
            if near:
                e = jnp.exp2((sn - top) * LOG2_E)
                low = e.astype(BF16)
                exp_ref[0, 0, h, far:, :] = low
                total = jnp.sum(e, axis=0, keepdims=True)
                out = dot(vnt[heads[h], :], low, 1, 0)
            total, out = lax.fori_loop(0, steps, weigh, (total, out))
            inverse = 1.0 / total
            inv_ref[0, 0, h : h + 1, :] = inverse
            outs.append(out * inverse)
        finish(outs)


def attention_forward(queries, keys_values, far, count, at, tile, into):
    near = into is not None
    total, width = queries.shape
    pairs = width // PAIR
    tiles = count // tile
    held = far + (tile if near else 0)
    block = at // tile
    specs = [
        pl.BlockSpec((tile, PAIR), lambda h, t: (block + t, h)),
        pl.BlockSpec((far, PAIR), lambda h, t: (0, 2 * h)),
        pl.BlockSpec((far, PAIR), lambda h, t: (0, 2 * h + 1)),
    ]
    operands = [queries, keys_values, keys_values]
    aliases = {}
    if near:
        first = far // tile
        specs += [
            pl.BlockSpec((tile, PAIR), lambda h, t: (first + t, 2 * h)),
            pl.BlockSpec((tile, PAIR), lambda h, t: (first + t, 2 * h + 1)),
            pl.BlockSpec(memory_space=pl.ANY),
        ]
        operands += [keys_values, keys_values, into]
        aliases = {5: 0}
    cells = count * held * width // HEAD_DIM
    return pl.pallas_call(
        functools.partial(attention_forward_kernel, near),
        grid=(pairs, tiles),
        in_specs=specs,
        out_specs=[
            pl.BlockSpec((tile, PAIR), lambda h, t: (block + t, h)),
            pl.BlockSpec((1, 1, 2, tile), lambda h, t: (h, t, 0, 0)),
            pl.BlockSpec((1, 1, 2, held, tile), lambda h, t: (h, t, 0, 0, 0)),
        ],
        out_shape=[
            jax.ShapeDtypeStruct((total, width), BF16),
            jax.ShapeDtypeStruct((pairs, tiles, 2, tile), F32),
            jax.ShapeDtypeStruct((pairs, tiles, 2, held, tile), BF16),
        ],
        scratch_shapes=[pltpu.VMEM((PAIR, far), BF16), pltpu.VMEM((far, tile), F32)],
        input_output_aliases=aliases,
        compiler_params=pltpu.CompilerParams(vmem_limit_bytes=VMEM_LIMIT),
        cost_estimate=pl.CostEstimate(
            flops=4 * cells * HEAD_DIM, bytes_accessed=2 * cells, transcendentals=cells
        ),
        name="attention_forward",
    )(*operands)


def attention_backward_kernel(cont_tiles, *refs):
    k_ref, v_ref, kn_ref, vn_ref = refs[:4]
    cont_refs, prompt_refs = refs[4:9], refs[9:14]
    rows_ref, prompt_rows_ref = refs[14:16]
    dq_ref, dkvn_ref, dkv_ref, weight_ref, sums_ref, kt_ref, dkt_ref, dvt_ref = refs[-8:]
    at = pl.program_id(1)

    @pl.when(at == 0)
    def _():
        kt_ref[...] = k_ref[...].T
        dkt_ref[...] = jnp.zeros_like(dkt_ref)
        dvt_ref[...] = jnp.zeros_like(dvt_ref)

    def tile_of(near, tile_refs, first):
        q_ref, out_ref, dout_ref, inv_ref, exp_ref = tile_refs
        far = k_ref.shape[0]
        tile = q_ref.shape[0]
        qt = q_ref[...].T
        dout = dout_ref[...].astype(F32).T
        product = out_ref[...].astype(F32).T * dout
        if near:
            knt = kn_ref[...].T
        zero = jnp.zeros((HEAD_DIM, tile), BF16)
        dqs, dkn, dvn = [], [], []
        for h in range(2):
            rows = slice(h * HEAD_DIM, (h + 1) * HEAD_DIM)
            inverse = inv_ref[0, 0, h : h + 1, :]
            delta = jnp.sum(product[rows, :], axis=0, keepdims=True) * inverse
            do = (dout[rows, :] * inverse).astype(BF16)
            padded = jnp.concatenate([do, zero] if h == 0 else [zero, do], 0)
            e = exp_ref[0, 0, h, 0:far, :]
            ds = (e.astype(F32) * (dot(v_ref[...], padded, 1, 0) - delta)).astype(BF16)
            dvt_ref[rows, :] += dot(do, e, 1, 1)
            dkt_ref[rows, :] += dot(qt[rows, :], ds, 1, 1)
            dq = dot(kt_ref[rows, :], ds, 1, 0)
            if near:
                e = exp_ref[0, 0, h, far:, :]
                ds = (e.astype(F32) * (dot(vn_ref[...], padded, 1, 0) - delta)).astype(BF16)
                dvn.append(dot(do, e, 1, 1))
                dkn.append(dot(qt[rows, :], ds, 1, 1))
                dq = dq + dot(knt[rows, :], ds, 1, 0)
            dqs.append(dq * HEAD_DIM ** (-0.5))
        row = pl.ds(pl.multiple_of(first, tile), tile)
        dq_ref[row, :] = jnp.concatenate(dqs, 0).T.astype(dq_ref.dtype)
        if near:
            dkvn_ref[row, :PAIR] = jnp.concatenate(dkn, 0).T.astype(dkvn_ref.dtype)
            dkvn_ref[row, PAIR:] = jnp.concatenate(dvn, 0).T.astype(dkvn_ref.dtype)

    @pl.when(at < cont_tiles)
    def _():
        tile_of(True, cont_refs, at * cont_refs[0].shape[0])

    @pl.when(at >= cont_tiles)
    def _():
        tile_of(False, prompt_refs, dkvn_ref.shape[0] + (at - cont_tiles) * prompt_refs[0].shape[0])

    @pl.when(at == pl.num_programs(1) - 1)
    def _():
        dkv_ref[:, :PAIR] = dkt_ref[...].T.astype(dkv_ref.dtype)
        dkv_ref[:, PAIR:] = dvt_ref[...].T.astype(dkv_ref.dtype)
        count = dkvn_ref.shape[0]
        weight_ref[:, :PAIR] = dot(rows_ref[...], dq_ref[...], 1, 0).astype(weight_ref.dtype)
        weight_ref[:, PAIR:] = (
            dot(prompt_rows_ref[...], dkv_ref[...], 1, 0)
            + dot(rows_ref[:, :count], dkvn_ref[...], 1, 0)
        ).astype(weight_ref.dtype)

        def sums_of(ref):
            return dot(jnp.ones((8, ref.shape[0]), BF16), ref[...], 1, 0)

        sums_ref[0, :, :PAIR] = sums_of(dq_ref)
        sums_ref[0, :, PAIR:] = sums_of(dkv_ref) + sums_of(dkvn_ref)


def attention_backward(
    queries, keys_values, far, context, d_context, cont_held, prompt_held, rows_t, prompt_t, h0, nh,
    into,
):
    total, width = queries.shape
    cont_tiles, length = cont_held[1].shape[1], cont_held[1].shape[4]
    tiles, tile = prompt_held[1].shape[1], prompt_held[1].shape[4]
    count = cont_tiles * length
    first, behind = far // length, count // tile

    def cont_at(t):
        return jnp.minimum(t, cont_tiles - 1)

    def prompt_at(t):
        return jnp.maximum(t - cont_tiles, 0)

    def tile_specs(size, held, start, at):
        row = pl.BlockSpec((size, PAIR), lambda h, t: (start + at(t), h0 + h))
        return [
            row,
            row,
            row,
            pl.BlockSpec((1, 1, 2, size), lambda h, t: (h0 + h, at(t), 0, 0)),
            pl.BlockSpec((1, 1, 2, held, size), lambda h, t: (h0 + h, at(t), 0, 0, 0)),
        ]

    specs = [
        pl.BlockSpec((far, PAIR), lambda h, t: (0, 2 * (h0 + h))),
        pl.BlockSpec((far, PAIR), lambda h, t: (0, 2 * (h0 + h) + 1)),
        pl.BlockSpec((length, PAIR), lambda h, t: (first + cont_at(t), 2 * (h0 + h))),
        pl.BlockSpec((length, PAIR), lambda h, t: (first + cont_at(t), 2 * (h0 + h) + 1)),
    ]
    specs += tile_specs(length, far + length, 0, cont_at)
    specs += tile_specs(tile, far, behind, prompt_at)
    whole = pl.Buffered(1)
    specs += [
        pl.BlockSpec((width, total), lambda h, t: (0, 0), pipeline_mode=whole),
        pl.BlockSpec((width, far), lambda h, t: (0, 0), pipeline_mode=whole),
    ]
    specs += [pl.BlockSpec(memory_space=pl.ANY)] * len(into)
    wide = 2 * PAIR
    cells = (count * (far + length) + tiles * tile * far) * nh * 2
    return pl.pallas_call(
        functools.partial(attention_backward_kernel, cont_tiles),
        grid=(nh, cont_tiles + tiles),
        in_specs=specs,
        out_specs=[
            pl.BlockSpec((total, PAIR), lambda h, t: (0, h0 + h)),
            pl.BlockSpec((count, wide), lambda h, t: (0, h0 + h)),
            pl.BlockSpec((far, wide), lambda h, t: (0, h)),
            pl.BlockSpec((width, 3 * PAIR), lambda h, t: (0, h)),
            pl.BlockSpec((1, 8, 3 * PAIR), lambda h, t: (h, 0, 0)),
        ],
        out_shape=[
            jax.ShapeDtypeStruct((total, width), BF16),
            jax.ShapeDtypeStruct((count, 2 * width), BF16),
            jax.ShapeDtypeStruct((far, nh * wide), BF16),
            jax.ShapeDtypeStruct((width, nh * 3 * PAIR), BF16),
            jax.ShapeDtypeStruct((nh, 8, 3 * PAIR), F32),
        ],
        scratch_shapes=[
            pltpu.VMEM((PAIR, far), BF16),
            pltpu.VMEM((PAIR, far), F32),
            pltpu.VMEM((PAIR, far), F32),
        ],
        input_output_aliases={16 + n: n for n in range(len(into))},
        compiler_params=pltpu.CompilerParams(vmem_limit_bytes=VMEM_LIMIT),
        cost_estimate=pl.CostEstimate(flops=cells, bytes_accessed=cells // 16, transcendentals=0),
        name="attention_backward",
    )(
        keys_values, keys_values, keys_values, keys_values,
        queries, context, d_context, *cont_held,
        queries, context, d_context, *prompt_held,
        rows_t, prompt_t, *into,
    )


def turn_kernel(x_ref, out_ref):
    out_ref[...] = x_ref[...].T


def turned(rows):
    count, width = rows.shape
    tile = count // 2 if (count // 2) % PAIR == 0 else count
    return pl.pallas_call(
        turn_kernel,
        grid=(count // tile,),
        in_specs=[pl.BlockSpec((tile, width), lambda t: (t, 0))],
        out_specs=pl.BlockSpec((width, tile), lambda t: (0, t)),
        out_shape=jax.ShapeDtypeStruct((width, count), rows.dtype),
        compiler_params=pltpu.CompilerParams(vmem_limit_bytes=VMEM_LIMIT),
        name="turn",
    )(rows)


def gelu_pair(pre):
    half = 0.5 * (1.0 + lax.erf(pre * (0.5**0.5)))
    slope = half + pre * (jnp.exp(-0.5 * pre * pre) * 0.3989422804014327)
    return pre * half, slope


def exact(left, right, left_dim, right_dim):
    return lax.dot_general(
        left,
        right,
        (((left_dim,), (right_dim,)), ((), ())),
        precision=HIGHEST,
        preferred_element_type=F32,
    )


def total_of(array):
    return jnp.sum(array, axis=0, keepdims=True)


def dense_kernel(cont_tiles, length, classes, *refs):
    (
        label_ref, x_ref, context_ref, cot_ref, first_weight_ref, reduce_ref, vector_ref, ebias_ref,
        student_ref, head_ref, pool_ref, class_ref,
        layer_ref, logits_ref, first_ref, hidden_ref, dmixed_ref, dpre_ref, dinner_ref,
        dinner_low_ref, dcontext_ref, small_ref, expand_sum_ref,
        hat_ref, mixed_ref, slope_ref, cotangent_ref,
    ) = refs
    at = pl.program_id(0)
    count, width = x_ref.shape
    lanes = student_ref.shape[1]
    inner = hidden_ref.shape[1]
    chunk = width
    obias, fgain, fshift, rbias, sgain, sshift = (vector_ref[i : i + 1, :] for i in range(2, 8))
    vectors_at = width + 2 * lanes + 4

    @pl.when(at == 0)
    def _():
        small_ref[...] = jnp.zeros_like(small_ref)
        expand_sum_ref[...] = jnp.zeros_like(expand_sum_ref)

    def add_vector(which, row):
        start = vectors_at + which * (width // lanes)
        for i in range(width // lanes):
            small_ref[start + i : start + i + 1, :] += row[:, i * lanes : (i + 1) * lanes]

    def normal(rows):
        center = rows - jnp.mean(rows, -1, keepdims=True)
        scale = lax.rsqrt(jnp.mean(center * center, -1, keepdims=True) + EPSILON)
        return center * scale, scale

    def normal_back(grad, hat, scale, gain):
        scaled = grad * gain
        return scale * (
            scaled
            - jnp.mean(scaled, -1, keepdims=True)
            - hat * jnp.mean(scaled * hat, -1, keepdims=True)
        )

    branch = dot(context_ref[...], first_weight_ref[:, :width], 1, 0) + obias
    hat, first_scale = normal(x_ref[...].astype(F32) + branch)
    hat_ref[...] = hat
    first = hat * fgain + fshift
    first_ref[...] = first.astype(BF16)
    mixed_ref[...] = first + rbias

    @pl.loop(0, inner // chunk)
    def _(c):
        columns = pl.ds(pl.multiple_of(c * chunk, chunk), chunk)
        behind = pl.ds(pl.multiple_of(width + c * chunk, chunk), chunk)
        pre = dot(first_ref[...], first_weight_ref[:, behind], 1, 0) + ebias_ref[:, columns]
        hidden, slope = gelu_pair(pre)
        hidden = hidden.astype(BF16)
        hidden_ref[:, columns] = hidden
        slope_ref[:, columns] = slope.astype(BF16)
        mixed_ref[...] += dot(hidden, reduce_ref[columns, :], 1, 0)

    hat, scale = normal(mixed_ref[...])
    layer_ref[...] = (hat * sgain + sshift).astype(BF16)
    mixed_ref[...] = hat
    cotangent_ref[...] = cot_ref[...].astype(F32)

    if cont_tiles:

        @pl.when(at < cont_tiles)
        def _():
            student_bias, query, pool_bias, class_bias = (head_ref[i : i + 1, :] for i in range(4))
            lane = lax.broadcasted_iota(jnp.int32, (lanes, lanes), 0) // (lanes // POOL_HEADS)
            same = jnp.where(
                lane == lax.broadcasted_iota(jnp.int32, (lanes, lanes), 1) // (lanes // POOL_HEADS),
                1.0,
                0.0,
            )
            scale = (lanes // POOL_HEADS) ** (-0.5)
            kind = lax.broadcasted_iota(jnp.int32, (1, lanes), 1)

            def eight(row):
                pad = lax.broadcasted_iota(jnp.int32, (8, lanes), 0) == 0
                return jnp.where(pad, jnp.broadcast_to(row, (8, lanes)), 0.0)

            @pl.loop(0, count // length)
            def _(c):
                rows = pl.ds(pl.multiple_of(c * length, length), length)
                layer = layer_ref[rows, :]
                student = dot(layer, student_ref[...], 1, 0) + student_bias
                scores = exact(student * query, same, 1, 0) * scale
                weights = jnp.exp(scores - jnp.max(scores, axis=0, keepdims=True))
                weights = weights / total_of(weights)
                pooled = total_of(weights * student)
                hidden = jnp.tanh(exact(eight(pooled), pool_ref[...], 1, 0)[0:1] + pool_bias)
                logits = exact(eight(hidden), class_ref[...], 1, 0)[0:1] + class_bias
                which = at * (count // length) + c
                logits_ref[pl.ds(which, 1), :] = logits
                logits = jnp.where(kind < classes, logits, NEGATIVE)
                chance = jnp.exp(logits - jnp.max(logits, axis=1, keepdims=True))
                chance = chance / jnp.sum(chance, axis=1, keepdims=True)
                d_logits = chance - jnp.where(kind == label_ref[which], 1.0, 0.0)
                d_hidden = exact(eight(d_logits), class_ref[...], 1, 1)[0:1]
                d_sum = d_hidden * (1.0 - hidden * hidden)
                d_pooled = exact(eight(d_sum), pool_ref[...], 1, 1)[0:1]
                d_weights = exact(student * d_pooled, same, 1, 0)
                d_scores = weights * (d_weights - total_of(weights * d_weights)) * scale
                d_student = weights * d_pooled + d_scores * query
                d_low = d_student.astype(BF16)
                cotangent_ref[rows, :] += dot(d_low, student_ref[...], 1, 1)
                small_ref[:width, :] += dot(layer, d_low, 0, 0)
                small_ref[width : width + lanes, :] += exact(eight(pooled), eight(d_sum), 0, 0)
                small_ref[width + lanes : width + 2 * lanes, :] += exact(
                    eight(hidden), eight(d_logits), 0, 0
                )
                start = width + 2 * lanes
                small_ref[start : start + 1, :] += total_of(d_student)
                small_ref[start + 1 : start + 2, :] += total_of(d_scores * student)
                small_ref[start + 2 : start + 3, :] += d_sum
                small_ref[start + 3 : start + 4, :] += d_logits

    cotangent = cotangent_ref[...]
    hat = mixed_ref[...]
    add_vector(4, total_of(cotangent * hat))
    add_vector(5, total_of(cotangent))
    d_mixed = normal_back(cotangent, hat, scale, sgain)
    add_vector(3, total_of(d_mixed))
    dmixed_ref[...] = d_mixed.astype(BF16)
    cotangent_ref[...] = d_mixed

    @pl.loop(0, inner // chunk)
    def _(c):
        columns = pl.ds(pl.multiple_of(c * chunk, chunk), chunk)
        behind = pl.ds(pl.multiple_of(width + c * chunk, chunk), chunk)
        d_pre = dot(dmixed_ref[...], reduce_ref[columns, :], 1, 1) * slope_ref[
            :, columns
        ].astype(F32)
        expand_sum_ref[:, columns] += jnp.sum(d_pre.reshape(-1, 8, chunk), axis=0)
        d_pre = d_pre.astype(BF16)
        dpre_ref[:, columns] = d_pre
        cotangent_ref[...] += dot(d_pre, first_weight_ref[:, behind], 1, 1)

    d_first = cotangent_ref[...]
    hat = hat_ref[...]
    add_vector(1, total_of(d_first * hat))
    add_vector(2, total_of(d_first))
    d_inner = normal_back(d_first, hat, first_scale, fgain)
    add_vector(0, total_of(d_inner))
    dinner_ref[...] = d_inner
    low = d_inner.astype(BF16)
    dinner_low_ref[...] = low
    dcontext_ref[...] = dot(low, first_weight_ref[:, :width], 1, 1).astype(BF16)

    @pl.when(at == pl.num_programs(0) - 1)
    def _():
        start = vectors_at + 6 * (width // lanes)
        for i in range(inner // lanes):
            small_ref[start + i : start + i + 1, :] = total_of(
                expand_sum_ref[:, i * lanes : (i + 1) * lanes]
            )


def dense(labels, rows, context, cotangents, weights, start, count, tile, cont_tiles, length):
    first_weight, reduce_full, vectors, ebias, student, head, pool, classify, classes = weights
    width, inner = rows.shape[1], reduce_full.shape[0]
    lanes = student.shape[1]
    first = start // tile
    small_rows = width + 2 * lanes + 4 + (6 * width + inner) // lanes
    small_rows += -small_rows % 8

    def row(size, behind=0):
        return pl.BlockSpec((tile, size), lambda t: (behind + t, 0))

    def whole(array):
        return pl.BlockSpec(array.shape, lambda t: (0, 0), pipeline_mode=pl.Buffered(1))

    def kept(shape):
        return pl.BlockSpec(shape, lambda t: (0, 0))

    conts = labels.shape[0]
    low, high = BF16, F32
    outs = [
        (width, low), None, (width, low), (inner, low), (width, low), (inner, low), (width, high),
        (width, low), (width, low),
    ]
    fixed = [whole(w) for w in (first_weight, reduce_full, vectors, ebias, student, head, pool, classify)]
    weight_cells = first_weight.size + reduce_full.size
    return pl.pallas_call(
        functools.partial(dense_kernel, cont_tiles, length, classes),
        grid=(count // tile,),
        in_specs=[pl.BlockSpec(memory_space=pltpu.SMEM), row(width, first), row(width, first)]
        + [row(width, first)]
        + fixed,
        out_specs=[row(o[0]) if o else kept((conts, lanes)) for o in outs]
        + [kept((small_rows, lanes)), kept((8, inner))],
        out_shape=[
            jax.ShapeDtypeStruct((count, o[0]) if o else (conts, lanes), o[1] if o else F32)
            for o in outs
        ]
        + [
            jax.ShapeDtypeStruct((small_rows, lanes), F32),
            jax.ShapeDtypeStruct((8, inner), F32),
        ],
        scratch_shapes=[
            pltpu.VMEM((tile, width), F32),
            pltpu.VMEM((tile, width), F32),
            pltpu.VMEM((tile, inner), BF16),
            pltpu.VMEM((tile, width), F32),
        ],
        compiler_params=pltpu.CompilerParams(vmem_limit_bytes=VMEM_LIMIT),
        cost_estimate=pl.CostEstimate(
            flops=4 * count * weight_cells,
            bytes_accessed=2 * weight_cells + 20 * count * (width + inner) // 4,
            transcendentals=2 * count * inner,
        ),
        name="dense",
    )(
        labels, rows, context, cotangents, first_weight, reduce_full, vectors, ebias, student, head,
        pool, classify,
    )


def rows_back_kernel(d_inner_ref, dq_ref, dkv_ref, joint_ref, out_ref):
    width = dq_ref.shape[1]
    out_ref[...] = (
        d_inner_ref[...]
        + dot(dq_ref[...], joint_ref[:, :width], 1, 1)
        + dot(dkv_ref[...], joint_ref[:, width : 3 * width], 1, 1)
    )


def rows_back(d_inner, d_queries, d_kv, joint, start, count, tile):
    width = d_inner.shape[1]
    first = start // tile
    return pl.pallas_call(
        rows_back_kernel,
        grid=(count // tile,),
        in_specs=[
            pl.BlockSpec((tile, width), lambda t: (first + t, 0)),
            pl.BlockSpec((tile, width), lambda t: (first + t, 0)),
            pl.BlockSpec((tile, 2 * width), lambda t: (t, 0)),
            pl.BlockSpec(joint.shape, lambda t: (0, 0), pipeline_mode=pl.Buffered(1)),
        ],
        out_specs=pl.BlockSpec((tile, width), lambda t: (t, 0)),
        out_shape=jax.ShapeDtypeStruct((count, width), F32),
        compiler_params=pltpu.CompilerParams(vmem_limit_bytes=VMEM_LIMIT),
        cost_estimate=pl.CostEstimate(flops=count, bytes_accessed=count, transcendentals=0),
        name="rows_back",
    )(d_inner, d_queries, d_kv, joint)


def bits_of(axis):
    size = lax.axis_size(axis)
    return [(axis, 1 << b) for b in reversed(range(size.bit_length() - 1))]


def across(array, axis, bit):
    return lax.ppermute(array, axis, [(i, i ^ bit) for i in range(lax.axis_size(axis))])


def bit_set(axis, bit):
    return (lax.axis_index(axis) // bit) % 2


def gather_bits(shard, order, dims):
    held = shard.reshape((1,) * len(dims) + shard.shape)
    for axis, bit in order:
        dim = dims.index((axis, bit))
        other = across(held, axis, bit)
        held = jnp.where(
            bit_set(axis, bit) == 0,
            jnp.concatenate([held, other], dim),
            jnp.concatenate([other, held], dim),
        )
    return held


def gather_relative(shard, axis):
    bits = bits_of(axis)
    held = shard.reshape((1,) * len(bits) + shard.shape)
    for dim, (_, bit) in enumerate(bits):
        held = jnp.concatenate([held, across(held, axis, bit)], dim)
    return held.reshape((-1,) + shard.shape[1:])


class Halves:
    def __init__(self, blocks):
        self.shape = blocks.shape[1:]
        self.bits = bits_of("seq")
        self.held = blocks
        self.split()

    def split(self):
        both = self.held.reshape((-1, 2) + self.shape)
        self.keep, self.give = both[:, 0], both[:, 1]

    def send(self):
        self.other = across(self.give, *self.bits.pop())

    def take(self):
        self.held = (self.keep.astype(F32) + self.other.astype(F32)).astype(BF16)
        if not self.bits:
            self.held = self.held.reshape(self.shape)
            return False
        self.split()
        return True

    def waiting(self):
        return self.give if self.bits else self.held

    def tied(self, value):
        if self.bits:
            self.give = value
        else:
            self.held = value


class Spread:
    def __init__(self, blocks):
        self.held, self.sent = blocks, False

    def send(self):
        self.other, self.sent = lax.all_to_all(self.held, BOTH, 0, 0), True

    def take(self):
        self.held = jnp.sum(self.other.astype(F32), 0)
        return False

    def waiting(self):
        return self.held

    def tied(self, value):
        self.held = value


class Sum:
    def __init__(self, value, order):
        self.held, self.order = value.astype(BF16), list(order)

    def send(self):
        axis, bit = self.order.pop(0)
        self.other = across(self.held, axis, bit)

    def take(self):
        self.held = self.held.astype(F32) + self.other.astype(F32)
        if self.order:
            self.held = self.held.astype(BF16)
        return bool(self.order)

    def waiting(self):
        return self.held

    def tied(self, value):
        self.held = value


class Exchanges:
    def __init__(self):
        self.live = []

    def add(self, chain):
        self.live.append((chain, True))
        return chain

    def step(self, value):
        going, flat = [], []
        for chain, new in self.live:
            if new or chain.take():
                going.append(chain)
        if value is not None:
            chains = [chain for chain, _ in self.live]
            value, flat = lax.optimization_barrier((value, [c.waiting() for c in chains]))
            for chain, tied in zip(chains, flat):
                chain.tied(tied)
        self.live = [(chain, False) for chain in going]
        for chain in going:
            chain.send()
        return value

    def finish(self):
        while self.live:
            self.step(None)


def local(
    prompt_in,
    cont_in,
    prompt_cot,
    cont_cot,
    labels,
    joint_weight,
    query_bias,
    value_bias,
    output_weight,
    output_bias,
    first_gain,
    first_shift,
    expand_weight,
    expand_bias,
    reduce_weight,
    reduce_bias,
    second_gain,
    second_shift,
    student_weight,
    student_bias,
    pool_query,
    pool_weight,
    pool_bias,
    class_weight,
    class_bias,
):
    prompt_rows = prompt_in[0]
    share, width = prompt_rows.shape
    _, conts, length, _ = cont_in.shape
    cont_count = conts * length
    part = joint_weight.shape[0]
    devices = width // part
    hidden_width = expand_weight.shape[1]
    fold = hidden_width // width
    tile = min(share, length)
    grp_bits, seq_bits = bits_of("grp"), bits_of("seq")
    dims = grp_bits + seq_bits
    gather_orders = (
        grp_bits + seq_bits,
        grp_bits[:-1] + seq_bits[:-1] + grp_bits[-1:] + seq_bits[-1:],
    )

    pairs = width // PAIR
    groups = [3, 2, 1] if pairs == 6 else [pairs]
    joint_low = joint_weight.astype(BF16)
    vectors = [
        query_bias,
        value_bias,
        output_bias,
        first_gain,
        first_shift,
        reduce_bias,
        second_gain,
        second_shift,
    ]
    beside = jnp.concatenate([v[None] for v in vectors], 0).astype(BF16).T
    beside = jnp.concatenate([beside, expand_bias.astype(BF16).reshape(part, fold)], 1)
    lanes = student_weight.shape[1]
    own_joint = [joint_low[:, :width]]
    for h in range(pairs):
        own_joint += [joint_low[:, (s * pairs + h) * PAIR :][:, :PAIR] for s in (1, 2)]
    own_joint.append(jnp.pad(beside, ((0, 0), (0, lanes - beside.shape[1]))))
    own_joint = jnp.concatenate(own_joint, 1)
    half = (3 * width // 2 + lanes) // PAIR * PAIR
    joint_all = jnp.concatenate(
        [
            gather_bits(piece, order, dims).reshape(width, -1)
            for piece, order in zip((own_joint[:, :half], own_joint[:, half:]), gather_orders)
        ],
        1,
    )
    joint_full = joint_all[:, : 3 * width]
    flat = joint_all[:, 3 * width :].astype(F32)
    by_vector = flat[:, : len(vectors)].T
    qbias, vbias = by_vector[0], by_vector[1]
    ebias = flat[:, 8 : 8 + fold].reshape(hidden_width)
    prompt_all = gather_relative(prompt_rows, "seq")
    far = prompt_all.shape[0]
    out_expand = lax.all_gather(
        jnp.concatenate([output_weight, expand_weight], 1).astype(BF16), BOTH, axis=0, tiled=True
    )
    reduce_full = lax.all_gather(reduce_weight.astype(BF16), BOTH, axis=0, tiled=True)

    cont_rows = cont_in[0].reshape(cont_count, width)
    rows = jnp.concatenate([cont_rows, prompt_rows], 0)
    key_rows = jnp.concatenate([prompt_all, cont_rows], 0)
    rows_t, prompt_t = turned(rows), turned(prompt_all)
    queries = (dot(rows, joint_full[:, :width], 1, 0) + qbias).astype(BF16) * HEAD_DIM ** (-0.5)
    kv_bias = jnp.pad(vbias.reshape(pairs, 1, PAIR), ((0, 0), (1, 0), (0, 0))).reshape(-1)
    keys_values = (dot(key_rows, joint_full[:, width:], 1, 0) + kv_bias).astype(BF16)

    context, prompt_inv, prompt_exp = attention_forward(
        queries, keys_values, far, share, cont_count, tile, None
    )
    context, cont_inv, cont_exp = attention_forward(
        queries, keys_values, far, cont_count, 0, length, context
    )

    classes = class_weight.shape[1]
    head = jnp.concatenate(
        [student_bias, pool_query, pool_bias, jnp.pad(class_bias, (0, lanes - classes))]
    ).reshape(4, lanes)
    weights = (
        out_expand,
        reduce_full,
        by_vector,
        ebias[None],
        student_weight.astype(BF16),
        jnp.pad(head, ((0, 4), (0, 0))),
        pool_weight,
        jnp.pad(class_weight, ((0, 0), (0, lanes - classes))),
        classes,
    )
    cotangents = jnp.concatenate([cont_cot[0].reshape(cont_count, width), prompt_cot[0]], 0)
    cont_tile = min(2 * length, cont_count)
    if cont_tile == share:
        results = dense(
            labels[0], rows, context, cotangents, weights, 0, rows.shape[0], share,
            cont_count // cont_tile, length,
        )
    else:
        of_conts = dense(
            labels[0], rows, context, cotangents, weights, 0, cont_count, cont_tile,
            cont_count // cont_tile, length,
        )
        of_prompt = dense(
            labels[0], rows, context, cotangents, weights, cont_count, share, share, 0, length
        )
        results = [
            of_conts[i]
            if i == 1
            else of_conts[i] + of_prompt[i]
            if i > 8
            else jnp.concatenate([of_conts[i], of_prompt[i]], 0)
            for i in range(len(of_conts))
        ]
    layer_low, logits, first_low, hidden, d_mixed_low, d_pre_low, d_inner = results[:7]
    d_inner_low, d_context, small = results[7:10]
    logits = logits[:, :classes]
    cont_layer = layer_low[:cont_count]
    exchanges = Exchanges()
    small = exchanges.add(Sum(small, dims))
    d_reduce_weight = dot(hidden, d_mixed_low, 0, 0).astype(BF16)
    d_expand_weight = dot(first_low, d_pre_low, 0, 0).astype(BF16)
    d_output_weight = dot(context, d_inner_low, 0, 0).astype(BF16)

    blocks = [d_output_weight.reshape(devices, part, width)]
    blocks += [
        d_expand_weight[:, i * width : (i + 1) * width].reshape(devices, part, width)
        for i in range(fold)
    ]
    blocks += [d_reduce_weight.reshape(devices, -1, width)]
    blocks, d_context, d_inner, rows_t, prompt_t = lax.optimization_barrier(
        (jnp.concatenate(blocks, 1), d_context, d_inner, rows_t, prompt_t)
    )
    early = lax.psum_scatter(blocks, BOTH, scatter_dimension=0, tiled=True)

    into, owns, joint_parts, sums = (), [], [], []
    h0 = 0
    for nh in groups:
        d_context = exchanges.step(d_context)
        *into, dkv_far, d_joint, sum_rows = attention_backward(
            queries, keys_values, far, context, d_context, (cont_inv, cont_exp),
            (prompt_inv, prompt_exp), rows_t, prompt_t, h0, nh, into,
        )
        if h0 + nh == pairs:
            sums.append(sum_rows[:, 0])
            sums = jnp.concatenate(sums, 0)
            sums = [sums[:, i * PAIR : (i + 1) * PAIR].reshape(devices, 1, part) for i in (0, 2)]
            sums = jnp.concatenate(sums, 1).astype(BF16)
            sums = jnp.pad(sums, ((0, 0), (0, 6), (0, 3 * nh * PAIR - part)))
            d_joint = jnp.concatenate([d_joint.reshape(devices, part, -1), sums], 1)
        else:
            sums.append(sum_rows[:, 0])
        owns.append(exchanges.add(Halves(dkv_far.reshape(-1, share, dkv_far.shape[1]))))
        joint_parts.append(exchanges.add(Spread(d_joint.reshape(devices, -1, 3 * nh * PAIR))))
        h0 += nh
    d_queries, d_kv = into
    early, d_queries = exchanges.step((early, d_queries))
    d_cont_rows = rows_back(d_inner, d_queries, d_kv, joint_all, 0, cont_count, cont_tile)
    exchanges.finish()
    early = early[0].astype(F32)
    output_grad = early[:part]
    expand_grad = jnp.concatenate(
        [early[part * (1 + i) : part * (2 + i)] for i in range(fold)], 1
    )
    reduce_grad = early[part * (1 + fold) :]
    parts = [p.held for p in joint_parts]
    joint_grad = jnp.concatenate(
        [p[:part].reshape(part, nh, 3, PAIR) for p, nh in zip(parts, groups)], 1
    )
    joint_grad = joint_grad.transpose(0, 2, 1, 3).reshape(part, 3 * width)

    d_own = jnp.concatenate([o.held.astype(BF16) for o in owns], 1)
    d_prompt_rows = rows_back(d_inner, d_queries, d_own, joint_all, cont_count, share, share)

    small = small.held
    index = lax.axis_index(BOTH)
    at = width + lanes
    head_grads = (
        small[:width],
        small[at + lanes],
        small[at + lanes + 1],
        small[width:at],
        small[at + lanes + 2],
        small[at : at + lanes, :classes],
        small[at + lanes + 3, :classes],
    )
    at += lanes + 4
    vector_grads = []
    for row in (part, part + 1):
        vector_grads.append(parts[-1][row, :part])
    for size in [width] * 6 + [hidden_width]:
        vector = small[at : at + size // lanes].reshape(size)
        own = size // devices
        vector_grads.append(lax.dynamic_slice(vector, (index * own,), (own,)))
        at += size // lanes
    (g_qbias, g_vbias, g_obias, g_fgain, g_fshift, g_rbias, g_sgain, g_sshift, g_ebias) = vector_grads
    return (
        layer_low[cont_count:][None],
        cont_layer.reshape(1, conts, length, width),
        logits[None],
        d_prompt_rows[None],
        d_cont_rows.reshape(1, conts, length, width),
        joint_grad,
        g_qbias,
        g_vbias,
        output_grad,
        g_obias,
        g_fgain,
        g_fshift,
        expand_grad,
        g_ebias,
        reduce_grad,
        g_rbias,
        g_sgain,
        g_sshift,
    ) + head_grads


def solution(mesh):
    placed = (
        P("grp", "seq", None),
        P("grp", "seq", None, None),
        P("grp", "seq", None),
        P("grp", "seq", None, None),
        P("grp", "seq"),
        P(("grp", "seq"), None),
        P(("grp", "seq")),
        P(("grp", "seq")),
        P(("grp", "seq"), None),
        P(("grp", "seq")),
        P(("grp", "seq")),
        P(("grp", "seq")),
        P(("grp", "seq"), None),
        P(("grp", "seq")),
        P(("grp", "seq"), None),
        P(("grp", "seq")),
        P(("grp", "seq")),
        P(("grp", "seq")),
        P(),
        P(),
        P(),
        P(),
        P(),
        P(),
        P(),
    )
    return jax.shard_map(
        local,
        mesh=mesh,
        in_specs=placed,
        out_specs=(
            P("grp", "seq", None),
            P("grp", "seq", None, None),
            P("grp", "seq", None),
            P("grp", "seq", None),
            P("grp", "seq", None, None),
            P(("grp", "seq"), None),
            P(("grp", "seq")),
            P(("grp", "seq")),
            P(("grp", "seq"), None),
            P(("grp", "seq")),
            P(("grp", "seq")),
            P(("grp", "seq")),
            P(("grp", "seq"), None),
            P(("grp", "seq")),
            P(("grp", "seq"), None),
            P(("grp", "seq")),
            P(("grp", "seq")),
            P(("grp", "seq")),
            P(),
            P(),
            P(),
            P(),
            P(),
            P(),
            P(),
        ),
        check_vma=False,
    )
```

```python
import functools

import jax
import jax.numpy as jnp
from jax import lax
from jax.experimental import pallas as pl
from jax.experimental.pallas import tpu as pltpu
from jax.sharding import PartitionSpec as P

HEAD_DIM = 64
POOL_HEADS = 2
PAIR = 2 * HEAD_DIM

EPSILON = 1e-06
HIGHEST = lax.Precision.HIGHEST
NEGATIVE = -1e30
BOTH = ("grp", "seq")
BF16 = jnp.bfloat16
F32 = jnp.float32
LOG2_E = 1.4426950408889634
SUM_LOW, SUM_HIGH = 1e-12, 1e18
VMEM_LIMIT = 56 << 20


def dot(left, right, left_dim, right_dim):
    return lax.dot_general(
        left, right, (((left_dim,), (right_dim,)), ((), ())), preferred_element_type=F32
    )


def precise(left, right):
    return jnp.dot(left, right, precision=HIGHEST, preferred_element_type=F32)


def attention_forward_kernel(near, *refs):
    if near:
        q_ref, k_ref, v_ref, kn_ref, vn_ref, _, out_ref, inv_ref, exp_ref, vt_ref, s_ref = refs
    else:
        q_ref, k_ref, v_ref, out_ref, inv_ref, exp_ref, vt_ref, s_ref = refs
    far = k_ref.shape[0]
    tile = q_ref.shape[0]

    @pl.when(pl.program_id(1) == 0)
    def _():
        vt_ref[...] = v_ref[...].T

    q = q_ref[...]
    lane = lax.broadcasted_iota(jnp.int32, q.shape, 1)
    masked = [
        jnp.where((lane < HEAD_DIM) if h == 0 else (lane >= HEAD_DIM), q, jnp.zeros_like(q))
        for h in range(2)
    ]
    heads = [slice(h * HEAD_DIM, (h + 1) * HEAD_DIM) for h in range(2)]
    if near:
        vnt = vn_ref[...].T
        allowed = lax.broadcasted_iota(jnp.int32, (tile, tile), 0) <= lax.broadcasted_iota(
            jnp.int32, (tile, tile), 1
        )

    def near_scores(h):
        return jnp.where(allowed, dot(kn_ref[...], masked[h], 1, 1), NEGATIVE)

    def finish(outs):
        out_ref[...] = jnp.concatenate(outs, 0).T.astype(out_ref.dtype)

    outs = []
    fine = None
    for h in range(2):
        e = jnp.exp2(dot(k_ref[...], masked[h], 1, 1) * LOG2_E)
        total = jnp.sum(e, axis=0, keepdims=True)
        low = e.astype(BF16)
        exp_ref[0, 0, h, 0:far, :] = low
        out = dot(vt_ref[heads[h], :], low, 1, 0)
        if near:
            e = jnp.exp2(near_scores(h) * LOG2_E)
            total = total + jnp.sum(e, axis=0, keepdims=True)
            low = e.astype(BF16)
            exp_ref[0, 0, h, far:, :] = low
            out = out + dot(vnt[heads[h], :], low, 1, 0)
        inverse = 1.0 / total
        inv_ref[0, 0, h : h + 1, :] = inverse
        outs.append(out * inverse)
        good = jnp.where((total > SUM_LOW) & (total < SUM_HIGH), 1.0, 0.0)
        fine = good if fine is None else jnp.minimum(fine, good)
    finish(outs)

    @pl.when(jnp.min(fine) < 0.5)
    def _():
        chunk = tile
        steps = far // chunk
        outs = []
        for h in range(2):

            def score(c, top):
                at = pl.multiple_of(c * chunk, chunk)
                s = dot(k_ref[pl.ds(at, chunk), :], masked[h], 1, 1)
                s_ref[pl.ds(at, chunk), :] = s
                return jnp.maximum(top, jnp.max(s, axis=0, keepdims=True))

            top = jnp.full((1, tile), NEGATIVE, F32)
            if near:
                sn = near_scores(h)
                top = jnp.max(sn, axis=0, keepdims=True)
            top = lax.fori_loop(0, steps, score, top)

            def weigh(c, carry):
                total, out = carry
                at = pl.multiple_of(c * chunk, chunk)
                e = jnp.exp2((s_ref[pl.ds(at, chunk), :] - top) * LOG2_E)
                low = e.astype(BF16)
                exp_ref[0, 0, h, pl.ds(at, chunk), :] = low
                part = dot(v_ref[pl.ds(at, chunk), :], low, 0, 0)[heads[h], :]
                return total + jnp.sum(e, axis=0, keepdims=True), out + part

            total = jnp.zeros((1, tile), F32)
            out = jnp.zeros((HEAD_DIM, tile), F32)
            if near:
                e = jnp.exp2((sn - top) * LOG2_E)
                low = e.astype(BF16)
                exp_ref[0, 0, h, far:, :] = low
                total = jnp.sum(e, axis=0, keepdims=True)
                out = dot(vnt[heads[h], :], low, 1, 0)
            total, out = lax.fori_loop(0, steps, weigh, (total, out))
            inverse = 1.0 / total
            inv_ref[0, 0, h : h + 1, :] = inverse
            outs.append(out * inverse)
        finish(outs)


def attention_forward(queries, keys_values, far, count, at, tile, into):
    near = into is not None
    total, width = queries.shape
    pairs = width // PAIR
    tiles = count // tile
    held = far + (tile if near else 0)
    block = at // tile
    specs = [
        pl.BlockSpec((tile, PAIR), lambda h, t: (block + t, h)),
        pl.BlockSpec((far, PAIR), lambda h, t: (0, 2 * h)),
        pl.BlockSpec((far, PAIR), lambda h, t: (0, 2 * h + 1)),
    ]
    operands = [queries, keys_values, keys_values]
    aliases = {}
    if near:
        first = far // tile
        specs += [
            pl.BlockSpec((tile, PAIR), lambda h, t: (first + t, 2 * h)),
            pl.BlockSpec((tile, PAIR), lambda h, t: (first + t, 2 * h + 1)),
            pl.BlockSpec(memory_space=pl.ANY),
        ]
        operands += [keys_values, keys_values, into]
        aliases = {5: 0}
    cells = count * held * width // HEAD_DIM
    return pl.pallas_call(
        functools.partial(attention_forward_kernel, near),
        grid=(pairs, tiles),
        in_specs=specs,
        out_specs=[
            pl.BlockSpec((tile, PAIR), lambda h, t: (block + t, h)),
            pl.BlockSpec((1, 1, 2, tile), lambda h, t: (h, t, 0, 0)),
            pl.BlockSpec((1, 1, 2, held, tile), lambda h, t: (h, t, 0, 0, 0)),
        ],
        out_shape=[
            jax.ShapeDtypeStruct((total, width), BF16),
            jax.ShapeDtypeStruct((pairs, tiles, 2, tile), F32),
            jax.ShapeDtypeStruct((pairs, tiles, 2, held, tile), BF16),
        ],
        scratch_shapes=[pltpu.VMEM((PAIR, far), BF16), pltpu.VMEM((far, tile), F32)],
        input_output_aliases=aliases,
        compiler_params=pltpu.CompilerParams(vmem_limit_bytes=VMEM_LIMIT),
        cost_estimate=pl.CostEstimate(
            flops=4 * cells * HEAD_DIM, bytes_accessed=2 * cells, transcendentals=cells
        ),
        name="attention_forward",
    )(*operands)


def attention_backward_kernel(cont_tiles, *refs):
    k_ref, v_ref, kn_ref, vn_ref = refs[:4]
    cont_refs, prompt_refs = refs[4:9], refs[9:14]
    rows_ref, prompt_rows_ref = refs[14:16]
    dq_ref, dkvn_ref, dkv_ref, weight_ref, sums_ref, kt_ref, dkt_ref, dvt_ref = refs[-8:]
    at = pl.program_id(1)

    @pl.when(at == 0)
    def _():
        kt_ref[...] = k_ref[...].T
        dkt_ref[...] = jnp.zeros_like(dkt_ref)
        dvt_ref[...] = jnp.zeros_like(dvt_ref)

    def tile_of(near, tile_refs, first):
        q_ref, out_ref, dout_ref, inv_ref, exp_ref = tile_refs
        far = k_ref.shape[0]
        tile = q_ref.shape[0]
        qt = q_ref[...].T
        dout = dout_ref[...].astype(F32).T
        product = out_ref[...].astype(F32).T * dout
        if near:
            knt = kn_ref[...].T
        zero = jnp.zeros((HEAD_DIM, tile), BF16)
        dqs, dkn, dvn = [], [], []
        for h in range(2):
            rows = slice(h * HEAD_DIM, (h + 1) * HEAD_DIM)
            inverse = inv_ref[0, 0, h : h + 1, :]
            delta = jnp.sum(product[rows, :], axis=0, keepdims=True) * inverse
            do = (dout[rows, :] * inverse).astype(BF16)
            padded = jnp.concatenate([do, zero] if h == 0 else [zero, do], 0)
            e = exp_ref[0, 0, h, 0:far, :]
            ds = (e.astype(F32) * (dot(v_ref[...], padded, 1, 0) - delta)).astype(BF16)
            dvt_ref[rows, :] += dot(do, e, 1, 1)
            dkt_ref[rows, :] += dot(qt[rows, :], ds, 1, 1)
            dq = dot(kt_ref[rows, :], ds, 1, 0)
            if near:
                e = exp_ref[0, 0, h, far:, :]
                ds = (e.astype(F32) * (dot(vn_ref[...], padded, 1, 0) - delta)).astype(BF16)
                dvn.append(dot(do, e, 1, 1))
                dkn.append(dot(qt[rows, :], ds, 1, 1))
                dq = dq + dot(knt[rows, :], ds, 1, 0)
            dqs.append(dq * HEAD_DIM ** (-0.5))
        row = pl.ds(pl.multiple_of(first, tile), tile)
        dq_ref[row, :] = jnp.concatenate(dqs, 0).T.astype(dq_ref.dtype)
        if near:
            dkvn_ref[row, :PAIR] = jnp.concatenate(dkn, 0).T.astype(dkvn_ref.dtype)
            dkvn_ref[row, PAIR:] = jnp.concatenate(dvn, 0).T.astype(dkvn_ref.dtype)

    @pl.when(at < cont_tiles)
    def _():
        tile_of(True, cont_refs, at * cont_refs[0].shape[0])

    @pl.when(at >= cont_tiles)
    def _():
        tile_of(False, prompt_refs, dkvn_ref.shape[0] + (at - cont_tiles) * prompt_refs[0].shape[0])

    @pl.when(at == pl.num_programs(1) - 1)
    def _():
        dkv_ref[:, :PAIR] = dkt_ref[...].T.astype(dkv_ref.dtype)
        dkv_ref[:, PAIR:] = dvt_ref[...].T.astype(dkv_ref.dtype)
        count = dkvn_ref.shape[0]
        weight_ref[:, :PAIR] = dot(rows_ref[...], dq_ref[...], 1, 0).astype(weight_ref.dtype)
        weight_ref[:, PAIR:] = (
            dot(prompt_rows_ref[...], dkv_ref[...], 1, 0)
            + dot(rows_ref[:, :count], dkvn_ref[...], 1, 0)
        ).astype(weight_ref.dtype)

        def sums_of(ref):
            return dot(jnp.ones((8, ref.shape[0]), BF16), ref[...], 1, 0)

        sums_ref[0, :, :PAIR] = sums_of(dq_ref)
        sums_ref[0, :, PAIR:] = sums_of(dkv_ref) + sums_of(dkvn_ref)


def attention_backward(
    queries, keys_values, far, context, d_context, cont_held, prompt_held, rows_t, prompt_t, h0, nh,
    into,
):
    total, width = queries.shape
    cont_tiles, length = cont_held[1].shape[1], cont_held[1].shape[4]
    tiles, tile = prompt_held[1].shape[1], prompt_held[1].shape[4]
    count = cont_tiles * length
    first, behind = far // length, count // tile

    def cont_at(t):
        return jnp.minimum(t, cont_tiles - 1)

    def prompt_at(t):
        return jnp.maximum(t - cont_tiles, 0)

    def tile_specs(size, held, start, at):
        row = pl.BlockSpec((size, PAIR), lambda h, t: (start + at(t), h0 + h))
        return [
            row,
            row,
            row,
            pl.BlockSpec((1, 1, 2, size), lambda h, t: (h0 + h, at(t), 0, 0)),
            pl.BlockSpec((1, 1, 2, held, size), lambda h, t: (h0 + h, at(t), 0, 0, 0)),
        ]

    specs = [
        pl.BlockSpec((far, PAIR), lambda h, t: (0, 2 * (h0 + h))),
        pl.BlockSpec((far, PAIR), lambda h, t: (0, 2 * (h0 + h) + 1)),
        pl.BlockSpec((length, PAIR), lambda h, t: (first + cont_at(t), 2 * (h0 + h))),
        pl.BlockSpec((length, PAIR), lambda h, t: (first + cont_at(t), 2 * (h0 + h) + 1)),
    ]
    specs += tile_specs(length, far + length, 0, cont_at)
    specs += tile_specs(tile, far, behind, prompt_at)
    whole = pl.Buffered(1)
    specs += [
        pl.BlockSpec((width, total), lambda h, t: (0, 0), pipeline_mode=whole),
        pl.BlockSpec((width, far), lambda h, t: (0, 0), pipeline_mode=whole),
    ]
    specs += [pl.BlockSpec(memory_space=pl.ANY)] * len(into)
    wide = 2 * PAIR
    cells = (count * (far + length) + tiles * tile * far) * nh * 2
    return pl.pallas_call(
        functools.partial(attention_backward_kernel, cont_tiles),
        grid=(nh, cont_tiles + tiles),
        in_specs=specs,
        out_specs=[
            pl.BlockSpec((total, PAIR), lambda h, t: (0, h0 + h)),
            pl.BlockSpec((count, wide), lambda h, t: (0, h0 + h)),
            pl.BlockSpec((far, wide), lambda h, t: (0, h)),
            pl.BlockSpec((width, 3 * PAIR), lambda h, t: (0, h)),
            pl.BlockSpec((1, 8, 3 * PAIR), lambda h, t: (h, 0, 0)),
        ],
        out_shape=[
            jax.ShapeDtypeStruct((total, width), BF16),
            jax.ShapeDtypeStruct((count, 2 * width), BF16),
            jax.ShapeDtypeStruct((far, nh * wide), BF16),
            jax.ShapeDtypeStruct((width, nh * 3 * PAIR), BF16),
            jax.ShapeDtypeStruct((nh, 8, 3 * PAIR), F32),
        ],
        scratch_shapes=[
            pltpu.VMEM((PAIR, far), BF16),
            pltpu.VMEM((PAIR, far), F32),
            pltpu.VMEM((PAIR, far), F32),
        ],
        input_output_aliases={16 + n: n for n in range(len(into))},
        compiler_params=pltpu.CompilerParams(vmem_limit_bytes=VMEM_LIMIT),
        cost_estimate=pl.CostEstimate(flops=cells, bytes_accessed=cells // 16, transcendentals=0),
        name="attention_backward",
    )(
        keys_values, keys_values, keys_values, keys_values,
        queries, context, d_context, *cont_held,
        queries, context, d_context, *prompt_held,
        rows_t, prompt_t, *into,
    )


def turn_kernel(x_ref, out_ref):
    out_ref[...] = x_ref[...].T


def turned(rows):
    count, width = rows.shape
    tile = count // 2 if (count // 2) % PAIR == 0 else count
    return pl.pallas_call(
        turn_kernel,
        grid=(count // tile,),
        in_specs=[pl.BlockSpec((tile, width), lambda t: (t, 0))],
        out_specs=pl.BlockSpec((width, tile), lambda t: (0, t)),
        out_shape=jax.ShapeDtypeStruct((width, count), rows.dtype),
        compiler_params=pltpu.CompilerParams(vmem_limit_bytes=VMEM_LIMIT),
        cost_estimate=pl.CostEstimate(
            flops=0, bytes_accessed=4 * count * width, transcendentals=0
        ),
        name="turn",
    )(rows)


def gelu_pair(pre):
    half = 0.5 * (1.0 + lax.erf(pre * (0.5**0.5)))
    slope = half + pre * (jnp.exp(-0.5 * pre * pre) * 0.3989422804014327)
    return pre * half, slope


def exact(left, right, left_dim, right_dim):
    return lax.dot_general(
        left,
        right,
        (((left_dim,), (right_dim,)), ((), ())),
        precision=HIGHEST,
        preferred_element_type=F32,
    )


def total_of(array):
    return jnp.sum(array, axis=0, keepdims=True)


def dense_kernel(cont_tiles, length, classes, *refs):
    (
        label_ref, x_ref, context_ref, cot_ref, first_weight_ref, reduce_ref, vector_ref, ebias_ref,
        student_ref, head_ref, pool_ref, class_ref,
        layer_ref, logits_ref, first_ref, hidden_ref, dmixed_ref, dpre_ref, dinner_ref,
        dinner_low_ref, dcontext_ref, small_ref, expand_sum_ref,
        hat_ref, mixed_ref, slope_ref, cotangent_ref,
    ) = refs
    at = pl.program_id(0)
    count, width = x_ref.shape
    lanes = student_ref.shape[1]
    inner = hidden_ref.shape[1]
    chunk = width
    obias, fgain, fshift, rbias, sgain, sshift = (vector_ref[i : i + 1, :] for i in range(2, 8))
    vectors_at = width + 2 * lanes + 4

    @pl.when(at == 0)
    def _():
        small_ref[...] = jnp.zeros_like(small_ref)
        expand_sum_ref[...] = jnp.zeros_like(expand_sum_ref)

    def add_vector(which, row):
        start = vectors_at + which * (width // lanes)
        for i in range(width // lanes):
            small_ref[start + i : start + i + 1, :] += row[:, i * lanes : (i + 1) * lanes]

    def normal(rows):
        center = rows - jnp.mean(rows, -1, keepdims=True)
        scale = lax.rsqrt(jnp.mean(center * center, -1, keepdims=True) + EPSILON)
        return center * scale, scale

    def normal_back(grad, hat, scale, gain):
        scaled = grad * gain
        return scale * (
            scaled
            - jnp.mean(scaled, -1, keepdims=True)
            - hat * jnp.mean(scaled * hat, -1, keepdims=True)
        )

    branch = dot(context_ref[...], first_weight_ref[:, :width], 1, 0) + obias
    hat, first_scale = normal(x_ref[...].astype(F32) + branch)
    hat_ref[...] = hat
    first = hat * fgain + fshift
    first_ref[...] = first.astype(BF16)
    mixed_ref[...] = first + rbias

    @pl.loop(0, inner // chunk)
    def _(c):
        columns = pl.ds(pl.multiple_of(c * chunk, chunk), chunk)
        behind = pl.ds(pl.multiple_of(width + c * chunk, chunk), chunk)
        pre = dot(first_ref[...], first_weight_ref[:, behind], 1, 0) + ebias_ref[:, columns]
        hidden, slope = gelu_pair(pre)
        hidden = hidden.astype(BF16)
        hidden_ref[:, columns] = hidden
        slope_ref[:, columns] = slope.astype(BF16)
        mixed_ref[...] += dot(hidden, reduce_ref[columns, :], 1, 0)

    hat, scale = normal(mixed_ref[...])
    layer_ref[...] = (hat * sgain + sshift).astype(BF16)
    mixed_ref[...] = hat
    cotangent_ref[...] = cot_ref[...].astype(F32)

    if cont_tiles:

        @pl.when(at < cont_tiles)
        def _():
            student_bias, query, pool_bias, class_bias = (head_ref[i : i + 1, :] for i in range(4))
            lane = lax.broadcasted_iota(jnp.int32, (lanes, lanes), 0) // (lanes // POOL_HEADS)
            same = jnp.where(
                lane == lax.broadcasted_iota(jnp.int32, (lanes, lanes), 1) // (lanes // POOL_HEADS),
                1.0,
                0.0,
            )
            scale = (lanes // POOL_HEADS) ** (-0.5)
            kind = lax.broadcasted_iota(jnp.int32, (1, lanes), 1)

            def eight(row):
                pad = lax.broadcasted_iota(jnp.int32, (8, lanes), 0) == 0
                return jnp.where(pad, jnp.broadcast_to(row, (8, lanes)), 0.0)

            @pl.loop(0, count // length)
            def _(c):
                rows = pl.ds(pl.multiple_of(c * length, length), length)
                layer = layer_ref[rows, :]
                student = dot(layer, student_ref[...], 1, 0) + student_bias
                scores = exact(student * query, same, 1, 0) * scale
                weights = jnp.exp(scores - jnp.max(scores, axis=0, keepdims=True))
                weights = weights / total_of(weights)
                pooled = total_of(weights * student)
                hidden = jnp.tanh(exact(eight(pooled), pool_ref[...], 1, 0)[0:1] + pool_bias)
                logits = exact(eight(hidden), class_ref[...], 1, 0)[0:1] + class_bias
                which = at * (count // length) + c
                logits_ref[pl.ds(which, 1), :] = logits
                logits = jnp.where(kind < classes, logits, NEGATIVE)
                chance = jnp.exp(logits - jnp.max(logits, axis=1, keepdims=True))
                chance = chance / jnp.sum(chance, axis=1, keepdims=True)
                d_logits = chance - jnp.where(kind == label_ref[which], 1.0, 0.0)
                d_hidden = exact(eight(d_logits), class_ref[...], 1, 1)[0:1]
                d_sum = d_hidden * (1.0 - hidden * hidden)
                d_pooled = exact(eight(d_sum), pool_ref[...], 1, 1)[0:1]
                d_weights = exact(student * d_pooled, same, 1, 0)
                d_scores = weights * (d_weights - total_of(weights * d_weights)) * scale
                d_student = weights * d_pooled + d_scores * query
                d_low = d_student.astype(BF16)
                cotangent_ref[rows, :] += dot(d_low, student_ref[...], 1, 1)
                small_ref[:width, :] += dot(layer, d_low, 0, 0)
                small_ref[width : width + lanes, :] += exact(eight(pooled), eight(d_sum), 0, 0)
                small_ref[width + lanes : width + 2 * lanes, :] += exact(
                    eight(hidden), eight(d_logits), 0, 0
                )
                start = width + 2 * lanes
                small_ref[start : start + 1, :] += total_of(d_student)
                small_ref[start + 1 : start + 2, :] += total_of(d_scores * student)
                small_ref[start + 2 : start + 3, :] += d_sum
                small_ref[start + 3 : start + 4, :] += d_logits

    cotangent = cotangent_ref[...]
    hat = mixed_ref[...]
    add_vector(4, total_of(cotangent * hat))
    add_vector(5, total_of(cotangent))
    d_mixed = normal_back(cotangent, hat, scale, sgain)
    add_vector(3, total_of(d_mixed))
    dmixed_ref[...] = d_mixed.astype(BF16)
    cotangent_ref[...] = d_mixed

    @pl.loop(0, inner // chunk)
    def _(c):
        columns = pl.ds(pl.multiple_of(c * chunk, chunk), chunk)
        behind = pl.ds(pl.multiple_of(width + c * chunk, chunk), chunk)
        d_pre = dot(dmixed_ref[...], reduce_ref[columns, :], 1, 1) * slope_ref[
            :, columns
        ].astype(F32)
        expand_sum_ref[:, columns] += jnp.sum(d_pre.reshape(-1, 8, chunk), axis=0)
        d_pre = d_pre.astype(BF16)
        dpre_ref[:, columns] = d_pre
        cotangent_ref[...] += dot(d_pre, first_weight_ref[:, behind], 1, 1)

    d_first = cotangent_ref[...]
    hat = hat_ref[...]
    add_vector(1, total_of(d_first * hat))
    add_vector(2, total_of(d_first))
    d_inner = normal_back(d_first, hat, first_scale, fgain)
    add_vector(0, total_of(d_inner))
    dinner_ref[...] = d_inner
    low = d_inner.astype(BF16)
    dinner_low_ref[...] = low
    dcontext_ref[...] = dot(low, first_weight_ref[:, :width], 1, 1).astype(BF16)

    @pl.when(at == pl.num_programs(0) - 1)
    def _():
        start = vectors_at + 6 * (width // lanes)
        for i in range(inner // lanes):
            small_ref[start + i : start + i + 1, :] = total_of(
                expand_sum_ref[:, i * lanes : (i + 1) * lanes]
            )


def dense(labels, rows, context, cotangents, weights, start, count, tile, cont_tiles, length):
    first_weight, reduce_full, vectors, ebias, student, head, pool, classify, classes = weights
    width, inner = rows.shape[1], reduce_full.shape[0]
    lanes = student.shape[1]
    first = start // tile
    small_rows = width + 2 * lanes + 4 + (6 * width + inner) // lanes
    small_rows += -small_rows % 8

    def row(size, behind=0):
        return pl.BlockSpec((tile, size), lambda t: (behind + t, 0))

    def whole(array):
        return pl.BlockSpec(array.shape, lambda t: (0, 0), pipeline_mode=pl.Buffered(1))

    def kept(shape):
        return pl.BlockSpec(shape, lambda t: (0, 0))

    conts = labels.shape[0]
    low, high = BF16, F32
    outs = [
        (width, low), None, (width, low), (inner, low), (width, low), (inner, low), (width, high),
        (width, low), (width, low),
    ]
    fixed = [whole(w) for w in (first_weight, reduce_full, vectors, ebias, student, head, pool, classify)]
    weight_cells = first_weight.size + reduce_full.size
    return pl.pallas_call(
        functools.partial(dense_kernel, cont_tiles, length, classes),
        grid=(count // tile,),
        in_specs=[pl.BlockSpec(memory_space=pltpu.SMEM), row(width, first), row(width, first)]
        + [row(width, first)]
        + fixed,
        out_specs=[row(o[0]) if o else kept((conts, lanes)) for o in outs]
        + [kept((small_rows, lanes)), kept((8, inner))],
        out_shape=[
            jax.ShapeDtypeStruct((count, o[0]) if o else (conts, lanes), o[1] if o else F32)
            for o in outs
        ]
        + [
            jax.ShapeDtypeStruct((small_rows, lanes), F32),
            jax.ShapeDtypeStruct((8, inner), F32),
        ],
        scratch_shapes=[
            pltpu.VMEM((tile, width), F32),
            pltpu.VMEM((tile, width), F32),
            pltpu.VMEM((tile, inner), BF16),
            pltpu.VMEM((tile, width), F32),
        ],
        compiler_params=pltpu.CompilerParams(vmem_limit_bytes=VMEM_LIMIT),
        cost_estimate=pl.CostEstimate(
            flops=4 * count * weight_cells,
            bytes_accessed=2 * weight_cells + 20 * count * (width + inner) // 4,
            transcendentals=2 * count * inner,
        ),
        name="dense",
    )(
        labels, rows, context, cotangents, first_weight, reduce_full, vectors, ebias, student, head,
        pool, classify,
    )


def rows_back_kernel(d_inner_ref, dq_ref, dkv_ref, joint_ref, out_ref):
    width = dq_ref.shape[1]
    out_ref[...] = (
        d_inner_ref[...]
        + dot(dq_ref[...], joint_ref[:, :width], 1, 1)
        + dot(dkv_ref[...], joint_ref[:, width : 3 * width], 1, 1)
    )


def rows_back(d_inner, d_queries, d_kv, joint, start, count, tile):
    width = d_inner.shape[1]
    first = start // tile
    return pl.pallas_call(
        rows_back_kernel,
        grid=(count // tile,),
        in_specs=[
            pl.BlockSpec((tile, width), lambda t: (first + t, 0)),
            pl.BlockSpec((tile, width), lambda t: (first + t, 0)),
            pl.BlockSpec((tile, 2 * width), lambda t: (t, 0)),
            pl.BlockSpec(joint.shape, lambda t: (0, 0), pipeline_mode=pl.Buffered(1)),
        ],
        out_specs=pl.BlockSpec((tile, width), lambda t: (t, 0)),
        out_shape=jax.ShapeDtypeStruct((count, width), F32),
        compiler_params=pltpu.CompilerParams(vmem_limit_bytes=VMEM_LIMIT),
        cost_estimate=pl.CostEstimate(flops=count, bytes_accessed=count, transcendentals=0),
        name="rows_back",
    )(d_inner, d_queries, d_kv, joint)


def bits_of(axis):
    size = lax.axis_size(axis)
    return [(axis, 1 << b) for b in reversed(range(size.bit_length() - 1))]


def across(array, axis, bit):
    return lax.ppermute(array, axis, [(i, i ^ bit) for i in range(lax.axis_size(axis))])


def bit_set(axis, bit):
    return (lax.axis_index(axis) // bit) % 2


def gather_bits(shard, order, dims):
    held = shard.reshape((1,) * len(dims) + shard.shape)
    for axis, bit in order:
        dim = dims.index((axis, bit))
        other = across(held, axis, bit)
        held = jnp.where(
            bit_set(axis, bit) == 0,
            jnp.concatenate([held, other], dim),
            jnp.concatenate([other, held], dim),
        )
    return held


def gather_relative(shard, axis):
    bits = bits_of(axis)
    held = shard.reshape((1,) * len(bits) + shard.shape)
    for dim, (_, bit) in enumerate(bits):
        held = jnp.concatenate([held, across(held, axis, bit)], dim)
    return held.reshape((-1,) + shard.shape[1:])


class Halves:
    def __init__(self, blocks):
        self.shape = blocks.shape[1:]
        self.bits = bits_of("seq")
        self.held = blocks
        self.split()

    def split(self):
        both = self.held.reshape((-1, 2) + self.shape)
        self.keep, self.give = both[:, 0], both[:, 1]

    def send(self):
        self.other = across(self.give, *self.bits.pop())

    def take(self):
        self.held = (self.keep.astype(F32) + self.other.astype(F32)).astype(BF16)
        if not self.bits:
            self.held = self.held.reshape(self.shape)
            return False
        self.split()
        return True

    def waiting(self):
        return self.give if self.bits else self.held

    def tied(self, value):
        if self.bits:
            self.give = value
        else:
            self.held = value


class Spread:
    def __init__(self, blocks):
        self.held, self.sent = blocks, False

    def send(self):
        self.other, self.sent = lax.all_to_all(self.held, BOTH, 0, 0), True

    def take(self):
        self.held = jnp.sum(self.other.astype(F32), 0)
        return False

    def waiting(self):
        return self.held

    def tied(self, value):
        self.held = value


class Sum:
    def __init__(self, value, order):
        self.held, self.order = value.astype(BF16), list(order)

    def send(self):
        axis, bit = self.order.pop(0)
        self.other = across(self.held, axis, bit)

    def take(self):
        self.held = self.held.astype(F32) + self.other.astype(F32)
        if self.order:
            self.held = self.held.astype(BF16)
        return bool(self.order)

    def waiting(self):
        return self.held

    def tied(self, value):
        self.held = value


class Exchanges:
    def __init__(self):
        self.live = []

    def add(self, chain):
        self.live.append((chain, True))
        return chain

    def step(self, value, last=False):
        going, flat = [], []
        for chain, new in self.live:
            if new or chain.take():
                going.append(chain)
        if value is not None:
            chains = [chain for chain, new in self.live if new or not last]
            value, flat = lax.optimization_barrier((value, [c.waiting() for c in chains]))
            for chain, tied in zip(chains, flat):
                chain.tied(tied)
        if last:
            for chain, new in self.live:
                if new:
                    chain.send()
            chains = [chain for chain, new in self.live if not new]
            value, flat = lax.optimization_barrier((value, [c.waiting() for c in chains]))
            for chain, tied in zip(chains, flat):
                chain.tied(tied)
            for chain in going:
                if chain in chains:
                    chain.send()
            self.live = [(chain, False) for chain in going]
            return value
        self.live = [(chain, False) for chain in going]
        for chain in going:
            chain.send()
        return value

    def move(self, chain, value):
        more = chain.take()
        value, tied = lax.optimization_barrier((value, chain.waiting()))
        chain.tied(tied)
        if more:
            chain.send()
        else:
            self.live = [entry for entry in self.live if entry[0] is not chain]
        return value

    def finish(self):
        while self.live:
            self.step(None)


def local(
    prompt_in,
    cont_in,
    prompt_cot,
    cont_cot,
    labels,
    joint_weight,
    query_bias,
    value_bias,
    output_weight,
    output_bias,
    first_gain,
    first_shift,
    expand_weight,
    expand_bias,
    reduce_weight,
    reduce_bias,
    second_gain,
    second_shift,
    student_weight,
    student_bias,
    pool_query,
    pool_weight,
    pool_bias,
    class_weight,
    class_bias,
):
    prompt_rows = prompt_in[0]
    share, width = prompt_rows.shape
    _, conts, length, _ = cont_in.shape
    cont_count = conts * length
    part = joint_weight.shape[0]
    devices = width // part
    hidden_width = expand_weight.shape[1]
    fold = hidden_width // width
    tile = min(share, length)
    grp_bits, seq_bits = bits_of("grp"), bits_of("seq")
    dims = grp_bits + seq_bits
    gather_orders = (
        grp_bits + seq_bits,
        grp_bits[:-1] + seq_bits[:-1] + grp_bits[-1:] + seq_bits[-1:],
    )

    pairs = width // PAIR
    groups = [3, 2, 1] if pairs == 6 else [pairs]
    joint_low = joint_weight.astype(BF16)
    vectors = [
        query_bias,
        value_bias,
        output_bias,
        first_gain,
        first_shift,
        reduce_bias,
        second_gain,
        second_shift,
    ]
    beside = jnp.concatenate([v[None] for v in vectors], 0).astype(BF16).T
    beside = jnp.concatenate([beside, expand_bias.astype(BF16).reshape(part, fold)], 1)
    lanes = student_weight.shape[1]
    own_joint = [joint_low[:, :width]]
    for h in range(pairs):
        own_joint += [joint_low[:, (s * pairs + h) * PAIR :][:, :PAIR] for s in (1, 2)]
    own_joint.append(jnp.pad(beside, ((0, 0), (0, lanes - beside.shape[1]))))
    own_joint = jnp.concatenate(own_joint, 1)
    half = (3 * width // 2 + lanes) // PAIR * PAIR
    joint_all = jnp.concatenate(
        [
            gather_bits(piece, order, dims).reshape(width, -1)
            for piece, order in zip((own_joint[:, :half], own_joint[:, half:]), gather_orders)
        ],
        1,
    )
    joint_all = lax.optimization_barrier(joint_all)
    joint_full = joint_all[:, : 3 * width]
    flat = joint_all[:, 3 * width :].astype(F32)
    by_vector = flat[:, : len(vectors)].T
    qbias, vbias = by_vector[0], by_vector[1]
    ebias = flat[:, 8 : 8 + fold].reshape(hidden_width)
    prompt_all = gather_relative(prompt_rows, "seq")
    far = prompt_all.shape[0]
    out_expand = lax.all_gather(
        jnp.concatenate([output_weight, expand_weight], 1).astype(BF16), BOTH, axis=0, tiled=True
    )
    reduce_full = lax.all_gather(reduce_weight.astype(BF16), BOTH, axis=0, tiled=True)

    cont_rows = cont_in[0].reshape(cont_count, width)
    rows = jnp.concatenate([cont_rows, prompt_rows], 0)
    key_rows = jnp.concatenate([prompt_all, cont_rows], 0)
    rows_t, prompt_t = turned(rows), turned(prompt_all)
    queries = (dot(rows, joint_full[:, :width], 1, 0) + qbias).astype(BF16) * HEAD_DIM ** (-0.5)
    kv_bias = jnp.pad(vbias.reshape(pairs, 1, PAIR), ((0, 0), (1, 0), (0, 0))).reshape(-1)
    keys_values = (dot(key_rows, joint_full[:, width:], 1, 0) + kv_bias).astype(BF16)

    context, prompt_inv, prompt_exp = attention_forward(
        queries, keys_values, far, share, cont_count, tile, None
    )
    context, cont_inv, cont_exp = attention_forward(
        queries, keys_values, far, cont_count, 0, length, context
    )

    classes = class_weight.shape[1]
    head = jnp.concatenate(
        [student_bias, pool_query, pool_bias, jnp.pad(class_bias, (0, lanes - classes))]
    ).reshape(4, lanes)
    weights = (
        out_expand,
        reduce_full,
        by_vector,
        ebias[None],
        student_weight.astype(BF16),
        jnp.pad(head, ((0, 4), (0, 0))),
        pool_weight,
        jnp.pad(class_weight, ((0, 0), (0, lanes - classes))),
        classes,
    )
    cotangents = jnp.concatenate([cont_cot[0].reshape(cont_count, width), prompt_cot[0]], 0)
    cont_tile = min(2 * length, cont_count)
    if cont_tile == share:
        results = dense(
            labels[0], rows, context, cotangents, weights, 0, rows.shape[0], share,
            cont_count // cont_tile, length,
        )
    else:
        of_conts = dense(
            labels[0], rows, context, cotangents, weights, 0, cont_count, cont_tile,
            cont_count // cont_tile, length,
        )
        of_prompt = dense(
            labels[0], rows, context, cotangents, weights, cont_count, share, share, 0, length
        )
        results = [
            of_conts[i]
            if i == 1
            else of_conts[i] + of_prompt[i]
            if i > 8
            else jnp.concatenate([of_conts[i], of_prompt[i]], 0)
            for i in range(len(of_conts))
        ]
    layer_low, logits, first_low, hidden, d_mixed_low, d_pre_low, d_inner = results[:7]
    d_inner_low, d_context, small = results[7:10]
    logits = logits[:, :classes]
    cont_layer = layer_low[:cont_count]
    exchanges = Exchanges()
    small = exchanges.add(Sum(small, dims))
    d_reduce_weight = dot(hidden, d_mixed_low, 0, 0).astype(BF16)
    d_expand_weight = dot(first_low, d_pre_low, 0, 0).astype(BF16)
    d_output_weight = dot(context, d_inner_low, 0, 0).astype(BF16)

    blocks = [d_output_weight.reshape(devices, part, width)]
    blocks += [
        d_expand_weight[:, i * width : (i + 1) * width].reshape(devices, part, width)
        for i in range(fold)
    ]
    blocks += [d_reduce_weight.reshape(devices, -1, width)]
    blocks, d_context, d_inner, rows_t, prompt_t = lax.optimization_barrier(
        (jnp.concatenate(blocks, 1), d_context, d_inner, rows_t, prompt_t)
    )
    early = lax.psum_scatter(blocks, BOTH, scatter_dimension=0, tiled=True)

    into, owns, joint_parts, sums = (), [], [], []
    h0 = 0
    for nh in groups:
        d_context = exchanges.step(d_context)
        *into, dkv_far, d_joint, sum_rows = attention_backward(
            queries, keys_values, far, context, d_context, (cont_inv, cont_exp),
            (prompt_inv, prompt_exp), rows_t, prompt_t, h0, nh, into,
        )
        if h0 + nh == pairs:
            sums.append(sum_rows[:, 0])
            sums = jnp.concatenate(sums, 0)
            sums = [sums[:, i * PAIR : (i + 1) * PAIR].reshape(devices, 1, part) for i in (0, 2)]
            sums = jnp.concatenate(sums, 1).astype(BF16)
            sums = jnp.pad(sums, ((0, 0), (0, 6), (0, 3 * nh * PAIR - part)))
            d_joint = jnp.concatenate([d_joint.reshape(devices, part, -1), sums], 1)
        else:
            sums.append(sum_rows[:, 0])
        owns.append(exchanges.add(Halves(dkv_far.reshape(-1, share, dkv_far.shape[1]))))
        joint_parts.append(exchanges.add(Spread(d_joint.reshape(devices, -1, 3 * nh * PAIR))))
        h0 += nh
    d_queries, d_kv = into
    early, d_queries = exchanges.step((early, d_queries), True)
    d_queries = exchanges.move(owns[-1], d_queries)
    d_cont_rows = rows_back(d_inner, d_queries, d_kv, joint_all, 0, cont_count, cont_tile)
    exchanges.finish()
    early = early[0].astype(F32)
    output_grad = early[:part]
    expand_grad = jnp.concatenate(
        [early[part * (1 + i) : part * (2 + i)] for i in range(fold)], 1
    )
    reduce_grad = early[part * (1 + fold) :]
    parts = [p.held for p in joint_parts]
    joint_grad = jnp.concatenate(
        [p[:part].reshape(part, nh, 3, PAIR) for p, nh in zip(parts, groups)], 1
    )
    joint_grad = joint_grad.transpose(0, 2, 1, 3).reshape(part, 3 * width)

    d_own = jnp.concatenate([o.held.astype(BF16) for o in owns], 1)
    d_prompt_rows = rows_back(d_inner, d_queries, d_own, joint_all, cont_count, share, share)

    small = small.held
    index = lax.axis_index(BOTH)
    at = width + lanes
    head_grads = (
        small[:width],
        small[at + lanes],
        small[at + lanes + 1],
        small[width:at],
        small[at + lanes + 2],
        small[at : at + lanes, :classes],
        small[at + lanes + 3, :classes],
    )
    at += lanes + 4
    vector_grads = []
    for row in (part, part + 1):
        vector_grads.append(parts[-1][row, :part])
    for size in [width] * 6 + [hidden_width]:
        vector = small[at : at + size // lanes].reshape(size)
        own = size // devices
        vector_grads.append(lax.dynamic_slice(vector, (index * own,), (own,)))
        at += size // lanes
    (g_qbias, g_vbias, g_obias, g_fgain, g_fshift, g_rbias, g_sgain, g_sshift, g_ebias) = vector_grads
    return (
        layer_low[cont_count:][None],
        cont_layer.reshape(1, conts, length, width),
        logits[None],
        d_prompt_rows[None],
        d_cont_rows.reshape(1, conts, length, width),
        joint_grad,
        g_qbias,
        g_vbias,
        output_grad,
        g_obias,
        g_fgain,
        g_fshift,
        expand_grad,
        g_ebias,
        reduce_grad,
        g_rbias,
        g_sgain,
        g_sshift,
    ) + head_grads


def solution(mesh):
    placed = (
        P("grp", "seq", None),
        P("grp", "seq", None, None),
        P("grp", "seq", None),
        P("grp", "seq", None, None),
        P("grp", "seq"),
        P(("grp", "seq"), None),
        P(("grp", "seq")),
        P(("grp", "seq")),
        P(("grp", "seq"), None),
        P(("grp", "seq")),
        P(("grp", "seq")),
        P(("grp", "seq")),
        P(("grp", "seq"), None),
        P(("grp", "seq")),
        P(("grp", "seq"), None),
        P(("grp", "seq")),
        P(("grp", "seq")),
        P(("grp", "seq")),
        P(),
        P(),
        P(),
        P(),
        P(),
        P(),
        P(),
    )
    return jax.shard_map(
        local,
        mesh=mesh,
        in_specs=placed,
        out_specs=(
            P("grp", "seq", None),
            P("grp", "seq", None, None),
            P("grp", "seq", None),
            P("grp", "seq", None),
            P("grp", "seq", None, None),
            P(("grp", "seq"), None),
            P(("grp", "seq")),
            P(("grp", "seq")),
            P(("grp", "seq"), None),
            P(("grp", "seq")),
            P(("grp", "seq")),
            P(("grp", "seq")),
            P(("grp", "seq"), None),
            P(("grp", "seq")),
            P(("grp", "seq"), None),
            P(("grp", "seq")),
            P(("grp", "seq")),
            P(("grp", "seq")),
            P(),
            P(),
            P(),
            P(),
            P(),
            P(),
            P(),
        ),
        check_vma=False,
    )
```

```python
import functools

import jax
import jax.numpy as jnp
from jax import lax
from jax.experimental import pallas as pl
from jax.experimental.pallas import tpu as pltpu
from jax.sharding import PartitionSpec as P

HEAD_DIM = 64
POOL_HEADS = 2
PAIR = 2 * HEAD_DIM

EPSILON = 1e-06
HIGHEST = lax.Precision.HIGHEST
NEGATIVE = -1e30
BOTH = ("grp", "seq")
BF16 = jnp.bfloat16
F32 = jnp.float32
LOG2_E = 1.4426950408889634
SUM_LOW, SUM_HIGH = 1e-12, 1e18
VMEM_LIMIT = 56 << 20


def dot(left, right, left_dim, right_dim):
    return lax.dot_general(
        left, right, (((left_dim,), (right_dim,)), ((), ())), preferred_element_type=F32
    )


def precise(left, right):
    return jnp.dot(left, right, precision=HIGHEST, preferred_element_type=F32)


def attention_forward_kernel(near, *refs):
    if near:
        q_ref, k_ref, v_ref, kn_ref, vn_ref, _, out_ref, inv_ref, exp_ref, vt_ref, s_ref = refs
    else:
        q_ref, k_ref, v_ref, out_ref, inv_ref, exp_ref, vt_ref, s_ref = refs
    far = k_ref.shape[0]
    tile = q_ref.shape[0]

    @pl.when(pl.program_id(1) == 0)
    def _():
        vt_ref[...] = v_ref[...].T

    q = q_ref[...]
    lane = lax.broadcasted_iota(jnp.int32, q.shape, 1)
    masked = [
        jnp.where((lane < HEAD_DIM) if h == 0 else (lane >= HEAD_DIM), q, jnp.zeros_like(q))
        for h in range(2)
    ]
    heads = [slice(h * HEAD_DIM, (h + 1) * HEAD_DIM) for h in range(2)]
    if near:
        vnt = vn_ref[...].T
        allowed = lax.broadcasted_iota(jnp.int32, (tile, tile), 0) <= lax.broadcasted_iota(
            jnp.int32, (tile, tile), 1
        )

    def near_scores(h):
        return jnp.where(allowed, dot(kn_ref[...], masked[h], 1, 1), NEGATIVE)

    def finish(outs):
        out_ref[...] = jnp.concatenate(outs, 0).T.astype(out_ref.dtype)

    outs = []
    fine = None
    for h in range(2):
        e = jnp.exp2(dot(k_ref[...], masked[h], 1, 1) * LOG2_E)
        total = jnp.sum(e, axis=0, keepdims=True)
        low = e.astype(BF16)
        exp_ref[0, 0, h, 0:far, :] = low
        out = dot(vt_ref[heads[h], :], low, 1, 0)
        if near:
            e = jnp.exp2(near_scores(h) * LOG2_E)
            total = total + jnp.sum(e, axis=0, keepdims=True)
            low = e.astype(BF16)
            exp_ref[0, 0, h, far:, :] = low
            out = out + dot(vnt[heads[h], :], low, 1, 0)
        inverse = 1.0 / total
        inv_ref[0, 0, h : h + 1, :] = inverse
        outs.append(out * inverse)
        good = jnp.where((total > SUM_LOW) & (total < SUM_HIGH), 1.0, 0.0)
        fine = good if fine is None else jnp.minimum(fine, good)
    finish(outs)

    @pl.when(jnp.min(fine) < 0.5)
    def _():
        chunk = tile
        steps = far // chunk
        outs = []
        for h in range(2):

            def score(c, top):
                at = pl.multiple_of(c * chunk, chunk)
                s = dot(k_ref[pl.ds(at, chunk), :], masked[h], 1, 1)
                s_ref[pl.ds(at, chunk), :] = s
                return jnp.maximum(top, jnp.max(s, axis=0, keepdims=True))

            top = jnp.full((1, tile), NEGATIVE, F32)
            if near:
                sn = near_scores(h)
                top = jnp.max(sn, axis=0, keepdims=True)
            top = lax.fori_loop(0, steps, score, top)

            def weigh(c, carry):
                total, out = carry
                at = pl.multiple_of(c * chunk, chunk)
                e = jnp.exp2((s_ref[pl.ds(at, chunk), :] - top) * LOG2_E)
                low = e.astype(BF16)
                exp_ref[0, 0, h, pl.ds(at, chunk), :] = low
                part = dot(v_ref[pl.ds(at, chunk), :], low, 0, 0)[heads[h], :]
                return total + jnp.sum(e, axis=0, keepdims=True), out + part

            total = jnp.zeros((1, tile), F32)
            out = jnp.zeros((HEAD_DIM, tile), F32)
            if near:
                e = jnp.exp2((sn - top) * LOG2_E)
                low = e.astype(BF16)
                exp_ref[0, 0, h, far:, :] = low
                total = jnp.sum(e, axis=0, keepdims=True)
                out = dot(vnt[heads[h], :], low, 1, 0)
            total, out = lax.fori_loop(0, steps, weigh, (total, out))
            inverse = 1.0 / total
            inv_ref[0, 0, h : h + 1, :] = inverse
            outs.append(out * inverse)
        finish(outs)


def attention_forward(queries, keys_values, far, count, at, tile, into):
    near = into is not None
    total, width = queries.shape
    pairs = width // PAIR
    tiles = count // tile
    held = far + (tile if near else 0)
    block = at // tile
    specs = [
        pl.BlockSpec((tile, PAIR), lambda h, t: (block + t, h)),
        pl.BlockSpec((far, PAIR), lambda h, t: (0, 2 * h)),
        pl.BlockSpec((far, PAIR), lambda h, t: (0, 2 * h + 1)),
    ]
    operands = [queries, keys_values, keys_values]
    aliases = {}
    if near:
        first = far // tile
        specs += [
            pl.BlockSpec((tile, PAIR), lambda h, t: (first + t, 2 * h)),
            pl.BlockSpec((tile, PAIR), lambda h, t: (first + t, 2 * h + 1)),
            pl.BlockSpec(memory_space=pl.ANY),
        ]
        operands += [keys_values, keys_values, into]
        aliases = {5: 0}
    cells = count * held * width // HEAD_DIM
    return pl.pallas_call(
        functools.partial(attention_forward_kernel, near),
        grid=(pairs, tiles),
        in_specs=specs,
        out_specs=[
            pl.BlockSpec((tile, PAIR), lambda h, t: (block + t, h)),
            pl.BlockSpec((1, 1, 2, tile), lambda h, t: (h, t, 0, 0)),
            pl.BlockSpec((1, 1, 2, held, tile), lambda h, t: (h, t, 0, 0, 0)),
        ],
        out_shape=[
            jax.ShapeDtypeStruct((total, width), BF16),
            jax.ShapeDtypeStruct((pairs, tiles, 2, tile), F32),
            jax.ShapeDtypeStruct((pairs, tiles, 2, held, tile), BF16),
        ],
        scratch_shapes=[pltpu.VMEM((PAIR, far), BF16), pltpu.VMEM((far, tile), F32)],
        input_output_aliases=aliases,
        compiler_params=pltpu.CompilerParams(vmem_limit_bytes=VMEM_LIMIT),
        cost_estimate=pl.CostEstimate(
            flops=4 * cells * HEAD_DIM, bytes_accessed=2 * cells, transcendentals=cells
        ),
        name="attention_forward",
    )(*operands)


def attention_backward_kernel(cont_tiles, *refs):
    k_ref, v_ref, kn_ref, vn_ref = refs[:4]
    cont_refs, prompt_refs = refs[4:9], refs[9:14]
    rows_ref, prompt_rows_ref = refs[14:16]
    dq_ref, dkvn_ref, dkv_ref, weight_ref, sums_ref, kt_ref, dkt_ref, dvt_ref = refs[-8:]
    at = pl.program_id(1)

    @pl.when(at == 0)
    def _():
        kt_ref[...] = k_ref[...].T
        dkt_ref[...] = jnp.zeros_like(dkt_ref)
        dvt_ref[...] = jnp.zeros_like(dvt_ref)

    def tile_of(near, tile_refs, first):
        q_ref, out_ref, dout_ref, inv_ref, exp_ref = tile_refs
        far = k_ref.shape[0]
        tile = q_ref.shape[0]
        qt = q_ref[...].T
        dout = dout_ref[...].astype(F32).T
        product = out_ref[...].astype(F32).T * dout
        if near:
            knt = kn_ref[...].T
        zero = jnp.zeros((HEAD_DIM, tile), BF16)
        dqs, dkn, dvn = [], [], []
        for h in range(2):
            rows = slice(h * HEAD_DIM, (h + 1) * HEAD_DIM)
            inverse = inv_ref[0, 0, h : h + 1, :]
            delta = jnp.sum(product[rows, :], axis=0, keepdims=True) * inverse
            do = (dout[rows, :] * inverse).astype(BF16)
            padded = jnp.concatenate([do, zero] if h == 0 else [zero, do], 0)
            e = exp_ref[0, 0, h, 0:far, :]
            ds = (e.astype(F32) * (dot(v_ref[...], padded, 1, 0) - delta)).astype(BF16)
            dvt_ref[rows, :] += dot(do, e, 1, 1)
            dkt_ref[rows, :] += dot(qt[rows, :], ds, 1, 1)
            dq = dot(kt_ref[rows, :], ds, 1, 0)
            if near:
                e = exp_ref[0, 0, h, far:, :]
                ds = (e.astype(F32) * (dot(vn_ref[...], padded, 1, 0) - delta)).astype(BF16)
                dvn.append(dot(do, e, 1, 1))
                dkn.append(dot(qt[rows, :], ds, 1, 1))
                dq = dq + dot(knt[rows, :], ds, 1, 0)
            dqs.append(dq * HEAD_DIM ** (-0.5))
        row = pl.ds(pl.multiple_of(first, tile), tile)
        dq_ref[row, :] = jnp.concatenate(dqs, 0).T.astype(dq_ref.dtype)
        if near:
            dkvn_ref[row, :PAIR] = jnp.concatenate(dkn, 0).T.astype(dkvn_ref.dtype)
            dkvn_ref[row, PAIR:] = jnp.concatenate(dvn, 0).T.astype(dkvn_ref.dtype)

    @pl.when(at < cont_tiles)
    def _():
        tile_of(True, cont_refs, at * cont_refs[0].shape[0])

    @pl.when(at >= cont_tiles)
    def _():
        tile_of(False, prompt_refs, dkvn_ref.shape[0] + (at - cont_tiles) * prompt_refs[0].shape[0])

    @pl.when(at == pl.num_programs(1) - 1)
    def _():
        dkv_ref[:, :PAIR] = dkt_ref[...].T.astype(dkv_ref.dtype)
        dkv_ref[:, PAIR:] = dvt_ref[...].T.astype(dkv_ref.dtype)
        count = dkvn_ref.shape[0]
        weight_ref[:, :PAIR] = dot(rows_ref[...], dq_ref[...], 1, 0).astype(weight_ref.dtype)
        weight_ref[:, PAIR:] = (
            dot(prompt_rows_ref[...], dkv_ref[...], 1, 0)
            + dot(rows_ref[:, :count], dkvn_ref[...], 1, 0)
        ).astype(weight_ref.dtype)

        def sums_of(ref):
            return dot(jnp.ones((8, ref.shape[0]), BF16), ref[...], 1, 0)

        sums_ref[0, :, :PAIR] = sums_of(dq_ref)
        sums_ref[0, :, PAIR:] = sums_of(dkv_ref) + sums_of(dkvn_ref)


def attention_backward(
    queries, keys_values, far, context, d_context, cont_held, prompt_held, rows_t, prompt_t, h0, nh,
    into,
):
    total, width = queries.shape
    cont_tiles, length = cont_held[1].shape[1], cont_held[1].shape[4]
    tiles, tile = prompt_held[1].shape[1], prompt_held[1].shape[4]
    count = cont_tiles * length
    first, behind = far // length, count // tile

    def cont_at(t):
        return jnp.minimum(t, cont_tiles - 1)

    def prompt_at(t):
        return jnp.maximum(t - cont_tiles, 0)

    def tile_specs(size, held, start, at):
        row = pl.BlockSpec((size, PAIR), lambda h, t: (start + at(t), h0 + h))
        return [
            row,
            row,
            row,
            pl.BlockSpec((1, 1, 2, size), lambda h, t: (h0 + h, at(t), 0, 0)),
            pl.BlockSpec((1, 1, 2, held, size), lambda h, t: (h0 + h, at(t), 0, 0, 0)),
        ]

    specs = [
        pl.BlockSpec((far, PAIR), lambda h, t: (0, 2 * (h0 + h))),
        pl.BlockSpec((far, PAIR), lambda h, t: (0, 2 * (h0 + h) + 1)),
        pl.BlockSpec((length, PAIR), lambda h, t: (first + cont_at(t), 2 * (h0 + h))),
        pl.BlockSpec((length, PAIR), lambda h, t: (first + cont_at(t), 2 * (h0 + h) + 1)),
    ]
    specs += tile_specs(length, far + length, 0, cont_at)
    specs += tile_specs(tile, far, behind, prompt_at)
    whole = pl.Buffered(1)
    specs += [
        pl.BlockSpec((width, total), lambda h, t: (0, 0), pipeline_mode=whole),
        pl.BlockSpec((width, far), lambda h, t: (0, 0), pipeline_mode=whole),
    ]
    specs += [pl.BlockSpec(memory_space=pl.ANY)] * len(into)
    wide = 2 * PAIR
    cells = (count * (far + length) + tiles * tile * far) * nh * 2
    return pl.pallas_call(
        functools.partial(attention_backward_kernel, cont_tiles),
        grid=(nh, cont_tiles + tiles),
        in_specs=specs,
        out_specs=[
            pl.BlockSpec((total, PAIR), lambda h, t: (0, h0 + h)),
            pl.BlockSpec((count, wide), lambda h, t: (0, h0 + h)),
            pl.BlockSpec((far, wide), lambda h, t: (0, h)),
            pl.BlockSpec((width, 3 * PAIR), lambda h, t: (0, h)),
            pl.BlockSpec((1, 8, 3 * PAIR), lambda h, t: (h, 0, 0)),
        ],
        out_shape=[
            jax.ShapeDtypeStruct((total, width), BF16),
            jax.ShapeDtypeStruct((count, 2 * width), BF16),
            jax.ShapeDtypeStruct((far, nh * wide), BF16),
            jax.ShapeDtypeStruct((width, nh * 3 * PAIR), BF16),
            jax.ShapeDtypeStruct((nh, 8, 3 * PAIR), F32),
        ],
        scratch_shapes=[
            pltpu.VMEM((PAIR, far), BF16),
            pltpu.VMEM((PAIR, far), F32),
            pltpu.VMEM((PAIR, far), F32),
        ],
        input_output_aliases={16 + n: n for n in range(len(into))},
        compiler_params=pltpu.CompilerParams(vmem_limit_bytes=VMEM_LIMIT),
        cost_estimate=pl.CostEstimate(flops=cells, bytes_accessed=cells // 16, transcendentals=0),
        name="attention_backward",
    )(
        keys_values, keys_values, keys_values, keys_values,
        queries, context, d_context, *cont_held,
        queries, context, d_context, *prompt_held,
        rows_t, prompt_t, *into,
    )


def turn_kernel(x_ref, out_ref):
    out_ref[...] = x_ref[...].T


def turned(rows):
    count, width = rows.shape
    tile = count // 2 if (count // 2) % PAIR == 0 else count
    return pl.pallas_call(
        turn_kernel,
        grid=(count // tile,),
        in_specs=[pl.BlockSpec((tile, width), lambda t: (t, 0))],
        out_specs=pl.BlockSpec((width, tile), lambda t: (0, t)),
        out_shape=jax.ShapeDtypeStruct((width, count), rows.dtype),
        compiler_params=pltpu.CompilerParams(vmem_limit_bytes=VMEM_LIMIT),
        cost_estimate=pl.CostEstimate(
            flops=0, bytes_accessed=4 * count * width, transcendentals=0
        ),
        name="turn",
    )(rows)


def gelu_pair(pre):
    half = 0.5 * (1.0 + lax.erf(pre * (0.5**0.5)))
    slope = half + pre * (jnp.exp(-0.5 * pre * pre) * 0.3989422804014327)
    return pre * half, slope


def exact(left, right, left_dim, right_dim):
    return lax.dot_general(
        left,
        right,
        (((left_dim,), (right_dim,)), ((), ())),
        precision=HIGHEST,
        preferred_element_type=F32,
    )


def total_of(array):
    return jnp.sum(array, axis=0, keepdims=True)


def dense_kernel(cont_tiles, length, classes, *refs):
    (
        label_ref, x_ref, context_ref, cot_ref, first_weight_ref, reduce_ref, vector_ref, ebias_ref,
        student_ref, head_ref, pool_ref, class_ref,
        layer_ref, logits_ref, first_ref, hidden_ref, dmixed_ref, dpre_ref, dinner_ref,
        dinner_low_ref, dcontext_ref, small_ref, expand_sum_ref,
        hat_ref, mixed_ref, slope_ref, cotangent_ref,
    ) = refs
    at = pl.program_id(0)
    count, width = x_ref.shape
    lanes = student_ref.shape[1]
    inner = hidden_ref.shape[1]
    chunk = width
    obias, fgain, fshift, rbias, sgain, sshift = (vector_ref[i : i + 1, :] for i in range(2, 8))
    vectors_at = width + 2 * lanes + 4

    @pl.when(at == 0)
    def _():
        small_ref[...] = jnp.zeros_like(small_ref)
        expand_sum_ref[...] = jnp.zeros_like(expand_sum_ref)

    def add_vector(which, row):
        start = vectors_at + which * (width // lanes)
        for i in range(width // lanes):
            small_ref[start + i : start + i + 1, :] += row[:, i * lanes : (i + 1) * lanes]

    def normal(rows):
        center = rows - jnp.mean(rows, -1, keepdims=True)
        scale = lax.rsqrt(jnp.mean(center * center, -1, keepdims=True) + EPSILON)
        return center * scale, scale

    def normal_back(grad, hat, scale, gain):
        scaled = grad * gain
        return scale * (
            scaled
            - jnp.mean(scaled, -1, keepdims=True)
            - hat * jnp.mean(scaled * hat, -1, keepdims=True)
        )

    branch = dot(context_ref[...], first_weight_ref[:, :width], 1, 0) + obias
    hat, first_scale = normal(x_ref[...].astype(F32) + branch)
    hat_ref[...] = hat
    first = hat * fgain + fshift
    first_ref[...] = first.astype(BF16)
    mixed_ref[...] = first + rbias

    @pl.loop(0, inner // chunk)
    def _(c):
        columns = pl.ds(pl.multiple_of(c * chunk, chunk), chunk)
        behind = pl.ds(pl.multiple_of(width + c * chunk, chunk), chunk)
        pre = dot(first_ref[...], first_weight_ref[:, behind], 1, 0) + ebias_ref[:, columns]
        hidden, slope = gelu_pair(pre)
        hidden = hidden.astype(BF16)
        hidden_ref[:, columns] = hidden
        slope_ref[:, columns] = slope.astype(BF16)
        mixed_ref[...] += dot(hidden, reduce_ref[columns, :], 1, 0)

    hat, scale = normal(mixed_ref[...])
    layer_ref[...] = (hat * sgain + sshift).astype(BF16)
    mixed_ref[...] = hat
    cotangent_ref[...] = cot_ref[...].astype(F32)

    if cont_tiles:

        @pl.when(at < cont_tiles)
        def _():
            student_bias, query, pool_bias, class_bias = (head_ref[i : i + 1, :] for i in range(4))
            lane = lax.broadcasted_iota(jnp.int32, (lanes, lanes), 0) // (lanes // POOL_HEADS)
            same = jnp.where(
                lane == lax.broadcasted_iota(jnp.int32, (lanes, lanes), 1) // (lanes // POOL_HEADS),
                1.0,
                0.0,
            )
            scale = (lanes // POOL_HEADS) ** (-0.5)
            kind = lax.broadcasted_iota(jnp.int32, (1, lanes), 1)

            def eight(row):
                pad = lax.broadcasted_iota(jnp.int32, (8, lanes), 0) == 0
                return jnp.where(pad, jnp.broadcast_to(row, (8, lanes)), 0.0)

            @pl.loop(0, count // length)
            def _(c):
                rows = pl.ds(pl.multiple_of(c * length, length), length)
                layer = layer_ref[rows, :]
                student = dot(layer, student_ref[...], 1, 0) + student_bias
                scores = exact(student * query, same, 1, 0) * scale
                weights = jnp.exp(scores - jnp.max(scores, axis=0, keepdims=True))
                weights = weights / total_of(weights)
                pooled = total_of(weights * student)
                hidden = jnp.tanh(exact(eight(pooled), pool_ref[...], 1, 0)[0:1] + pool_bias)
                logits = exact(eight(hidden), class_ref[...], 1, 0)[0:1] + class_bias
                which = at * (count // length) + c
                logits_ref[pl.ds(which, 1), :] = logits
                logits = jnp.where(kind < classes, logits, NEGATIVE)
                chance = jnp.exp(logits - jnp.max(logits, axis=1, keepdims=True))
                chance = chance / jnp.sum(chance, axis=1, keepdims=True)
                d_logits = chance - jnp.where(kind == label_ref[which], 1.0, 0.0)
                d_hidden = exact(eight(d_logits), class_ref[...], 1, 1)[0:1]
                d_sum = d_hidden * (1.0 - hidden * hidden)
                d_pooled = exact(eight(d_sum), pool_ref[...], 1, 1)[0:1]
                d_weights = exact(student * d_pooled, same, 1, 0)
                d_scores = weights * (d_weights - total_of(weights * d_weights)) * scale
                d_student = weights * d_pooled + d_scores * query
                d_low = d_student.astype(BF16)
                cotangent_ref[rows, :] += dot(d_low, student_ref[...], 1, 1)
                small_ref[:width, :] += dot(layer, d_low, 0, 0)
                small_ref[width : width + lanes, :] += exact(eight(pooled), eight(d_sum), 0, 0)
                small_ref[width + lanes : width + 2 * lanes, :] += exact(
                    eight(hidden), eight(d_logits), 0, 0
                )
                start = width + 2 * lanes
                small_ref[start : start + 1, :] += total_of(d_student)
                small_ref[start + 1 : start + 2, :] += total_of(d_scores * student)
                small_ref[start + 2 : start + 3, :] += d_sum
                small_ref[start + 3 : start + 4, :] += d_logits

    cotangent = cotangent_ref[...]
    hat = mixed_ref[...]
    add_vector(4, total_of(cotangent * hat))
    add_vector(5, total_of(cotangent))
    d_mixed = normal_back(cotangent, hat, scale, sgain)
    add_vector(3, total_of(d_mixed))
    dmixed_ref[...] = d_mixed.astype(BF16)
    cotangent_ref[...] = d_mixed

    @pl.loop(0, inner // chunk)
    def _(c):
        columns = pl.ds(pl.multiple_of(c * chunk, chunk), chunk)
        behind = pl.ds(pl.multiple_of(width + c * chunk, chunk), chunk)
        d_pre = dot(dmixed_ref[...], reduce_ref[columns, :], 1, 1) * slope_ref[
            :, columns
        ].astype(F32)
        expand_sum_ref[:, columns] += jnp.sum(d_pre.reshape(-1, 8, chunk), axis=0)
        d_pre = d_pre.astype(BF16)
        dpre_ref[:, columns] = d_pre
        cotangent_ref[...] += dot(d_pre, first_weight_ref[:, behind], 1, 1)

    d_first = cotangent_ref[...]
    hat = hat_ref[...]
    add_vector(1, total_of(d_first * hat))
    add_vector(2, total_of(d_first))
    d_inner = normal_back(d_first, hat, first_scale, fgain)
    add_vector(0, total_of(d_inner))
    dinner_ref[...] = d_inner
    low = d_inner.astype(BF16)
    dinner_low_ref[...] = low
    dcontext_ref[...] = dot(low, first_weight_ref[:, :width], 1, 1).astype(BF16)

    @pl.when(at == pl.num_programs(0) - 1)
    def _():
        start = vectors_at + 6 * (width // lanes)
        for i in range(inner // lanes):
            small_ref[start + i : start + i + 1, :] = total_of(
                expand_sum_ref[:, i * lanes : (i + 1) * lanes]
            )


def dense(labels, rows, context, cotangents, weights, start, count, tile, cont_tiles, length):
    first_weight, reduce_full, vectors, ebias, student, head, pool, classify, classes = weights
    width, inner = rows.shape[1], reduce_full.shape[0]
    lanes = student.shape[1]
    first = start // tile
    small_rows = width + 2 * lanes + 4 + (6 * width + inner) // lanes
    small_rows += -small_rows % 8

    def row(size, behind=0):
        return pl.BlockSpec((tile, size), lambda t: (behind + t, 0))

    def whole(array):
        return pl.BlockSpec(array.shape, lambda t: (0, 0), pipeline_mode=pl.Buffered(1))

    def kept(shape):
        return pl.BlockSpec(shape, lambda t: (0, 0))

    conts = labels.shape[0]
    low, high = BF16, F32
    outs = [
        (width, low), None, (width, low), (inner, low), (width, low), (inner, low), (width, high),
        (width, low), (width, low),
    ]
    fixed = [whole(w) for w in (first_weight, reduce_full, vectors, ebias, student, head, pool, classify)]
    weight_cells = first_weight.size + reduce_full.size
    return pl.pallas_call(
        functools.partial(dense_kernel, cont_tiles, length, classes),
        grid=(count // tile,),
        in_specs=[pl.BlockSpec(memory_space=pltpu.SMEM), row(width, first), row(width, first)]
        + [row(width, first)]
        + fixed,
        out_specs=[row(o[0]) if o else kept((conts, lanes)) for o in outs]
        + [kept((small_rows, lanes)), kept((8, inner))],
        out_shape=[
            jax.ShapeDtypeStruct((count, o[0]) if o else (conts, lanes), o[1] if o else F32)
            for o in outs
        ]
        + [
            jax.ShapeDtypeStruct((small_rows, lanes), F32),
            jax.ShapeDtypeStruct((8, inner), F32),
        ],
        scratch_shapes=[
            pltpu.VMEM((tile, width), F32),
            pltpu.VMEM((tile, width), F32),
            pltpu.VMEM((tile, inner), BF16),
            pltpu.VMEM((tile, width), F32),
        ],
        compiler_params=pltpu.CompilerParams(vmem_limit_bytes=VMEM_LIMIT),
        cost_estimate=pl.CostEstimate(
            flops=4 * count * weight_cells,
            bytes_accessed=2 * weight_cells + 20 * count * (width + inner) // 4,
            transcendentals=2 * count * inner,
        ),
        name="dense",
    )(
        labels, rows, context, cotangents, first_weight, reduce_full, vectors, ebias, student, head,
        pool, classify,
    )


def rows_back_kernel(d_inner_ref, dq_ref, dkv_ref, joint_ref, out_ref):
    width = dq_ref.shape[1]
    out_ref[...] = (
        d_inner_ref[...]
        + dot(dq_ref[...], joint_ref[:, :width], 1, 1)
        + dot(dkv_ref[...], joint_ref[:, width : 3 * width], 1, 1)
    )


def rows_back(d_inner, d_queries, d_kv, joint, start, count, tile):
    width = d_inner.shape[1]
    first = start // tile
    return pl.pallas_call(
        rows_back_kernel,
        grid=(count // tile,),
        in_specs=[
            pl.BlockSpec((tile, width), lambda t: (first + t, 0)),
            pl.BlockSpec((tile, width), lambda t: (first + t, 0)),
            pl.BlockSpec((tile, 2 * width), lambda t: (t, 0)),
            pl.BlockSpec(joint.shape, lambda t: (0, 0), pipeline_mode=pl.Buffered(1)),
        ],
        out_specs=pl.BlockSpec((tile, width), lambda t: (t, 0)),
        out_shape=jax.ShapeDtypeStruct((count, width), F32),
        compiler_params=pltpu.CompilerParams(vmem_limit_bytes=VMEM_LIMIT),
        cost_estimate=pl.CostEstimate(flops=count, bytes_accessed=count, transcendentals=0),
        name="rows_back",
    )(d_inner, d_queries, d_kv, joint)


def reduce_grad_kernel(hidden_ref, d_ref, out_ref):
    out_ref[...] = dot(hidden_ref[...], d_ref[...], 0, 0).reshape(out_ref.shape).astype(BF16)


def other_grads_kernel(context_ref, d_inner_ref, first_ref, d_pre_ref, _, out_ref):
    @pl.when(pl.program_id(0) == 0)
    def _():
        grad = dot(context_ref[...], d_inner_ref[...], 0, 0)
        out_ref[...] = grad.reshape(out_ref.shape).astype(BF16)

    @pl.when(pl.program_id(0) > 0)
    def _():
        grad = dot(first_ref[...], d_pre_ref[...], 0, 0)
        out_ref[...] = grad.reshape(out_ref.shape).astype(BF16)


def matrix_grads(hidden, d_mixed, context, d_inner, first, d_pre, devices):
    total, width = d_mixed.shape
    fold = hidden.shape[1] // width
    part = width // devices
    shape = jax.ShapeDtypeStruct((devices, part * (2 * fold + 1), width), BF16)

    def kept():
        return pl.BlockSpec((total, width), lambda j: (0, 0), pipeline_mode=pl.Buffered(1))

    params = pltpu.CompilerParams(vmem_limit_bytes=VMEM_LIMIT)
    grads = pl.pallas_call(
        reduce_grad_kernel,
        grid=(fold,),
        in_specs=[pl.BlockSpec((total, width), lambda j: (0, j)), kept()],
        out_specs=pl.BlockSpec((devices // fold, part * fold, width), lambda j: (j, 0, 0)),
        out_shape=shape,
        compiler_params=params,
        cost_estimate=pl.CostEstimate(
            flops=2 * total * width * width * fold, bytes_accessed=0, transcendentals=0
        ),
        name="reduce_grad",
    )(hidden, d_mixed)
    return pl.pallas_call(
        other_grads_kernel,
        grid=(1 + fold,),
        in_specs=[
            kept(),
            kept(),
            kept(),
            pl.BlockSpec((total, width), lambda j: (0, jnp.maximum(j - 1, 0))),
            pl.BlockSpec(memory_space=pl.ANY),
        ],
        out_specs=pl.BlockSpec((devices, part, width), lambda j: (0, fold + j, 0)),
        out_shape=shape,
        input_output_aliases={4: 0},
        compiler_params=params,
        cost_estimate=pl.CostEstimate(
            flops=2 * total * width * width * (1 + fold), bytes_accessed=0, transcendentals=0
        ),
        name="other_grads",
    )(context, d_inner, first, d_pre, grads)


def bits_of(axis):
    size = lax.axis_size(axis)
    return [(axis, 1 << b) for b in reversed(range(size.bit_length() - 1))]


def across(array, axis, bit):
    return lax.ppermute(array, axis, [(i, i ^ bit) for i in range(lax.axis_size(axis))])


def bit_set(axis, bit):
    return (lax.axis_index(axis) // bit) % 2


def gather_bits(shard, order, dims):
    held = shard.reshape((1,) * len(dims) + shard.shape)
    for axis, bit in order:
        dim = dims.index((axis, bit))
        other = across(held, axis, bit)
        held = jnp.where(
            bit_set(axis, bit) == 0,
            jnp.concatenate([held, other], dim),
            jnp.concatenate([other, held], dim),
        )
    return held


def gather_relative(shard, axis):
    bits = bits_of(axis)
    held = shard.reshape((1,) * len(bits) + shard.shape)
    for dim, (_, bit) in enumerate(bits):
        held = jnp.concatenate([held, across(held, axis, bit)], dim)
    return held.reshape((-1,) + shard.shape[1:])


class Halves:
    def __init__(self, blocks):
        self.shape = blocks.shape[1:]
        self.bits = bits_of("seq")
        self.held = blocks
        self.split()

    def split(self):
        both = self.held.reshape((-1, 2) + self.shape)
        self.keep, self.give = both[:, 0], both[:, 1]

    def send(self):
        self.other = across(self.give, *self.bits.pop())

    def take(self):
        self.held = (self.keep.astype(F32) + self.other.astype(F32)).astype(BF16)
        if not self.bits:
            self.held = self.held.reshape(self.shape)
            return False
        self.split()
        return True

    def waiting(self):
        return self.give if self.bits else self.held

    def tied(self, value):
        if self.bits:
            self.give = value
        else:
            self.held = value


class Spread:
    def __init__(self, blocks):
        self.held, self.sent = blocks, False

    def send(self):
        self.other, self.sent = lax.all_to_all(self.held, BOTH, 0, 0), True

    def take(self):
        self.held = jnp.sum(self.other.astype(F32), 0)
        return False

    def waiting(self):
        return self.held

    def tied(self, value):
        self.held = value


class Sum:
    def __init__(self, value, order):
        self.held, self.order = value.astype(BF16), list(order)

    def send(self):
        axis, bit = self.order.pop(0)
        self.other = across(self.held, axis, bit)

    def take(self):
        self.held = self.held.astype(F32) + self.other.astype(F32)
        if self.order:
            self.held = self.held.astype(BF16)
        return bool(self.order)

    def waiting(self):
        return self.held

    def tied(self, value):
        self.held = value


class Exchanges:
    def __init__(self):
        self.live = []

    def add(self, chain):
        self.live.append((chain, True))
        return chain

    def step(self, value, last=False):
        going, flat = [], []
        for chain, new in self.live:
            if new or chain.take():
                going.append(chain)
        if value is not None:
            chains = [chain for chain, new in self.live if new or not last]
            value, flat = lax.optimization_barrier((value, [c.waiting() for c in chains]))
            for chain, tied in zip(chains, flat):
                chain.tied(tied)
        if last:
            for chain, new in self.live:
                if new:
                    chain.send()
            chains = [chain for chain, new in self.live if not new]
            value, flat = lax.optimization_barrier((value, [c.waiting() for c in chains]))
            for chain, tied in zip(chains, flat):
                chain.tied(tied)
            for chain in going:
                if chain in chains:
                    chain.send()
            self.live = [(chain, False) for chain in going]
            return value
        self.live = [(chain, False) for chain in going]
        for chain in going:
            chain.send()
        return value

    def move(self, chain, value):
        more = chain.take()
        value, tied = lax.optimization_barrier((value, chain.waiting()))
        chain.tied(tied)
        if more:
            chain.send()
        else:
            self.live = [entry for entry in self.live if entry[0] is not chain]
        return value

    def finish(self):
        while self.live:
            self.step(None)


def local(
    prompt_in,
    cont_in,
    prompt_cot,
    cont_cot,
    labels,
    joint_weight,
    query_bias,
    value_bias,
    output_weight,
    output_bias,
    first_gain,
    first_shift,
    expand_weight,
    expand_bias,
    reduce_weight,
    reduce_bias,
    second_gain,
    second_shift,
    student_weight,
    student_bias,
    pool_query,
    pool_weight,
    pool_bias,
    class_weight,
    class_bias,
):
    prompt_rows = prompt_in[0]
    share, width = prompt_rows.shape
    _, conts, length, _ = cont_in.shape
    cont_count = conts * length
    part = joint_weight.shape[0]
    devices = width // part
    hidden_width = expand_weight.shape[1]
    fold = hidden_width // width
    tile = min(share, length)
    grp_bits, seq_bits = bits_of("grp"), bits_of("seq")
    dims = grp_bits + seq_bits
    gather_orders = (
        grp_bits + seq_bits,
        grp_bits[:-1] + seq_bits[:-1] + grp_bits[-1:] + seq_bits[-1:],
    )

    pairs = width // PAIR
    groups = [3, 2, 1] if pairs == 6 else [pairs]
    joint_low = joint_weight.astype(BF16)
    vectors = [
        query_bias,
        value_bias,
        output_bias,
        first_gain,
        first_shift,
        reduce_bias,
        second_gain,
        second_shift,
    ]
    beside = jnp.concatenate([v[None] for v in vectors], 0).astype(BF16).T
    beside = jnp.concatenate([beside, expand_bias.astype(BF16).reshape(part, fold)], 1)
    lanes = student_weight.shape[1]
    own_joint = [joint_low[:, :width]]
    for h in range(pairs):
        own_joint += [joint_low[:, (s * pairs + h) * PAIR :][:, :PAIR] for s in (1, 2)]
    own_joint.append(jnp.pad(beside, ((0, 0), (0, lanes - beside.shape[1]))))
    own_joint = jnp.concatenate(own_joint, 1)
    half = (3 * width // 2 + lanes) // PAIR * PAIR
    joint_all = jnp.concatenate(
        [
            gather_bits(piece, order, dims).reshape(width, -1)
            for piece, order in zip((own_joint[:, :half], own_joint[:, half:]), gather_orders)
        ],
        1,
    )
    joint_all = lax.optimization_barrier(joint_all)
    joint_full = joint_all[:, : 3 * width]
    flat = joint_all[:, 3 * width :].astype(F32)
    by_vector = flat[:, : len(vectors)].T
    qbias, vbias = by_vector[0], by_vector[1]
    ebias = flat[:, 8 : 8 + fold].reshape(hidden_width)
    prompt_all = gather_relative(prompt_rows, "seq")
    far = prompt_all.shape[0]
    out_expand = lax.all_gather(
        jnp.concatenate([output_weight, expand_weight], 1).astype(BF16), BOTH, axis=0, tiled=True
    )
    reduce_full = lax.all_gather(reduce_weight.astype(BF16), BOTH, axis=0, tiled=True)

    cont_rows = cont_in[0].reshape(cont_count, width)
    rows = jnp.concatenate([cont_rows, prompt_rows], 0)
    key_rows = jnp.concatenate([prompt_all, cont_rows], 0)
    rows_t, prompt_t = turned(rows), turned(prompt_all)
    queries = (dot(rows, joint_full[:, :width], 1, 0) + qbias).astype(BF16) * HEAD_DIM ** (-0.5)
    kv_bias = jnp.pad(vbias.reshape(pairs, 1, PAIR), ((0, 0), (1, 0), (0, 0))).reshape(-1)
    keys_values = (dot(key_rows, joint_full[:, width:], 1, 0) + kv_bias).astype(BF16)

    context, prompt_inv, prompt_exp = attention_forward(
        queries, keys_values, far, share, cont_count, tile, None
    )
    context, cont_inv, cont_exp = attention_forward(
        queries, keys_values, far, cont_count, 0, length, context
    )

    classes = class_weight.shape[1]
    head = jnp.concatenate(
        [student_bias, pool_query, pool_bias, jnp.pad(class_bias, (0, lanes - classes))]
    ).reshape(4, lanes)
    weights = (
        out_expand,
        reduce_full,
        by_vector,
        ebias[None],
        student_weight.astype(BF16),
        jnp.pad(head, ((0, 4), (0, 0))),
        pool_weight,
        jnp.pad(class_weight, ((0, 0), (0, lanes - classes))),
        classes,
    )
    cotangents = jnp.concatenate([cont_cot[0].reshape(cont_count, width), prompt_cot[0]], 0)
    cont_tile = min(2 * length, cont_count)
    if cont_tile == share:
        results = dense(
            labels[0], rows, context, cotangents, weights, 0, rows.shape[0], share,
            cont_count // cont_tile, length,
        )
    else:
        of_conts = dense(
            labels[0], rows, context, cotangents, weights, 0, cont_count, cont_tile,
            cont_count // cont_tile, length,
        )
        of_prompt = dense(
            labels[0], rows, context, cotangents, weights, cont_count, share, share, 0, length
        )
        results = [
            of_conts[i]
            if i == 1
            else of_conts[i] + of_prompt[i]
            if i > 8
            else jnp.concatenate([of_conts[i], of_prompt[i]], 0)
            for i in range(len(of_conts))
        ]
    layer_low, logits, first_low, hidden, d_mixed_low, d_pre_low, d_inner = results[:7]
    d_inner_low, d_context, small = results[7:10]
    logits = logits[:, :classes]
    cont_layer = layer_low[:cont_count]
    exchanges = Exchanges()
    small = exchanges.add(Sum(small, dims))
    if part % 8 == 0 and devices % fold == 0:
        blocks = matrix_grads(
            hidden, d_mixed_low, context, d_inner_low, first_low, d_pre_low, devices
        )
    else:
        d_expand_weight = dot(first_low, d_pre_low, 0, 0).astype(BF16)
        blocks = [
            dot(hidden, d_mixed_low, 0, 0).astype(BF16).reshape(devices, -1, width),
            dot(context, d_inner_low, 0, 0).astype(BF16).reshape(devices, part, width),
        ] + [
            d_expand_weight[:, i * width : (i + 1) * width].reshape(devices, part, width)
            for i in range(fold)
        ]
        blocks = jnp.concatenate(blocks, 1)
    blocks, d_context, d_inner, rows_t, prompt_t = lax.optimization_barrier(
        (blocks, d_context, d_inner, rows_t, prompt_t)
    )
    early = lax.psum_scatter(blocks, BOTH, scatter_dimension=0, tiled=True)

    into, owns, joint_parts, sums = (), [], [], []
    h0 = 0
    for nh in groups:
        d_context = exchanges.step(d_context)
        *into, dkv_far, d_joint, sum_rows = attention_backward(
            queries, keys_values, far, context, d_context, (cont_inv, cont_exp),
            (prompt_inv, prompt_exp), rows_t, prompt_t, h0, nh, into,
        )
        if h0 + nh == pairs:
            sums.append(sum_rows[:, 0])
            sums = jnp.concatenate(sums, 0)
            sums = [sums[:, i * PAIR : (i + 1) * PAIR].reshape(devices, 1, part) for i in (0, 2)]
            sums = jnp.concatenate(sums, 1).astype(BF16)
            sums = jnp.pad(sums, ((0, 0), (0, 6), (0, 3 * nh * PAIR - part)))
            d_joint = jnp.concatenate([d_joint.reshape(devices, part, -1), sums], 1)
        else:
            sums.append(sum_rows[:, 0])
        owns.append(exchanges.add(Halves(dkv_far.reshape(-1, share, dkv_far.shape[1]))))
        joint_parts.append(exchanges.add(Spread(d_joint.reshape(devices, -1, 3 * nh * PAIR))))
        h0 += nh
    d_queries, d_kv = into
    early, d_queries = exchanges.step((early, d_queries), True)
    d_queries = exchanges.move(owns[-1], d_queries)
    d_cont_rows = rows_back(d_inner, d_queries, d_kv, joint_all, 0, cont_count, cont_tile)
    exchanges.finish()
    early = early[0].astype(F32)
    reduce_grad = early[: part * fold]
    output_grad = early[part * fold : part * (fold + 1)]
    expand_grad = jnp.concatenate(
        [early[part * (1 + fold + i) : part * (2 + fold + i)] for i in range(fold)], 1
    )
    parts = [p.held for p in joint_parts]
    joint_grad = jnp.concatenate(
        [p[:part].reshape(part, nh, 3, PAIR) for p, nh in zip(parts, groups)], 1
    )
    joint_grad = joint_grad.transpose(0, 2, 1, 3).reshape(part, 3 * width)

    d_own = jnp.concatenate([o.held.astype(BF16) for o in owns], 1)
    d_prompt_rows = rows_back(d_inner, d_queries, d_own, joint_all, cont_count, share, share)

    small = small.held
    index = lax.axis_index(BOTH)
    at = width + lanes
    head_grads = (
        small[:width],
        small[at + lanes],
        small[at + lanes + 1],
        small[width:at],
        small[at + lanes + 2],
        small[at : at + lanes, :classes],
        small[at + lanes + 3, :classes],
    )
    at += lanes + 4
    vector_grads = []
    for row in (part, part + 1):
        vector_grads.append(parts[-1][row, :part])
    for size in [width] * 6 + [hidden_width]:
        vector = small[at : at + size // lanes].reshape(size)
        own = size // devices
        vector_grads.append(lax.dynamic_slice(vector, (index * own,), (own,)))
        at += size // lanes
    (g_qbias, g_vbias, g_obias, g_fgain, g_fshift, g_rbias, g_sgain, g_sshift, g_ebias) = vector_grads
    return (
        layer_low[cont_count:][None],
        cont_layer.reshape(1, conts, length, width),
        logits[None],
        d_prompt_rows[None],
        d_cont_rows.reshape(1, conts, length, width),
        joint_grad,
        g_qbias,
        g_vbias,
        output_grad,
        g_obias,
        g_fgain,
        g_fshift,
        expand_grad,
        g_ebias,
        reduce_grad,
        g_rbias,
        g_sgain,
        g_sshift,
    ) + head_grads


def solution(mesh):
    placed = (
        P("grp", "seq", None),
        P("grp", "seq", None, None),
        P("grp", "seq", None),
        P("grp", "seq", None, None),
        P("grp", "seq"),
        P(("grp", "seq"), None),
        P(("grp", "seq")),
        P(("grp", "seq")),
        P(("grp", "seq"), None),
        P(("grp", "seq")),
        P(("grp", "seq")),
        P(("grp", "seq")),
        P(("grp", "seq"), None),
        P(("grp", "seq")),
        P(("grp", "seq"), None),
        P(("grp", "seq")),
        P(("grp", "seq")),
        P(("grp", "seq")),
        P(),
        P(),
        P(),
        P(),
        P(),
        P(),
        P(),
    )
    return jax.shard_map(
        local,
        mesh=mesh,
        in_specs=placed,
        out_specs=(
            P("grp", "seq", None),
            P("grp", "seq", None, None),
            P("grp", "seq", None),
            P("grp", "seq", None),
            P("grp", "seq", None, None),
            P(("grp", "seq"), None),
            P(("grp", "seq")),
            P(("grp", "seq")),
            P(("grp", "seq"), None),
            P(("grp", "seq")),
            P(("grp", "seq")),
            P(("grp", "seq")),
            P(("grp", "seq"), None),
            P(("grp", "seq")),
            P(("grp", "seq"), None),
            P(("grp", "seq")),
            P(("grp", "seq")),
            P(("grp", "seq")),
            P(),
            P(),
            P(),
            P(),
            P(),
            P(),
            P(),
        ),
        check_vma=False,
    )
```
